32 devices in a mesh: dp: 8 (over y, x, core), mp: 4 (over z).
Axes of the slice: x: 2, y: 2, z: 4, core: 2. Of those that a mesh axis runs over, the one named last changes fastest.
Arguments:
- tokens: bfloat16 [16, 1024, 768], P('dp', 'mp'), may hold values from -6 to 6
- segment_ids: int32 [16, 1024], P('dp'), may hold values from 0 to 3, never falling along the last dimension, each value on 1 to 512 neighbouring positions
- mask_flags: int32 [16, 1024], P('dp', 'mp'), may hold values 0 or 1
- mask_embed: float32 [768], replicated, may hold values from -4 to 4
- first_gain: float32 [768], replicated, may hold values from 0.5 to 1.5
- first_shift: float32 [768], replicated, may hold values from -1.2 to 1.2
- query_key_value_weight: bfloat16 [3, 768, 768], P(None, None, 'mp'), may hold values from -0.21875 to 0.21875
- qv_bias: float32 [2, 768], P(None, 'mp'), may hold values from -2 to 2
- output_weight: bfloat16 [768, 768], P('mp'), may hold values from -1.75 to 1.75
- out_bias: float32 [768], replicated, may hold values from -1.2 to 1.2
- second_gain: float32 [768], replicated, may hold values from 0.5 to 1.5
- second_shift: float32 [768], replicated, may hold values from -1.2 to 1.2
- up_weight: bfloat16 [768, 3072], P(None, 'mp'), may hold values from -0.21875 to 0.21875
- expand_bias: float32 [3072], P('mp'), may hold values from -2 to 2
- down_weight: bfloat16 [3072, 768], P('mp'), may hold values from -0.109375 to 0.109375
- down_bias: float32 [768], replicated, may hold values from -1.2 to 1.2
- out_grad: bfloat16 [16, 1024, 768], P('dp', 'mp'), may hold values from -6 to 6
Outputs:
- activations: bfloat16 [16, 1024, 768], P('dp', 'mp')
- tokens_grad: float32 [16, 1024, 768], P('dp', 'mp')
- mask_embed_grad: float32 [768], replicated
- first_gain_grad: float32 [768], replicated
- first_shift_grad: float32 [768], replicated
- w_qkv_grad: float32 [3, 768, 768], P(None, None, 'mp')
- qv_bias_grad: float32 [2, 768], P(None, 'mp')
- w_out_grad: float32 [768, 768], P('mp')
- out_bias_grad: float32 [768], replicated
- second_gain_grad: float32 [768], replicated
- second_shift_grad: float32 [768], replicated
- up_weight_grad: float32 [768, 3072], P(None, 'mp')
- up_bias_grad: float32 [3072], P('mp')
- down_weight_grad: float32 [3072, 768], P('mp')
- down_bias_grad: float32 [768], replicated
The draws below stay inside these ranges and needn't reach their ends.
Inputs may be any that keep to these rules, and one draw needn't show every extreme that they name: `segment_ids`: in each row the ids never fall; each segment holds 1 to 512 positions, and one holds exactly 512.
All inputs are finite; a program needn't handle non-finite values. No bound on the sum of `mask_flags` on one device may be relied on, other than what follows from the above.
Results may differ from the reference program's by a relative error of at most 0.015.
Values may be sent and summed in bfloat16 or wider, within the bound.
No kernel may reach another device: no remote copies, remote signals or barrier semaphores. Data moves between devices by JAX's collectives and lax.ppermute only.
A program may use at most 128 MiB of HBM per device.

```python
import math
import jax
import jax.numpy as jnp
import numpy as np
from jax import lax

D = 768
HEADS = 12
HD = 64
FF = 3072
LEN = 1024
SEQS = 16


def with_ends(result, own_key, smallest, high):
    spot = [jax.random.randint(jax.random.fold_in(own_key, axis), (), 0, length) for axis, length in enumerate(result.shape)]
    main_axis = result.shape.index(max(result.shape))
    beside = spot[:main_axis] + [(spot[main_axis] + 1) % result.shape[main_axis]] + spot[main_axis + 1:]
    return result.at[tuple(spot)].set(smallest).at[tuple(beside)].set(high)


def steps_of(stream_key, dims, shards, smallest, high):
    level = 1.0
    for axis_at, blocks in shards:
        steps = jax.random.uniform(jax.random.fold_in(jax.random.fold_in(stream_key, 6), axis_at), (blocks,), jnp.float32, smallest / len(shards), high / len(shards))
        level = level * jnp.repeat(jnp.exp(steps), dims[axis_at] // blocks).reshape((-1,) + (1,) * (len(dims) - 1 - axis_at))
    return level


def length_profile(number_of, total, most, slope):
    portions = [(1 << 20) // math.isqrt(standing ** slope) + 1 for standing in range(2, number_of + 1)]
    spare, counts = total - most - (number_of - 1), [1] * (number_of - 1)
    while spare > 0:
        candidates = [i for i in range(number_of - 1) if counts[i] < most]
        pool, left = sum([portions[i] for i in candidates]), spare
        for i in candidates:
            extra = min(most - counts[i], max(1, left * portions[i] // pool), spare)
            counts[i] = counts[i] + extra
            spare = spare - extra
    return np.array([most] + counts)


def uneven(key, count, total, most, lean):
    if count == 2:
        one = jax.random.randint(key, (), max(1, total - most), min(most, total - 1) + 1)
        return jnp.stack([one, total - one])
    sizes = jnp.asarray(length_profile(count, total, most, lean), jnp.int32)
    pairs = (count - 1) // 2
    donor, receiver = sizes[1:1 + 2 * pairs:2], sizes[2:2 + 2 * pairs:2]
    slack = jnp.minimum(donor - 1, most - receiver)
    passed = jax.random.randint(jax.random.fold_in(key, 1), (pairs,), 0, 1 << 20) % (slack + 1)
    sizes = sizes.at[1:1 + 2 * pairs:2].set(donor - passed).at[2:2 + 2 * pairs:2].set(receiver + passed)
    return sizes[jax.random.permutation(jax.random.fold_in(key, 2), count)]


def scatter_about(rng, extent, width, most, shards=(), dtype=jnp.bfloat16):
    level = steps_of(rng, extent, shards, -0.22, 0.18) if shards else 1.0
    entries = jax.random.normal(rng, extent, jnp.float32) * width * level
    return jnp.minimum(jnp.maximum(entries, -most), most).astype(dtype)


def setup_inputs(seed: int = 0) -> dict:
    seeds = jax.random.split(jax.random.key(seed), 18)
    return {
        "tokens": scatter_about(seeds[0], (SEQS, LEN, D), 1.0, 6.0, ((0, 8), (1, 4))),
        "segment_ids": jax.vmap(lambda own: jnp.searchsorted(jnp.cumsum(uneven(own, 4, LEN, LEN // 2, 0)), jnp.arange(LEN), side="right"))(jax.random.split(seeds[1], SEQS)).reshape((SEQS, LEN)).astype(jnp.int32),
        "mask_flags": with_ends((jax.random.randint(seeds[2], (SEQS, LEN), 0, 10) < 3).astype(jnp.int32), jax.random.fold_in(seeds[2], 1), 0, 1),
        "mask_embed": scatter_about(seeds[3], (D,), 1.0, 4.0, (), jnp.float32),
        "first_gain": jnp.clip(1.0 + 0.1 * jax.random.normal(seeds[4], (D,), jnp.float32), 0.5, 1.5),
        "first_shift": scatter_about(seeds[5], (D,), 0.3, 1.2, (), jnp.float32),
        "query_key_value_weight": scatter_about(seeds[6], (3, D, D), D ** -0.5, 0.21875, ((2, 4),)),
        "qv_bias": scatter_about(seeds[7], (2, D), 0.5, 2.0, ((1, 4),), jnp.float32),
        "output_weight": scatter_about(seeds[8], (D, D), (D // 64) ** -0.5, 1.75, ((0, 4),)),
        "out_bias": scatter_about(seeds[9], (D,), 0.3, 1.2, (), jnp.float32),
        "second_gain": jnp.clip(1.0 + 0.1 * jax.random.normal(seeds[10], (D,), jnp.float32), 0.5, 1.5),
        "second_shift": scatter_about(seeds[11], (D,), 0.3, 1.2, (), jnp.float32),
        "up_weight": scatter_about(seeds[12], (D, FF), D ** -0.5, 0.21875, ((1, 4),)),
        "expand_bias": scatter_about(seeds[13], (FF,), 0.5, 2.0, ((0, 4),), jnp.float32),
        "down_weight": scatter_about(seeds[14], (FF, D), FF ** -0.5, 0.109375, ((0, 4),)),
        "down_bias": scatter_about(seeds[15], (D,), 0.3, 1.2, (), jnp.float32),
        "out_grad": scatter_about(seeds[16], (SEQS, LEN, D), 1.0, 6.0, ((0, 8), (1, 4))),
    }


@jax.custom_vjp
def low(v):
    return lax.optimization_barrier(v.astype(jnp.bfloat16)).astype(jnp.float32)

@jax.custom_vjp
def reduced_backward(v):
    return v

def low_keep(v):
    return (low(v), None)

def low_pass(kept, grad):
    return (grad,)

def back_keep(v):
    return (v, None)

def back_low(kept, grad):
    return (low(grad),)
low.defvjp(low_keep, low_pass)
reduced_backward.defvjp(back_keep, back_low)
EPSILON = 1e-06
NEG_FILL = -1e+30
PRECISION_LEVEL = lax.Precision.HIGHEST

def both_ways(value):
    return low(reduced_backward(value))

def layer_norm(rows, gain, shift):
    row_mean = lax.optimization_barrier(jnp.mean(rows, axis=-1, keepdims=True))
    centred = rows - row_mean
    variance = lax.optimization_barrier(jnp.mean(centred * centred, axis=-1, keepdims=True))
    return centred * lax.rsqrt(variance + EPSILON) * gain + shift

def attend_sequence(seq_items):
    queries, key_rows, value_rows, seg_row = seq_items
    length = queries.shape[0]
    queries = queries.reshape(length, HEADS, HD)
    key_rows = key_rows.reshape(length, HEADS, HD)
    value_rows = value_rows.reshape(length, HEADS, HD)
    scores = reduced_backward(jnp.einsum('qhd,khd->hqk', queries, key_rows, precision=PRECISION_LEVEL) * HD ** (-0.5))
    same_seg = seg_row[:, None] == seg_row[None, :]
    scores = jnp.where(same_seg[None, :, :], scores, NEG_FILL)
    attn_probs = jax.nn.softmax(scores, axis=-1)
    context_rows = jnp.einsum('hqk,khd->qhd', low(attn_probs), value_rows, precision=PRECISION_LEVEL)
    return context_rows.reshape(length, HEADS * HD)

def reference(tokens, segment_ids, mask_flags, mask_embed, first_gain, first_shift, query_key_value_weight, qv_bias, output_weight, out_bias, second_gain, second_shift, up_weight, expand_bias, down_weight, down_bias, out_grad):
    masked = (mask_flags == 1)[:, :, None]

    def layer(token_rows, embed_row, gain_one, shift_one, query_key_value_matrix, qkv_shift, output_matrix, out_shift, gain_two, shift_two, up_matrix, expand_shift, down_matrix, down_shift):
        start_rows = jnp.where(masked, embed_row, token_rows)
        first_normalized = low(layer_norm(start_rows, gain_one, shift_one))
        projected_rows = jnp.einsum('gaw,pwn->pgan', first_normalized, query_key_value_matrix, precision=PRECISION_LEVEL)
        queries = both_ways(projected_rows[0] + qkv_shift[0])
        key_rows = both_ways(projected_rows[1])
        value_rows = both_ways(projected_rows[2] + qkv_shift[1])
        context_rows = lax.map(jax.checkpoint(attend_sequence), (queries, key_rows, value_rows, segment_ids))
        context_rows = both_ways(context_rows)
        attention_total = reduced_backward(jnp.einsum('itq,qp->itp', context_rows, output_matrix, precision=PRECISION_LEVEL))
        mid_rows = start_rows + attention_total + out_shift
        second_normalized = low(layer_norm(mid_rows, gain_two, shift_two))
        hidden_rows = reduced_backward(jnp.einsum('coz,zb->cob', second_normalized, up_matrix, precision=PRECISION_LEVEL) + expand_shift)
        active_tokens = low(jax.nn.gelu(hidden_rows, approximate=False))
        feedforward_total = reduced_backward(jnp.einsum('oci,iz->ocz', active_tokens, down_matrix, precision=PRECISION_LEVEL))
        return mid_rows + feedforward_total + down_shift
    primals = (tokens.astype(jnp.float32), mask_embed, first_gain, first_shift, query_key_value_weight.astype(jnp.float32), qv_bias, output_weight.astype(jnp.float32), out_bias, second_gain, second_shift, up_weight.astype(jnp.float32), expand_bias, down_weight.astype(jnp.float32), down_bias)
    final_rows, pullback = jax.vjp(layer, *primals)
    grads = pullback(out_grad.astype(jnp.float32))
    return (final_rows.astype(jnp.bfloat16), grads[0], grads[1], grads[2], grads[3], grads[4], grads[5], grads[6], grads[7], grads[8], grads[9], grads[10], grads[11], grads[12], grads[13])
```

```python
import jax
import jax.numpy as jnp
from jax import lax
from jax.experimental import pallas as pl
from jax.experimental.pallas import tpu as pltpu
from jax.sharding import PartitionSpec as P

HD = 64
EPSILON = 1e-06
NEG_FILL = -1e30
BF = jnp.bfloat16
F32 = jnp.float32
BOTH = ("dp", "mp")
BLOCK_ORDER = (0, 2, 1, 3)
NT = (((1,), (1,)), ((), ()))
NN = (((1,), (0,)), ((), ()))
TN = (((0,), (0,)), ((), ()))


def dot(left, right, dims):
    return lax.dot_general(left, right, dims, preferred_element_type=F32)


def swap_dp(value, bit, dp_size):
    return lax.ppermute(value, "dp", [(i, i ^ bit) for i in range(dp_size)])


def swap_mp(value, bit):
    return lax.ppermute(value, "mp", [(i, i ^ bit) for i in range(4)])


def row_routes(dp_size):
    first, second = [], []
    for pair in range(dp_size // 2):
        for core in range(2):
            for place in range(4):
                source = (2 * pair + core) * 4 + place
                for row in range(2):
                    target = (2 * pair + place // 2) * 4 + 2 * core + row
                    (first if row == place % 2 else second).append((source, target))
    return first, second


def to_rows(first, second, dp_size):
    routes = row_routes(dp_size)
    return (lax.ppermute(first, BOTH, routes[0]), lax.ppermute(second, BOTH, routes[1]))


def from_rows(first, second, dp_size):
    back = [[(target, source) for source, target in route] for route in row_routes(dp_size)]
    return (lax.ppermute(first, BOTH, back[0]), lax.ppermute(second, BOTH, back[1]))


def plane_groups(dp_size):
    return [[base * 8 + core + 2 * k for k in range(4)] for base in range(dp_size // 8) for core in range(2)]


def plane_gather(value, dp_size):
    spread = jnp.broadcast_to(value[None], (4,) + value.shape)
    return lax.all_to_all(spread, "dp", 0, 0, tiled=True, axis_index_groups=plane_groups(dp_size))


def plane_scatter(value, dp_size):
    pieces = lax.all_to_all(value, "dp", 0, 0, tiled=True, axis_index_groups=plane_groups(dp_size))
    return jnp.sum(pieces.astype(F32), axis=0).astype(BF)


def tie(*values):
    return lax.optimization_barrier(values)


def add(left, right):
    return (left.astype(F32) + right.astype(F32)).astype(BF)


def whole(value):
    rank = value.ndim
    return pl.BlockSpec(value.shape, lambda *i: (0,) * rank)


def scalars():
    return pl.BlockSpec(memory_space=pltpu.SMEM)


def call(kernel, name, grid, in_specs, out_specs, out_shape, scratch, flops, moved, args):
    return pl.pallas_call(
        kernel,
        grid=grid,
        in_specs=in_specs,
        out_specs=out_specs,
        out_shape=out_shape,
        scratch_shapes=scratch,
        compiler_params=pltpu.CompilerParams(vmem_limit_bytes=44 << 20),
        cost_estimate=pl.CostEstimate(flops=flops, transcendentals=0, bytes_accessed=moved),
        name=name,
    )(*args)


def centre(rows):
    row_mean = jnp.mean(rows, axis=-1, keepdims=True)
    centred = rows - row_mean
    variance = jnp.mean(centred * centred, axis=-1, keepdims=True)
    inv_scale = lax.rsqrt(variance + EPSILON)
    return (centred * inv_scale, inv_scale)


def centre_back(incoming, unit_rows, inv_scale, gain):
    scaled = incoming * gain
    inner_one = jnp.mean(scaled, axis=-1, keepdims=True)
    inner_two = jnp.mean(scaled * unit_rows, axis=-1, keepdims=True)
    return inv_scale * (scaled - inner_one - unit_rows * inner_two)


def project_kernel(place, one, two, gain, shift, local, near, other, q_bias, v_bias, normed, q, kv, weights):
    strip = one.shape[0]
    for i, rows in enumerate((one, two)):
        unit, _ = centre(rows[...].astype(F32))
        normed[i * strip : (i + 1) * strip] = (unit * gain[...] + shift[...]).astype(BF)
    core = place[0]
    weights[:, 0] = local[...]
    for k in range(4):
        weights[2 * core + k // 2, 1:4, k % 2] = near[k]
        weights[2 - 2 * core + k // 2, 1:4, k % 2] = other[k]
    width = one.shape[1]
    rows = normed[...]
    q[...] = (dot(rows, weights[0].reshape(width, width), NT) + q_bias[...]).astype(BF)
    kv[0] = dot(rows, weights[1].reshape(width, width), NT).astype(BF)
    kv[1] = (dot(rows, weights[2].reshape(width, width), NT) + v_bias[...]).astype(BF)


def project(place, one, two, gain, shift, local, near, other, q_bias, v_bias):
    strip, width = one.shape
    tokens = 2 * strip
    args = (place, one, two, gain, shift, local, near, other, q_bias, v_bias)
    shapes = [
        jax.ShapeDtypeStruct((tokens, width), BF),
        jax.ShapeDtypeStruct((tokens, width), BF),
        jax.ShapeDtypeStruct((2, tokens, width), BF),
        jax.ShapeDtypeStruct((4, 4, 2, width // 8, width), BF),
    ]
    return call(
        project_kernel,
        "project",
        (1,),
        [scalars()] + [whole(x) for x in args[1:]],
        [whole(x) for x in shapes],
        shapes,
        [],
        6 * tokens * width * width,
        12 * width * width,
        args,
    )


def attend_kernel(
    q_ref, own_ref, far_ref, segq_ref, segk_ref, one, two, wo, o_bias, gain, shift,
    ctx_ref, lse_ref, mid_ref, normed_ref, keys, values_t, total,
):
    half = own_ref.shape[1]
    keys[:half] = own_ref[0]
    keys[half:] = far_ref[0]
    values_t[:, :half] = own_ref[1].T
    values_t[:, half:] = far_ref[1].T
    tokens = q_ref.shape[0]
    block = 256
    step = pl.program_id(0)
    for start in range(0, tokens, block):
        span = slice(start, start + block)
        same = segk_ref[...] == segq_ref[:, span]
        query = q_ref[span, :] * jnp.asarray(HD**-0.5, BF)
        lanes = lax.broadcasted_iota(jnp.int32, query.shape, 1)
        pieces = []
        for head in range(2):
            own = (lanes >= HD) if head else (lanes < HD)
            scores = dot(keys[...], jnp.where(own, query, jnp.zeros_like(query)), NT)
            scores = jnp.where(same, scores, NEG_FILL)
            row_max = jnp.max(scores, axis=0, keepdims=True)
            exp_scores = jnp.exp(scores - row_max)
            row_total = jnp.sum(exp_scores, axis=0, keepdims=True)
            part = dot(values_t[head * HD : (head + 1) * HD, :], exp_scores.astype(BF), NN)
            pieces.append(part / row_total)
            lse_ref[0, head : head + 1, span] = row_max + jnp.log(row_total)
        context = jnp.concatenate(pieces, axis=0).T.astype(BF)
        ctx_ref[span, :] = context
        mixed = dot(context, wo[...], NN)

        @pl.when(step == 0)
        def _():
            total[span, :] = mixed

        @pl.when(step > 0)
        def _():
            total[span, :] += mixed

    @pl.when(step == pl.num_programs(0) - 1)
    def _():
        strip = one.shape[0]
        for i, rows in enumerate((one, two)):
            span = slice(i * strip, (i + 1) * strip)
            mid = rows[...].astype(F32) + total[span, :] + o_bias[...]
            mid_ref[span, :] = mid
            unit, _ = centre(mid)
            normed_ref[span, :] = (unit * gain[...] + shift[...]).astype(BF)


def attend(q, own, far, seg_q, seg_k, one, two, wo, o_bias, gain, shift):
    rows, width = q.shape
    pairs = width // 128
    half = own.shape[1]
    args = (q, own, far, seg_q, seg_k, one, two, wo, o_bias, gain, shift)
    head_block = pl.BlockSpec((rows, 128), lambda i: (0, i))
    key_block = pl.BlockSpec((2, half, 128), lambda i: (0, 0, i))
    shapes = [
        jax.ShapeDtypeStruct((rows, width), BF),
        jax.ShapeDtypeStruct((pairs, 2, rows), F32),
        jax.ShapeDtypeStruct((rows, width), F32),
        jax.ShapeDtypeStruct((rows, width), BF),
    ]
    return call(
        attend_kernel,
        "attend",
        (pairs,),
        [head_block, key_block, key_block, whole(seg_q), whole(seg_k), whole(one), whole(two)]
        + [pl.BlockSpec((128, width), lambda i: (3 * pairs + i, 0)), whole(o_bias), whole(gain), whole(shift)],
        [head_block, pl.BlockSpec((1, 2, rows), lambda i: (i, 0, 0)), whole(shapes[2]), whole(shapes[3])],
        shapes,
        [pltpu.VMEM((2 * half, 128), BF), pltpu.VMEM((128, 2 * half), BF), pltpu.VMEM((rows, width), F32)],
        16 * rows * half * width,
        rows * width * 16,
        args,
    )


def load_block(place, flip, at_y, local, first, second, along_x, block):
    piece = local.shape[1]
    core = place[0] if not flip else 1 - place[0]
    for x in range(2):
        spot = place[1 + 2 * at_y + x]
        block[x, 0] = local[core * 4 + spot]
        if along_x:
            block[x, 1:4] = (second if at_y else first)[x]
        else:
            block[x, 1:4] = (second if x else first)[at_y]


def expand_kernel(
    place, normed, mid, bias, local_up, local_down, up0, up1, up2, up3, down0, down1, down2, down3, d_bias,
    active, slope, out, up, down, total,
):
    step = pl.program_id(0)
    ups, downs = (up0, up1, up2, up3), (down0, down1, down2, down3)
    for j in range(4):

        @pl.when(step == j)
        def _():
            g = j - j % 2
            load_block(place, j // 2, j % 2, local_up, ups[g], ups[g + 1], True, up)
            load_block(place, j // 2, j % 2, local_down, downs[g], downs[g + 1], False, down)

    width = normed.shape[1]
    hidden = dot(normed[...], up[...].reshape(width, width), NT) + bias[0]
    cdf = 0.5 * (1.0 + lax.erf(hidden * (0.5**0.5)))
    pulled = cdf + hidden * jnp.exp(-0.5 * hidden * hidden) * 0.3989422804014327
    slope[...] = pulled.astype(BF)
    active[...] = (hidden * cdf).astype(BF)
    part = dot(active[...], down[...].reshape(width, width), NN)

    @pl.when(step == 0)
    def _():
        total[...] = mid[...] + d_bias[...] + part

    @pl.when((step > 0) & (step < 3))
    def _():
        total[...] += part

    @pl.when(step == 3)
    def _():
        out[...] = (total[...] + part).astype(BF)


def expand(place, normed, mid, bias, local_up, local_down, ups, downs, d_bias):
    tokens, width = normed.shape
    piece = width // 8
    args = (place, normed, mid, bias, local_up, local_down, *ups, *downs, d_bias)
    hidden = pl.BlockSpec((tokens, width), lambda j: (0, j))
    shapes = [
        jax.ShapeDtypeStruct((tokens, 4 * width), BF),
        jax.ShapeDtypeStruct((tokens, 4 * width), BF),
        jax.ShapeDtypeStruct((tokens, width), BF),
    ]
    specs = [scalars()] + [whole(x) for x in args[1:]]
    specs[3] = pl.BlockSpec((1, 1, width), lambda j: (j, 0, 0))
    return call(
        expand_kernel,
        "expand",
        (4,),
        specs,
        [hidden, hidden, whole(shapes[2])],
        shapes,
        [pltpu.VMEM((2, 4, piece, width), BF)] * 2 + [pltpu.VMEM((tokens, width), F32)],
        16 * tokens * width * width,
        20 * width * width,
        args,
    )


def expand_back_kernel(
    flip, place, grad, normed, active, slope, local_up, local_down, up0, up1, down0, down1, before,
    up_grad, down_grad, normed_grad, bias_grad, up, down,
):
    step = pl.program_id(0)
    for j in range(2):

        @pl.when(step == j)
        def _():
            load_block(place, flip, j, local_up, up0, up1, True, up)
            load_block(place, flip, j, local_down, down0, down1, False, down)

    width = normed.shape[1]
    wide = up.shape
    incoming = dot(grad[...], down[...].reshape(width, width), NT)
    grad_hidden = (incoming * slope[...].astype(F32)).astype(BF)
    bias_grad[0] = jnp.sum(grad_hidden.astype(F32), axis=0, keepdims=True)
    down_grad[...] = dot(active[...], grad[...], TN).astype(BF).reshape(2, 1, *wide[1:])
    up_grad[0] = dot(grad_hidden, normed[...], TN).astype(BF).reshape(wide)
    part = dot(grad_hidden, up[...].reshape(width, width), NN)

    @pl.when(step == 0)
    def _():
        if before is None:
            normed_grad[...] = part
        else:
            normed_grad[...] = before[...] + part

    @pl.when(step > 0)
    def _():
        normed_grad[...] += part


def expand_back(flip, place, grad, normed, active, slope, local_up, local_down, ups, downs, before):
    tokens, width = normed.shape
    piece = width // 8
    args = (place, grad, normed, active, slope, local_up, local_down, *ups, *downs)
    if before is not None:
        args = args + (before,)

    def kernel(*refs):
        if before is None:
            refs = refs[:11] + (None,) + refs[11:]
        return expand_back_kernel(flip, *refs)

    hidden = pl.BlockSpec((tokens, width), lambda j: (0, j + 2 * flip))
    shapes = [
        jax.ShapeDtypeStruct((2, 2, 4, piece, width), BF),
        jax.ShapeDtypeStruct((2, 2, 4, piece, width), BF),
        jax.ShapeDtypeStruct((tokens, width), F32),
        jax.ShapeDtypeStruct((2, 1, width), F32),
    ]
    specs = [scalars()] + [whole(x) for x in args[1:]]
    specs[3] = specs[4] = hidden
    return call(
        kernel,
        "expand_back_other" if flip else "expand_back_own",
        (2,),
        specs,
        [
            pl.BlockSpec((1, 2, 4, piece, width), lambda j: (j, 0, 0, 0, 0)),
            pl.BlockSpec((2, 1, 4, piece, width), lambda j: (0, j, 0, 0, 0)),
            whole(shapes[2]),
            pl.BlockSpec((1, 1, width), lambda j: (j, 0, 0)),
        ],
        shapes,
        [pltpu.VMEM((2, 4, piece, width), BF)] * 2,
        20 * tokens * width * width,
        16 * width * width,
        args,
    )


def settle_kernel(incoming, mid, grad, gain, wo, grad_mid, grad_attn, grad_context, sums):
    strip = 256
    parts = None
    for at in range(0, mid.shape[0], strip):
        span = slice(at, at + strip)
        unit, inv_scale = centre(mid[span, :])
        given = incoming[span, :]
        outer = grad[span, :].astype(F32)
        made = outer + centre_back(given, unit, inv_scale, gain[...])
        grad_mid[span, :] = made
        grad_attn[span, :] = made.astype(BF)
        grad_context[span, :] = dot(made.astype(BF), wo[...], NT).astype(BF)
        rows = [jnp.sum(v, axis=0, keepdims=True) for v in (made, given * unit, given, outer)]
        parts = rows if parts is None else [a + b for a, b in zip(parts, rows)]
    for i, row in enumerate(parts):
        sums[i : i + 1, :] = row


def settle(incoming, mid, grad, gain, weights):
    tokens, width = mid.shape
    args = (incoming, mid, grad, gain, weights)
    specs = [whole(x) for x in args]
    specs[4] = pl.BlockSpec((width, width), lambda i: (3, 0))
    shapes = [
        jax.ShapeDtypeStruct((tokens, width), F32),
        jax.ShapeDtypeStruct((tokens, width), BF),
        jax.ShapeDtypeStruct((tokens, width), BF),
        jax.ShapeDtypeStruct((8, width), F32),
    ]
    return call(
        settle_kernel,
        "settle",
        (1,),
        specs,
        [whole(x) for x in shapes],
        shapes,
        [],
        2 * tokens * width * width,
        14 * tokens * width,
        args,
    )


def weigh_kernel(flip, place, dq, mine, got, context, normed, grad, out, left, right):
    core = place[0] if not flip else 1 - place[0]
    width = dq.shape[1]
    piece = width // 8

    @pl.when(core == 0)
    def _():
        left[0] = dq[...]
        left[1] = (mine[0].astype(F32) + got[0].astype(F32)).astype(BF)
        right[...] = normed[...]

    @pl.when(core == 1)
    def _():
        left[0] = (mine[1].astype(F32) + got[1].astype(F32)).astype(BF)
        left[1] = context[...]
        right[...] = grad[...]

    for i in range(2):
        rows = normed[...] if i == 0 else right[...]
        made = dot(left[i], rows, TN).astype(BF).reshape(4, 2, piece, width)
        out[2 * i] = made[:, 0]
        out[2 * i + 1] = made[:, 1]


def weigh(flip, place, dq, mine, got, context, normed, grad):
    tokens, width = dq.shape
    args = (place, dq, mine, got, context, normed, grad)
    shape = jax.ShapeDtypeStruct((4, 4, width // 8, width), BF)
    return call(
        lambda *refs: weigh_kernel(flip, *refs),
        "weigh_other" if flip else "weigh_own",
        (1,),
        [scalars()] + [whole(x) for x in args[1:]],
        whole(shape),
        shape,
        [pltpu.VMEM((2, tokens, width), BF), pltpu.VMEM((tokens, width), BF)],
        4 * tokens * width * width,
        8 * width * width,
        args,
    )


def finish_kernel(dq, mine, got, weights, one, two, gain, grad_mid, flags, out_one, out_two, sums, total):
    width = dq.shape[1]
    keys = (mine[0].astype(F32) + got[0].astype(F32)).astype(BF)
    values = (mine[1].astype(F32) + got[1].astype(F32)).astype(BF)
    total[...] = dot(dq[...], weights[0].reshape(width, width), NN)
    total[...] += dot(keys, weights[1].reshape(width, width), NN)
    total[...] += dot(values, weights[2].reshape(width, width), NN)
    strip = one.shape[0]
    gathered = None
    for i, rows in enumerate((one, two)):
        span = slice(i * strip, (i + 1) * strip)
        unit, inv_scale = centre(rows[...].astype(F32))
        incoming = total[span, :]
        grad_start = grad_mid[span, :] + centre_back(incoming, unit, inv_scale, gain[...])
        (out_two if i else out_one)[...] = grad_start.astype(BF)
        masked = jnp.where(flags[span, :] == 1, grad_start, 0.0)
        parts = [jnp.sum(v, axis=0, keepdims=True) for v in (masked, incoming * unit, incoming)]
        gathered = parts if gathered is None else [a + b for a, b in zip(gathered, parts)]
    gathered.append(jnp.sum(dq[...].astype(F32), axis=0, keepdims=True))
    gathered.append(jnp.sum(values.astype(F32), axis=0, keepdims=True))
    for i, row in enumerate(gathered):
        sums[i : i + 1, :] = row


def finish(dq, mine, got, weights, one, two, gain, grad_mid, flags):
    tokens, width = dq.shape
    args = (dq, mine, got, weights, one, two, gain, grad_mid, flags)
    specs = [whole(x) for x in args]
    specs[3] = pl.BlockSpec((3,) + weights.shape[1:], lambda i: (0,) * 5)
    shapes = [
        jax.ShapeDtypeStruct((tokens // 2, width), BF),
        jax.ShapeDtypeStruct((tokens // 2, width), BF),
        jax.ShapeDtypeStruct((8, width), F32),
    ]
    return call(
        finish_kernel,
        "finish",
        (1,),
        specs,
        [whole(x) for x in shapes],
        shapes,
        [pltpu.VMEM((tokens, width), F32)],
        6 * tokens * width * width,
        12 * width * width,
        args,
    )


def attend_back_kernel(
    q_ref,
    own_ref,
    far_ref,
    g_ref,
    ctx_ref,
    lse_ref,
    segq_ref,
    segk_ref,
    dq_ref,
    own_grad_ref,
    far_grad_ref,
    keys,
    keys_t,
    values,
    dk_total,
    dv_total,
):
    half = own_ref.shape[1]
    keys[:half] = own_ref[0]
    keys[half:] = far_ref[0]
    keys_t[:, :half] = own_ref[0].T
    keys_t[:, half:] = far_ref[0].T
    values[:half] = own_ref[1]
    values[half:] = far_ref[1]
    total = q_ref.shape[0]
    block = 256
    scale = jnp.asarray(HD**-0.5, BF)
    for start in range(0, total, block):
        span = slice(start, start + block)
        same = segk_ref[...] == segq_ref[:, span]
        query = q_ref[span, :] * scale
        grad = g_ref[span, :]
        product = (grad.astype(F32) * ctx_ref[span, :].astype(F32)).T
        lanes = lax.broadcasted_iota(jnp.int32, query.shape, 1)
        pieces = []
        for head in range(2):
            own = (lanes >= HD) if head else (lanes < HD)
            query_own = jnp.where(own, query, jnp.zeros_like(query))
            grad_own = jnp.where(own, grad, jnp.zeros_like(grad))
            scores = dot(keys[...], query_own, NT)
            probs = jnp.exp(jnp.where(same, scores, NEG_FILL) - lse_ref[0, head : head + 1, span])
            grad_probs = dot(values[...], grad_own, NT)
            row_dot = jnp.sum(product[head * HD : (head + 1) * HD, :], axis=0, keepdims=True)
            grad_scores = (probs * (grad_probs - row_dot)).astype(BF)
            dv = dot(probs.astype(BF), grad_own, NN)
            dk = dot(grad_scores, query_own, NN)
            if start == 0 and head == 0:
                dv_total[...] = dv
                dk_total[...] = dk
            else:
                dv_total[...] += dv
                dk_total[...] += dk
            pieces.append(dot(keys_t[head * HD : (head + 1) * HD, :], grad_scores, NN))
        dq_ref[span, :] = (jnp.concatenate(pieces, axis=0).T * HD**-0.5).astype(BF)
    own_grad_ref[0] = dk_total[:half].astype(BF)
    far_grad_ref[0] = dk_total[half:].astype(BF)
    own_grad_ref[1] = dv_total[:half].astype(BF)
    far_grad_ref[1] = dv_total[half:].astype(BF)


def attend_back(q, own, far, grad, ctx, lse, seg_q, seg_k):
    rows, width = q.shape
    pairs = width // 128
    half = own.shape[1]
    head_block = pl.BlockSpec((rows, 128), lambda i: (0, i))
    key_block = pl.BlockSpec((2, half, 128), lambda i: (0, 0, i))
    return pl.pallas_call(
        attend_back_kernel,
        grid=(pairs,),
        in_specs=[head_block]
        + [key_block] * 2
        + [
            head_block,
            head_block,
            pl.BlockSpec((1, 2, rows), lambda i: (i, 0, 0)),
            pl.BlockSpec((1, rows), lambda i: (0, 0)),
            pl.BlockSpec((2 * half, 1), lambda i: (0, 0)),
        ],
        out_specs=[head_block] + [key_block] * 2,
        out_shape=[jax.ShapeDtypeStruct((rows, width), BF)]
        + [jax.ShapeDtypeStruct((2, half, width), BF)] * 2,
        scratch_shapes=[
            pltpu.VMEM((2 * half, 128), BF),
            pltpu.VMEM((128, 2 * half), BF),
            pltpu.VMEM((2 * half, 128), BF),
            pltpu.VMEM((2 * half, 128), F32),
            pltpu.VMEM((2 * half, 128), F32),
        ],
        compiler_params=pltpu.CompilerParams(vmem_limit_bytes=40 << 20),
        cost_estimate=pl.CostEstimate(
            flops=10 * rows * 2 * half * width * 2,
            transcendentals=rows * 2 * half * pairs * 2,
            bytes_accessed=rows * width * 24,
        ),
        name="attend_back",
    )(q, own, far, grad, ctx, lse, seg_q, seg_k)


def make_body(dp_size):
    def body(
        tokens,
        segment_ids,
        mask_flags,
        mask_embed,
        first_gain,
        first_shift,
        query_key_value_weight,
        qv_bias,
        output_weight,
        out_bias,
        second_gain,
        second_shift,
        up_weight,
        expand_bias,
        down_weight,
        down_bias,
        out_grad,
    ):
        dp_at = lax.axis_index("dp")
        mp_at = lax.axis_index("mp")
        core = dp_at % 2
        spot = (dp_at // 2) % 4
        parity = mp_at % 2
        width = tokens.shape[2]
        strip = tokens.shape[1]
        piece = width // 8
        place = jnp.stack([core] + [spot ^ r for r in range(4)]).astype(jnp.int32)

        def across(value, bit):
            return swap_dp(value, bit, dp_size)

        def pick(values):
            return (
                lax.dynamic_index_in_dim(values, parity, 0, keepdims=False),
                lax.dynamic_index_in_dim(values, 1 - parity, 0, keepdims=False),
            )

        def row(vector):
            return vector.reshape(1, -1)

        local_attention = jnp.concatenate(
            [query_key_value_weight.transpose(0, 2, 1).reshape(-1, width), output_weight], axis=0
        )
        offset = (core * 4 + spot) * piece
        share_a = lax.dynamic_slice_in_dim(local_attention, offset, piece, 0)
        local_up = up_weight.T
        share_f = jnp.stack(
            [
                lax.dynamic_slice_in_dim(local_up, offset, piece, 0),
                lax.dynamic_slice_in_dim(down_weight, offset, piece, 0),
            ]
        )
        start_rows = jnp.where((mask_flags == 1)[:, :, None], mask_embed.astype(BF), tokens)
        rows_one, rows_two = pick(start_rows)
        grads_one, grads_two = pick(out_grad)
        flags_one, flags_two = pick(mask_flags)
        vectors = jnp.concatenate([qv_bias.reshape(-1), expand_bias])

        def line_of(share, far):
            near = swap_mp(jnp.stack([share, far]), 1)
            return jnp.stack([far, near[0], near[1]])

        far_a = swap_mp(share_a, 2)
        far_a, share_f, rows_one, rows_two = tie(far_a, share_f, rows_one, rows_two)
        line_a = line_of(share_a, far_a)
        far_f = swap_mp(share_f, 2)
        rows_one, rows_two = to_rows(rows_one, rows_two, dp_size)
        line_a, far_f, vectors, segment_ids = tie(line_a, far_f, vectors, segment_ids)
        near_a = plane_gather(line_a, dp_size)
        line_f = line_of(share_f, far_f)
        far_vectors = swap_mp(vectors, 2)
        other_segments = across(segment_ids, 1)
        line_f, far_vectors, rows_one, rows_two, grads_one, grads_two, flags_one, flags_two = tie(
            line_f, far_vectors, rows_one, rows_two, grads_one, grads_two, flags_one, flags_two
        )
        near_vectors = swap_mp(jnp.stack([vectors, far_vectors]), 1)
        line_f, near_a = tie(line_f, near_a)
        other_a = across(near_a, 1)

        row_segments = jnp.where(mp_at // 2 == core, segment_ids, other_segments)
        row_segments = lax.dynamic_index_in_dim(row_segments, parity, 0, keepdims=False)
        quarters = row_segments.reshape(4, strip)

        def quarter(at):
            return lax.dynamic_index_in_dim(quarters, at, 0, keepdims=False)

        own_segments = jnp.concatenate([quarter(2 * core + parity), quarter(2 * core + 1 - parity)])
        far_segments = jnp.concatenate([quarter(2 - 2 * core + parity), quarter(3 - 2 * core - parity)])
        seg_q = own_segments[None, :]
        seg_k = jnp.concatenate([own_segments, far_segments])[:, None]

        vectors = jnp.stack([vectors, far_vectors, near_vectors[0], near_vectors[1]])
        q_width = qv_bias.shape[1]
        q_bias = vectors[:, :q_width].reshape(1, -1)
        v_bias = vectors[:, q_width : 2 * q_width].reshape(1, -1)

        def turn(values, axes):
            for axis, bit in zip(axes, (core, spot // 2, spot % 2)):
                values = jnp.where(bit == 1, jnp.flip(values, axis), values)
            return values

        hidden_bias = turn(vectors[:, 2 * q_width :].reshape(4, 2, 2, 2, piece), (1, 2, 3))
        hidden_bias = hidden_bias.transpose(1, 2, 3, 0, 4).reshape(4, 1, width)

        normed_one, queries, own_kv, weights = project(
            place,
            rows_one,
            rows_two,
            row(first_gain),
            row(first_shift),
            local_attention.reshape(4, 2, piece, width),
            near_a,
            other_a,
            q_bias,
            v_bias,
        )
        flat_weights = weights.reshape(-1, width)
        side_u = across(line_f[:, 0], 2)
        side_d = across(line_f[:, 1], 4)
        far_kv = across(own_kv, 1)
        far_kv, side_u, side_d = tie(far_kv, side_u, side_d)
        first_u = jnp.stack([line_f[:, 0], side_u])
        first_d = jnp.stack([line_f[:, 1], side_d])
        second_u = across(first_u, 4)
        second_d = across(first_d, 2)
        grads_one, grads_two = to_rows(grads_one, grads_two, dp_size)
        flags_one, flags_two = to_rows(flags_one, flags_two, dp_size)
        first_u_far = across(first_u, 1)
        first_d_far = across(first_d, 1)
        context, log_total, mid_rows, normed_two = attend(
            queries,
            own_kv,
            far_kv,
            seg_q,
            seg_k,
            rows_one,
            rows_two,
            flat_weights,
            row(out_bias),
            row(second_gain),
            row(second_shift),
        )
        mid_rows, second_u, second_d, grads_one, grads_two, flags_one, flags_two = tie(
            mid_rows, second_u, second_d, grads_one, grads_two, flags_one, flags_two
        )
        second_u_far = across(second_u, 1)
        second_d_far = across(second_d, 1)
        flags_in = jnp.concatenate([flags_one, flags_two], axis=0)[:, None]
        grads_in = jnp.concatenate([grads_one, grads_two], axis=0)
        ups = (first_u, second_u, first_u_far, second_u_far)
        downs = (first_d, second_d, first_d_far, second_d_far)
        local_up = local_up.reshape(8, piece, width)
        local_down = down_weight.reshape(8, piece, width)
        active, slope, final_rows = expand(
            place, normed_two, mid_rows, hidden_bias, local_up, local_down, ups, downs, row(down_bias)
        )
        back_one, back_two = from_rows(final_rows[:strip], final_rows[strip:], dp_size)

        up_other, down_other, normed_grad, bias_other = expand_back(
            1, place, grads_in, normed_two, active, slope, local_up, local_down, ups[2:], downs[2:], None
        )
        up_got = across(up_other, 1)
        down_got = across(down_other, 1)
        up_own, down_own, normed_grad, bias_own = expand_back(
            0, place, grads_in, normed_two, active, slope, local_up, local_down, ups[:2], downs[:2], normed_grad
        )
        back_one, back_two, normed_grad = tie(back_one, back_two, normed_grad)
        grad_mid, grad_attn, grad_context, sums_two = settle(
            normed_grad, mid_rows, grads_in, row(second_gain), flat_weights
        )
        up_got, down_got, grad_context = tie(up_got, down_got, grad_context)
        up_sent = across(add(up_own[1], up_got[1]), 4)
        down_sent = across(add(down_own[1], down_got[1]), 2)
        up_kept = add(up_own[0], up_got[0])
        down_kept = add(down_own[0], down_got[0])
        dq, own_grad, far_grad = attend_back(
            queries, own_kv, far_kv, grad_context, context, log_total, seg_q, seg_k
        )
        up_sent, down_sent, dq, far_grad = tie(up_sent, down_sent, dq, far_grad)
        got_kv = across(far_grad, 1)
        up_kept = add(up_kept, up_sent)
        down_kept = add(down_kept, down_sent)
        up_sent = across(up_kept[1], 2)
        down_sent = across(down_kept[1], 4)
        attention_other = weigh(1, place, dq, own_grad, got_kv, context, normed_one, grad_attn)
        attention_got = across(attention_other, 1)
        attention_own = weigh(0, place, dq, own_grad, got_kv, context, normed_one, grad_attn)
        up_sent, down_sent, attention_got, attention_own = tie(up_sent, down_sent, attention_got, attention_own)
        pair = jnp.stack([add(up_kept[0], up_sent), add(down_kept[0], down_sent)], axis=1)
        pair_sent = swap_mp(pair[2:], 1)
        attention_grad = plane_scatter(add(attention_own, attention_got), dp_size)
        out_one, out_two, sums_one = finish(
            dq, own_grad, got_kv, weights, rows_one, rows_two, row(first_gain), grad_mid, flags_in
        )
        pair_sent, out_one, out_two, sums_one, bias_own = tie(pair_sent, out_one, out_two, sums_one, bias_own)
        pair = add(pair[:2], pair_sent)
        pair_sent = swap_mp(pair[1], 2)
        start_one, start_two = from_rows(out_one, out_two, dp_size)

        def placed(values):
            values = jnp.stack([values[i] for i in (0, 2, 1, 3)]).reshape(2, 2, -1)
            for axis, bit in ((0, mp_at // 2), (1, mp_at % 2)):
                values = jnp.where(bit == 1, jnp.flip(values, axis), values)
            return values.reshape(4, -1)

        hidden_sum = jnp.concatenate([bias_own, bias_other]).reshape(2, 2, 2, 4, piece)
        hidden_sum = turn(hidden_sum.transpose(3, 0, 1, 2, 4), (1, 2, 3)).reshape(4, width)
        qv_sum = jnp.concatenate([sums_one[3].reshape(4, -1), sums_one[4].reshape(4, -1)], axis=1)
        small = jnp.concatenate(
            [sums_one[:3], sums_two[:4], placed(qv_sum).reshape(2, width), placed(hidden_sum)], axis=0
        )
        bits = [1 << n for n in range(dp_size.bit_length() - 1)]
        for bit in bits[:2]:
            small = small + across(small, bit)
        pair_sent, attention_grad, small = tie(pair_sent, attention_grad, small)
        attention_sent = swap_mp(attention_grad[2:], 1)

        def gather_back(value):
            for bit in bits[3:]:
                value = value + across(value, bit)
            near = plane_gather(value, dp_size)
            other = across(near, 1)
            return jnp.stack([jnp.where(core == 0, near, other), jnp.where(core == 0, other, near)])

        for bit in bits[2:]:
            small = small + across(small, bit)
        attention_sent, pair, small = tie(attention_sent, pair, small)
        pair = gather_back(add(pair[0], pair_sent))
        attention_grad = add(attention_grad[:2], attention_sent)
        attention_sent = swap_mp(attention_grad[1], 2)
        for bit in (1, 2):
            small = small + swap_mp(small, bit)
        attention_grad = gather_back(add(attention_grad[0], attention_sent)).reshape(4, 2 * piece, width)

        activations = jnp.where(
            parity == 0, jnp.stack([back_one, back_two]), jnp.stack([back_two, back_one])
        )
        grad_start = jnp.where(
            parity == 0, jnp.stack([start_one, start_two]), jnp.stack([start_two, start_one])
        )
        tokens_grad = jnp.where((mask_flags == 1)[:, :, None], 0.0, grad_start.astype(F32))
        up_weight_grad = pair[:, :, 0].reshape(width, width).astype(F32).T
        down_weight_grad = pair[:, :, 1].reshape(width, width).astype(F32)
        w_qkv_grad = attention_grad[:3].astype(F32).transpose(0, 2, 1)
        w_out_grad = attention_grad[3].astype(F32)
        qv_bias_grad = lax.dynamic_index_in_dim(small[7:9].reshape(4, 2, -1), mp_at, 0, keepdims=False)
        up_bias_grad = lax.dynamic_index_in_dim(small[9:13], mp_at, 0, keepdims=False)
        return (
            activations,
            tokens_grad,
            small[0],
            small[1],
            small[2],
            w_qkv_grad,
            qv_bias_grad,
            w_out_grad,
            small[3],
            small[4],
            small[5],
            up_weight_grad,
            up_bias_grad,
            down_weight_grad,
            small[6],
        )

    return body


def solution(mesh):
    in_specs = (
        P("dp", "mp", None),
        P("dp", None),
        P("dp", "mp"),
        P(),
        P(),
        P(),
        P(None, None, "mp"),
        P(None, "mp"),
        P("mp", None),
        P(),
        P(),
        P(),
        P(None, "mp"),
        P("mp"),
        P("mp", None),
        P(),
        P("dp", "mp", None),
    )
    out_specs = (
        P("dp", "mp", None),
        P("dp", "mp", None),
        P(),
        P(),
        P(),
        P(None, None, "mp"),
        P(None, "mp"),
        P("mp", None),
        P(),
        P(),
        P(),
        P(None, "mp"),
        P("mp"),
        P("mp", None),
        P(),
    )
    return jax.shard_map(
        make_body(mesh.shape["dp"]), mesh=mesh, in_specs=in_specs, out_specs=out_specs, check_vma=False
    )
```

```python
import jax
import jax.numpy as jnp
from jax import lax
from jax.experimental import pallas as pl
from jax.experimental.pallas import tpu as pltpu
from jax.sharding import PartitionSpec as P

HD = 64
EPSILON = 1e-06
NEG_FILL = -1e30
BF = jnp.bfloat16
F32 = jnp.float32
BOTH = ("dp", "mp")
BLOCK_ORDER = (0, 2, 1, 3)
NT = (((1,), (1,)), ((), ()))
NN = (((1,), (0,)), ((), ()))
TN = (((0,), (0,)), ((), ()))


def dot(left, right, dims):
    return lax.dot_general(left, right, dims, preferred_element_type=F32)


def swap_dp(value, bit, dp_size):
    return lax.ppermute(value, "dp", [(i, i ^ bit) for i in range(dp_size)])


def swap_mp(value, bit):
    return lax.ppermute(value, "mp", [(i, i ^ bit) for i in range(4)])


def row_routes(dp_size):
    first, second = [], []
    for pair in range(dp_size // 2):
        for core in range(2):
            for place in range(4):
                source = (2 * pair + core) * 4 + place
                for row in range(2):
                    target = (2 * pair + place // 2) * 4 + 2 * core + row
                    (first if row == place % 2 else second).append((source, target))
    return first, second


def to_rows(first, second, dp_size):
    routes = row_routes(dp_size)
    return (lax.ppermute(first, BOTH, routes[0]), lax.ppermute(second, BOTH, routes[1]))


def from_rows(first, second, dp_size):
    back = [[(target, source) for source, target in route] for route in row_routes(dp_size)]
    return (lax.ppermute(first, BOTH, back[0]), lax.ppermute(second, BOTH, back[1]))


EXTRA = 16
MIB_ATTEND = 18
COST = pl.CostEstimate(flops=1000000, transcendentals=0, bytes_accessed=1000)


def plane_groups(dp_size):
    return [[base * 8 + core + 2 * k for k in range(4)] for base in range(dp_size // 8) for core in range(2)]


def plane_gather(value, dp_size):
    spread = jnp.broadcast_to(value[None], (4,) + value.shape)
    return lax.all_to_all(spread, "dp", 0, 0, tiled=True, axis_index_groups=plane_groups(dp_size))


def plane_scatter(value, dp_size):
    pieces = lax.all_to_all(value, "dp", 0, 0, tiled=True, axis_index_groups=plane_groups(dp_size))
    return jnp.sum(pieces.astype(F32), axis=0).astype(BF)


def tie(*values):
    return lax.optimization_barrier(values)


def add(left, right):
    return (left.astype(F32) + right.astype(F32)).astype(BF)


def whole(value):
    rank = value.ndim
    return pl.BlockSpec(value.shape, lambda *i: (0,) * rank, pipeline_mode=pl.Buffered(1))


def scalars():
    return pl.BlockSpec(memory_space=pltpu.SMEM)


def call(kernel, name, mib, grid, in_specs, out_specs, out_shape, scratch, flops, moved, args):
    return pl.pallas_call(
        kernel,
        grid=grid,
        in_specs=in_specs,
        out_specs=out_specs,
        out_shape=out_shape,
        scratch_shapes=scratch,
        compiler_params=pltpu.CompilerParams(vmem_limit_bytes=mib << 20),
        cost_estimate=COST,
        name=name,
    )(*args)


def centre(rows):
    row_mean = jnp.mean(rows, axis=-1, keepdims=True)
    centred = rows - row_mean
    variance = jnp.mean(centred * centred, axis=-1, keepdims=True)
    inv_scale = lax.rsqrt(variance + EPSILON)
    return (centred * inv_scale, inv_scale)


def centre_back(incoming, unit_rows, inv_scale, gain):
    scaled = incoming * gain
    inner_one = jnp.mean(scaled, axis=-1, keepdims=True)
    inner_two = jnp.mean(scaled * unit_rows, axis=-1, keepdims=True)
    return inv_scale * (scaled - inner_one - unit_rows * inner_two)


def project_kernel(place, one, two, gain, shift, local, near, other, q_bias, v_bias, normed, q, kv, weights):
    strip = normed.shape[0] // 2
    for i, rows in enumerate((one, two)):
        unit, _ = centre(rows[:strip].astype(F32))
        normed[i * strip : (i + 1) * strip] = (unit * gain[...] + shift[...]).astype(BF)
    core = place[0]
    weights[:, 0] = local[...]
    for k in range(4):
        weights[2 * core + k // 2, 1:4, k % 2] = near[k]
        weights[2 - 2 * core + k // 2, 1:4, k % 2] = other[k]
    width = one.shape[1]
    rows = normed[...]
    q[...] = (dot(rows, weights[0].reshape(width, width), NT) + q_bias[...]).astype(BF)
    kv[0] = dot(rows, weights[1].reshape(width, width), NT).astype(BF)
    kv[1] = (dot(rows, weights[2].reshape(width, width), NT) + v_bias[...]).astype(BF)


def project(place, one, two, gain, shift, local, near, other, q_bias, v_bias):
    width = one.shape[1]
    tokens = 2 * (one.shape[0] - EXTRA)
    args = (place, one, two, gain, shift, local, near, other, q_bias, v_bias)
    shapes = [
        jax.ShapeDtypeStruct((tokens, width), BF),
        jax.ShapeDtypeStruct((tokens, width), BF),
        jax.ShapeDtypeStruct((2, tokens, width), BF),
        jax.ShapeDtypeStruct((4, 4, 2, width // 8, width), BF),
    ]
    return call(
        project_kernel,
        "project",
        24,
        (1,),
        [scalars()] + [whole(x) for x in args[1:]],
        [whole(x) for x in shapes],
        shapes,
        [],
        6 * tokens * width * width,
        12 * width * width,
        args,
    )


def attend_kernel(q_ref, own_ref, far_ref, segq_ref, segk_ref, weights, *refs):
    one, two, o_bias, gain, shift, ctx_ref, lse_ref, mid_ref, normed_ref, keys, values_t, total = refs
    half = own_ref.shape[1]
    keys[:half] = own_ref[0]
    keys[half:] = far_ref[0]
    values_t[:, :half] = own_ref[1].T
    values_t[:, half:] = far_ref[1].T
    tokens = q_ref.shape[0]
    block = 256
    step = pl.program_id(0)
    for start in range(0, tokens, block):
        span = slice(start, start + block)
        same = segk_ref[...] == segq_ref[:, span]
        query = q_ref[span, :] * jnp.asarray(HD**-0.5, BF)
        lanes = lax.broadcasted_iota(jnp.int32, query.shape, 1)
        pieces = []
        for head in range(2):
            own = (lanes >= HD) if head else (lanes < HD)
            scores = dot(keys[...], jnp.where(own, query, jnp.zeros_like(query)), NT)
            scores = jnp.where(same, scores, NEG_FILL)
            row_max = jnp.max(scores, axis=0, keepdims=True)
            exp_scores = jnp.exp(scores - row_max)
            row_total = jnp.sum(exp_scores, axis=0, keepdims=True)
            part = dot(values_t[head * HD : (head + 1) * HD, :], exp_scores.astype(BF), NN)
            pieces.append(part / row_total)
            lse_ref[0, head : head + 1, span] = row_max + jnp.log(row_total)
        context = jnp.concatenate(pieces, axis=0).T.astype(BF)
        ctx_ref[span, :] = context
        mixed = dot(context, weights[...], NN)

        @pl.when(step == 0)
        def _():
            total[span, :] = mixed

        @pl.when(step > 0)
        def _():
            total[span, :] += mixed

    @pl.when(step == pl.num_programs(0) - 1)
    def _():
        strip = tokens // 2
        for i, rows in enumerate((one, two)):
            span = slice(i * strip, (i + 1) * strip)
            mid = rows[:strip].astype(F32) + total[span, :] + o_bias[...]
            mid_ref[span, :] = mid
            unit, _ = centre(mid)
            normed_ref[span, :] = (unit * gain[...] + shift[...]).astype(BF)


def attend(q, own, far, seg_q, seg_k, weights, one, two, o_bias, gain, shift):
    rows, width = q.shape
    pairs = width // 128
    half = own.shape[1]
    args = (q, own, far, seg_q, seg_k, weights, one, two, o_bias, gain, shift)
    head_block = pl.BlockSpec((rows, 128), lambda i: (0, i))
    key_block = pl.BlockSpec((2, half, 128), lambda i: (0, 0, i))
    shapes = [
        jax.ShapeDtypeStruct((rows, width), BF),
        jax.ShapeDtypeStruct((pairs, 2, rows), F32),
        jax.ShapeDtypeStruct((rows, width), F32),
        jax.ShapeDtypeStruct((rows, width), BF),
    ]
    specs = [head_block, key_block, key_block, whole(seg_q), whole(seg_k)]
    specs.append(pl.BlockSpec((128, width), lambda i: (3 * pairs + i, 0)))
    return call(
        attend_kernel,
        "attend",
        MIB_ATTEND,
        (pairs,),
        specs + [whole(x) for x in args[6:]],
        [head_block, pl.BlockSpec((1, 2, rows), lambda i: (i, 0, 0)), whole(shapes[2]), whole(shapes[3])],
        shapes,
        [pltpu.VMEM((2 * half, 128), BF), pltpu.VMEM((128, 2 * half), BF), pltpu.VMEM((rows, width), F32)],
        0,
        0,
        args,
    )


def load_block(place, flip, at_y, mat, local, pieces, block):
    core = place[0] if not flip else 1 - place[0]
    line, along_x, along_y, diagonal = pieces
    for x in range(2):
        spot = place[1 + 2 * at_y + x]
        block[x, 0] = local[core * 4 + spot]
        if at_y and x:
            block[x, 1:4] = diagonal[...]
        else:
            block[x, 1:4] = (along_y if at_y else along_x if x else line)[mat]


def expand_kernel(
    place, normed, mid, bias, local_up, local_down, line, line_far, xs, xs_far, ys, ys_far, du, du_far, dd, dd_far,
    d_bias, active, slope, out, up, down, total,
):
    step = pl.program_id(0)
    for j in range(4):

        @pl.when(step == j)
        def _():
            flip = j // 2
            three = (line_far, xs_far, ys_far) if flip else (line, xs, ys)
            load_block(place, flip, j % 2, 0, local_up, three + ((du_far if flip else du),), up)
            load_block(place, flip, j % 2, 1, local_down, three + ((dd_far if flip else dd),), down)

    width = normed.shape[1]
    hidden = dot(normed[...], up[...].reshape(width, width), NT) + bias[0]
    cdf = 0.5 * (1.0 + lax.erf(hidden * (0.5**0.5)))
    pulled = cdf + hidden * jnp.exp(-0.5 * hidden * hidden) * 0.3989422804014327
    slope[...] = pulled.astype(BF)
    active[...] = (hidden * cdf).astype(BF)
    part = dot(active[...], down[...].reshape(width, width), NN)

    @pl.when(step == 0)
    def _():
        total[...] = mid[...] + d_bias[...] + part

    @pl.when((step > 0) & (step < 3))
    def _():
        total[...] += part

    @pl.when(step == 3)
    def _():
        out[...] = (total[...] + part).astype(BF)


def expand(place, normed, mid, bias, local_up, local_down, pieces, d_bias):
    tokens, width = normed.shape
    piece = width // 8
    args = (place, normed, mid, bias, local_up, local_down, *pieces, d_bias)
    hidden = pl.BlockSpec((tokens, width), lambda j: (0, j))
    shapes = [
        jax.ShapeDtypeStruct((tokens, 4 * width), BF),
        jax.ShapeDtypeStruct((tokens, 4 * width), BF),
        jax.ShapeDtypeStruct((tokens, width), BF),
    ]
    specs = [scalars()] + [whole(x) for x in args[1:]]
    specs[3] = pl.BlockSpec((1, 1, width), lambda j: (j, 0, 0))
    return call(
        expand_kernel,
        "expand",
        32,
        (4,),
        specs,
        [hidden, hidden, whole(shapes[2])],
        shapes,
        [pltpu.VMEM((2, 4, piece, width), BF)] * 2 + [pltpu.VMEM((tokens, width), F32)],
        16 * tokens * width * width,
        20 * width * width,
        args,
    )


def expand_back_kernel(
    flip, place, grad, normed, active, slope, local_up, local_down, line, xs, ys, du, dd, before,
    up_grad, down_grad, normed_grad, bias_grad, up, down,
):
    step = pl.program_id(0)
    for j in range(2):

        @pl.when(step == j)
        def _():
            load_block(place, flip, j, 0, local_up, (line, xs, ys, du), up)
            load_block(place, flip, j, 1, local_down, (line, xs, ys, dd), down)

    width = normed.shape[1]
    wide = up.shape
    incoming = dot(grad[...], down[...].reshape(width, width), NT)
    grad_hidden = (incoming * slope[...].astype(F32)).astype(BF)
    bias_grad[0] = jnp.sum(grad_hidden.astype(F32), axis=0, keepdims=True)
    down_grad[...] = dot(active[...], grad[...], TN).astype(BF).reshape(2, 1, *wide[1:])
    up_grad[0] = dot(grad_hidden, normed[...], TN).astype(BF).reshape(wide)
    part = dot(grad_hidden, up[...].reshape(width, width), NN)

    @pl.when(step == 0)
    def _():
        if before is None:
            normed_grad[...] = part
        else:
            normed_grad[...] = before[...] + part

    @pl.when(step > 0)
    def _():
        normed_grad[...] += part


def expand_back(flip, place, grad, normed, active, slope, local_up, local_down, pieces, before):
    tokens, width = normed.shape
    piece = width // 8
    args = (place, grad, normed, active, slope, local_up, local_down, *pieces)
    if before is not None:
        args = args + (before,)

    def kernel(*refs):
        if before is None:
            refs = refs[:12] + (None,) + refs[12:]
        return expand_back_kernel(flip, *refs)

    hidden = pl.BlockSpec((tokens, width), lambda j: (0, j + 2 * flip))
    shapes = [
        jax.ShapeDtypeStruct((2, 2, 4, piece, width), BF),
        jax.ShapeDtypeStruct((2, 2, 4, piece, width), BF),
        jax.ShapeDtypeStruct((tokens, width), F32),
        jax.ShapeDtypeStruct((2, 1, width), F32),
    ]
    specs = [scalars()] + [whole(x) for x in args[1:]]
    specs[3] = specs[4] = hidden
    return call(
        kernel,
        "expand_back_other" if flip else "expand_back_own",
        32,
        (2,),
        specs,
        [
            pl.BlockSpec((1, 2, 4, piece, width), lambda j: (j, 0, 0, 0, 0)),
            pl.BlockSpec((2, 1, 4, piece, width), lambda j: (0, j, 0, 0, 0)),
            whole(shapes[2]),
            pl.BlockSpec((1, 1, width), lambda j: (j, 0, 0)),
        ],
        shapes,
        [pltpu.VMEM((2, 4, piece, width), BF)] * 2,
        20 * tokens * width * width,
        16 * width * width,
        args,
    )


def settle_kernel(incoming, mid, grad, gain, wo, grad_mid, grad_attn, grad_context, sums):
    strip = 256
    parts = None
    for at in range(0, mid.shape[0], strip):
        span = slice(at, at + strip)
        unit, inv_scale = centre(mid[span, :])
        given = incoming[span, :]
        outer = grad[span, :].astype(F32)
        made = outer + centre_back(given, unit, inv_scale, gain[...])
        grad_mid[span, :] = made
        grad_attn[span, :] = made.astype(BF)
        grad_context[span, :] = dot(made.astype(BF), wo[...], NT).astype(BF)
        rows = [jnp.sum(v, axis=0, keepdims=True) for v in (made, given * unit, given, outer)]
        parts = rows if parts is None else [a + b for a, b in zip(parts, rows)]
    for i, row in enumerate(parts):
        sums[i : i + 1, :] = row


def settle(incoming, mid, grad, gain, weights):
    tokens, width = mid.shape
    args = (incoming, mid, grad, gain, weights)
    specs = [whole(x) for x in args]
    specs[4] = pl.BlockSpec((width, width), lambda i: (3, 0))
    shapes = [
        jax.ShapeDtypeStruct((tokens, width), F32),
        jax.ShapeDtypeStruct((tokens, width), BF),
        jax.ShapeDtypeStruct((tokens, width), BF),
        jax.ShapeDtypeStruct((8, width), F32),
    ]
    return call(
        settle_kernel,
        "settle",
        16,
        (1,),
        specs,
        [whole(x) for x in shapes],
        shapes,
        [],
        2 * tokens * width * width,
        14 * tokens * width,
        args,
    )


def merge_kernel(up_kept, up_got, down_kept, down_got, kept, sent):
    for i, (own, got) in enumerate(((up_kept, up_got), (down_kept, down_got))):
        kept[:, i] = (own[:2].astype(F32) + got[:2].astype(F32)).astype(BF)
        sent[:, i] = (own[2:].astype(F32) + got[2:].astype(F32)).astype(BF)


def merge(up_kept, up_got, down_kept, down_got):
    args = (up_kept, up_got, down_kept, down_got)
    shapes = [jax.ShapeDtypeStruct((2, 2) + up_kept.shape[1:], BF)] * 2
    return call(
        merge_kernel,
        "merge",
        12,
        (1,),
        [whole(x) for x in args],
        [whole(x) for x in shapes],
        shapes,
        [],
        0,
        0,
        args,
    )


def close_pair_kernel(place, near, other, up_grad, down_grad, small):
    width = near.shape[2]
    piece = width // 8
    for c in range(2):
        for ref, core in ((near, place[0]), (other, 1 - place[0])):

            @pl.when(core == c)
            def _():
                for k in range(4):
                    at = (4 * c + k) * piece
                    down_grad[at : at + piece, :] = ref[k, piece : 2 * piece].astype(F32)
                rows = jnp.concatenate([ref[k, :piece] for k in range(4)], axis=0)
                up_grad[:, 4 * c * piece : 4 * (c + 1) * piece] = rows.astype(F32).T

    total = None
    for k in range(4):
        for at in (2 * piece, 2 * piece + EXTRA):
            part = near[k, at : at + EXTRA].astype(F32)
            total = part if total is None else total + part
    small[...] = total


def close_pair(place, near, other):
    width = near.shape[2]
    args = (place, near, other)
    shapes = [
        jax.ShapeDtypeStruct((width, width), F32),
        jax.ShapeDtypeStruct((width, width), F32),
        jax.ShapeDtypeStruct((EXTRA, width), F32),
    ]
    return call(
        close_pair_kernel,
        "close_pair",
        20,
        (1,),
        [scalars(), whole(near), whole(other)],
        [whole(x) for x in shapes],
        shapes,
        [],
        0,
        0,
        args,
    )


def close_attention_kernel(place, near, other, qkv_grad, out_grad):
    piece = near.shape[1]
    for c in range(2):
        for ref, core in ((near, place[0]), (other, 1 - place[0])):

            @pl.when(core == c)
            def _():
                for k in range(4):
                    span = slice(k % 2 * piece, (k % 2 + 1) * piece)
                    part = ref[k].astype(F32)
                    if 2 * c + k // 2 < 3:
                        qkv_grad[2 * c + k // 2, span, :] = part
                    else:
                        out_grad[span, :] = part


def close_attention(place, near, other):
    piece, width = near.shape[1:]
    args = (place, near, other)
    shapes = [
        jax.ShapeDtypeStruct((3, 2 * piece, width), F32),
        jax.ShapeDtypeStruct((2 * piece, width), F32),
    ]
    return call(
        close_attention_kernel,
        "close_attention",
        20,
        (1,),
        [scalars(), whole(near), whole(other)],
        [whole(x) for x in shapes],
        shapes,
        [],
        0,
        0,
        args,
    )


def flip_kernel(value, out):
    out[...] = value[...].T


def flip(value):
    shape = jax.ShapeDtypeStruct(value.shape[::-1], value.dtype)
    return call(flip_kernel, "flip", 8, (1,), [whole(value)], whole(shape), shape, [], 0, 0, (value,))


def weigh_kernel(flip, place, dq, mine, got, context, normed, grad, before, out, left, right):
    core = place[0] if not flip else 1 - place[0]
    width = dq.shape[1]
    piece = width // 8

    @pl.when(core == 0)
    def _():
        left[0] = dq[...]
        left[1] = (mine[0].astype(F32) + got[0].astype(F32)).astype(BF)
        right[...] = normed[...]

    @pl.when(core == 1)
    def _():
        left[0] = (mine[1].astype(F32) + got[1].astype(F32)).astype(BF)
        left[1] = context[...]
        right[...] = grad[...]

    for i in range(2):
        rows = normed[...] if i == 0 else right[...]
        made = dot(left[i], rows, TN).reshape(4, 2, piece, width)
        for k in range(2):
            part = made[:, k]
            if before is not None:
                part = part + before[2 * i + k].astype(F32)
            out[2 * i + k] = part.astype(BF)


def weigh(flip, place, dq, mine, got, context, normed, grad, before):
    tokens, width = dq.shape
    args = (place, dq, mine, got, context, normed, grad)
    if before is not None:
        args = args + (before,)

    def kernel(*refs):
        if before is None:
            refs = refs[:7] + (None,) + refs[7:]
        return weigh_kernel(flip, *refs)

    shape = jax.ShapeDtypeStruct((4, 4, width // 8, width), BF)
    return call(
        kernel,
        "weigh_other" if flip else "weigh_own",
        20,
        (1,),
        [scalars()] + [whole(x) for x in args[1:]],
        whole(shape),
        shape,
        [pltpu.VMEM((2, tokens, width), BF), pltpu.VMEM((tokens, width), BF)],
        4 * tokens * width * width,
        8 * width * width,
        args,
    )


def finish_kernel(dq, mine, got, weights, one, two, gain, grad_mid, out_one, out_two, sums, total):
    width = dq.shape[1]
    keys = (mine[0].astype(F32) + got[0].astype(F32)).astype(BF)
    values = (mine[1].astype(F32) + got[1].astype(F32)).astype(BF)
    total[...] = dot(dq[...], weights[0].reshape(width, width), NN)
    total[...] += dot(keys, weights[1].reshape(width, width), NN)
    total[...] += dot(values, weights[2].reshape(width, width), NN)
    strip = dq.shape[0] // 2
    gathered = None
    for i, rows in enumerate((one, two)):
        span = slice(i * strip, (i + 1) * strip)
        unit, inv_scale = centre(rows[:strip].astype(F32))
        incoming = total[span, :]
        grad_start = grad_mid[span, :] + centre_back(incoming, unit, inv_scale, gain[...])
        high = grad_start.astype(BF)
        (out_two if i else out_one)[...] = high
        low = (grad_start - high.astype(F32)).astype(BF)
        flags = rows[strip : strip + 16, :strip]
        masked = (dot(flags, high, NN) + dot(flags, low, NN))[:1]
        parts = [masked] + [jnp.sum(v, axis=0, keepdims=True) for v in (incoming * unit, incoming)]
        gathered = parts if gathered is None else [a + b for a, b in zip(gathered, parts)]
    gathered.append(jnp.sum(dq[...].astype(F32), axis=0, keepdims=True))
    gathered.append(jnp.sum(values.astype(F32), axis=0, keepdims=True))
    for i, row in enumerate(gathered):
        sums[i : i + 1, :] = row


def finish(dq, mine, got, weights, one, two, gain, grad_mid):
    tokens, width = dq.shape
    args = (dq, mine, got, weights, one, two, gain, grad_mid)
    specs = [whole(x) for x in args]
    specs[3] = pl.BlockSpec((3,) + weights.shape[1:], lambda i: (0,) * 5)
    shapes = [
        jax.ShapeDtypeStruct((tokens // 2, width), BF),
        jax.ShapeDtypeStruct((tokens // 2, width), BF),
        jax.ShapeDtypeStruct((8, width), F32),
    ]
    return call(
        finish_kernel,
        "finish",
        20,
        (1,),
        specs,
        [whole(x) for x in shapes],
        shapes,
        [pltpu.VMEM((tokens, width), F32)],
        6 * tokens * width * width,
        12 * width * width,
        args,
    )


def attend_back_kernel(
    q_ref,
    own_ref,
    far_ref,
    g_ref,
    ctx_ref,
    lse_ref,
    segq_ref,
    segk_ref,
    dq_ref,
    own_grad_ref,
    far_grad_ref,
    keys,
    keys_t,
    values,
    dk_total,
    dv_total,
):
    half = own_ref.shape[1]
    keys[:half] = own_ref[0]
    keys[half:] = far_ref[0]
    keys_t[:, :half] = own_ref[0].T
    keys_t[:, half:] = far_ref[0].T
    values[:half] = own_ref[1]
    values[half:] = far_ref[1]
    total = q_ref.shape[0]
    block = 256
    scale = jnp.asarray(HD**-0.5, BF)
    for start in range(0, total, block):
        span = slice(start, start + block)
        same = segk_ref[...] == segq_ref[:, span]
        query = q_ref[span, :] * scale
        grad = g_ref[span, :]
        product = (grad.astype(F32) * ctx_ref[span, :].astype(F32)).T
        lanes = lax.broadcasted_iota(jnp.int32, query.shape, 1)
        pieces = []
        for head in range(2):
            own = (lanes >= HD) if head else (lanes < HD)
            query_own = jnp.where(own, query, jnp.zeros_like(query))
            grad_own = jnp.where(own, grad, jnp.zeros_like(grad))
            scores = dot(keys[...], query_own, NT)
            probs = jnp.exp(jnp.where(same, scores, NEG_FILL) - lse_ref[0, head : head + 1, span])
            grad_probs = dot(values[...], grad_own, NT)
            row_dot = jnp.sum(product[head * HD : (head + 1) * HD, :], axis=0, keepdims=True)
            grad_scores = (probs * (grad_probs - row_dot)).astype(BF)
            dv = dot(probs.astype(BF), grad_own, NN)
            dk = dot(grad_scores, query_own, NN)
            if start == 0 and head == 0:
                dv_total[...] = dv
                dk_total[...] = dk
            else:
                dv_total[...] += dv
                dk_total[...] += dk
            pieces.append(dot(keys_t[head * HD : (head + 1) * HD, :], grad_scores, NN))
        dq_ref[span, :] = (jnp.concatenate(pieces, axis=0).T * HD**-0.5).astype(BF)
    own_grad_ref[0] = dk_total[:half].astype(BF)
    far_grad_ref[0] = dk_total[half:].astype(BF)
    own_grad_ref[1] = dv_total[:half].astype(BF)
    far_grad_ref[1] = dv_total[half:].astype(BF)


def attend_back(q, own, far, grad, ctx, lse, seg_q, seg_k):
    rows, width = q.shape
    pairs = width // 128
    half = own.shape[1]
    args = (q, own, far, grad, ctx, lse, seg_q, seg_k)
    head_block = pl.BlockSpec((rows, 128), lambda i: (0, i))
    key_block = pl.BlockSpec((2, half, 128), lambda i: (0, 0, i))
    lse_block = pl.BlockSpec((1, 2, rows), lambda i: (i, 0, 0))
    shapes = [jax.ShapeDtypeStruct((rows, width), BF)] + [jax.ShapeDtypeStruct((2, half, width), BF)] * 2
    return call(
        attend_back_kernel,
        "attend_back",
        MIB_ATTEND,
        (pairs,),
        [head_block, key_block, key_block, head_block, head_block, lse_block, whole(seg_q), whole(seg_k)],
        [head_block, key_block, key_block],
        shapes,
        [
            pltpu.VMEM((2 * half, 128), BF),
            pltpu.VMEM((128, 2 * half), BF),
            pltpu.VMEM((2 * half, 128), BF),
            pltpu.VMEM((2 * half, 128), F32),
            pltpu.VMEM((2 * half, 128), F32),
        ],
        0,
        0,
        args,
    )


def make_body(dp_size):
    def body(
        tokens,
        segment_ids,
        mask_flags,
        mask_embed,
        first_gain,
        first_shift,
        query_key_value_weight,
        qv_bias,
        output_weight,
        out_bias,
        second_gain,
        second_shift,
        up_weight,
        expand_bias,
        down_weight,
        down_bias,
        out_grad,
    ):
        dp_at = lax.axis_index("dp")
        mp_at = lax.axis_index("mp")
        core = dp_at % 2
        spot = (dp_at // 2) % 4
        parity = mp_at % 2
        width = tokens.shape[2]
        strip = tokens.shape[1]
        piece = width // 8
        place = jnp.stack([core] + [spot ^ r for r in range(4)]).astype(jnp.int32)

        def across(value, bit):
            return swap_dp(value, bit, dp_size)

        def pick(values):
            return (
                lax.dynamic_index_in_dim(values, parity, 0, keepdims=False),
                lax.dynamic_index_in_dim(values, 1 - parity, 0, keepdims=False),
            )

        def row(vector):
            return vector.reshape(1, -1)

        local_attention = jnp.concatenate(
            [query_key_value_weight.transpose(0, 2, 1).reshape(-1, width), output_weight], axis=0
        )
        offset = (core * 4 + spot) * piece
        vectors = jnp.concatenate([qv_bias.reshape(-1), expand_bias])
        vector_high = vectors.astype(BF)
        vector_low = (vectors - vector_high.astype(F32)).astype(BF)
        vector_rows = jnp.concatenate([vector_high, vector_low]).reshape(-1, width)
        share_a = jnp.concatenate(
            [
                lax.dynamic_slice_in_dim(local_attention, offset, piece, 0),
                jnp.pad(vector_rows, ((0, EXTRA - vector_rows.shape[0]), (0, 0))),
            ],
            axis=0,
        )
        local_up = flip(up_weight)
        share_f = jnp.stack(
            [
                lax.dynamic_slice_in_dim(local_up, offset, piece, 0),
                lax.dynamic_slice_in_dim(down_weight, offset, piece, 0),
            ]
        )
        start_rows = jnp.where((mask_flags == 1)[:, :, None], mask_embed.astype(BF), tokens)
        flag_rows = jnp.pad(mask_flags.astype(BF)[:, None, :], ((0, 0), (0, 0), (0, width - strip)))
        segment_rows = segment_ids.astype(BF).reshape(segment_ids.shape[0], 2, -1)
        segment_rows = jnp.pad(segment_rows, ((0, 0), (0, EXTRA - 3), (0, width - segment_rows.shape[2])))
        messages = jnp.concatenate([start_rows, flag_rows, segment_rows], axis=1)
        rows_one, rows_two = pick(messages)
        grads_one, grads_two = pick(out_grad)

        def line_of(share, far):
            near = swap_mp(jnp.stack([share, far]), 1)
            return jnp.stack([far, near[0], near[1]])

        far_a = swap_mp(share_a, 2)
        far_a, share_f = tie(far_a, share_f)
        line_a = line_of(share_a, far_a)
        far_f = swap_mp(share_f, 2)
        line_a, far_f, rows_one, rows_two = tie(line_a, far_f, rows_one, rows_two)
        near_a = plane_gather(line_a[:, :piece], dp_size)
        rows_one, rows_two = to_rows(rows_one, rows_two, dp_size)
        near_f = swap_mp(jnp.stack([share_f, far_f]), 1)
        line_f = jnp.stack([far_f, near_f[0], near_f[1]], axis=1)
        got = line_a[:, piece : piece + vector_rows.shape[0]].astype(F32).reshape(3, 2, -1)
        vectors = jnp.concatenate([vectors[None], got[:, 0] + got[:, 1]])
        q_width = qv_bias.shape[1]
        q_bias = vectors[:, :q_width].reshape(1, -1)
        v_bias = vectors[:, q_width : 2 * q_width].reshape(1, -1)

        def turn(values, axes):
            for axis, bit in zip(axes, (core, spot // 2, spot % 2)):
                values = jnp.where(bit == 1, jnp.flip(values, axis), values)
            return values

        hidden_bias = turn(vectors[:, 2 * q_width :].reshape(4, 2, 2, 2, piece), (1, 2, 3))
        hidden_bias = hidden_bias.transpose(1, 2, 3, 0, 4).reshape(4, 1, width)

        local_rows = local_attention.reshape(4, 2, piece, width)
        rows_one, rows_two, line_f, near_a, local_rows, local_up, grads_one, grads_two, hidden_bias, q_bias = tie(
            rows_one, rows_two, line_f, near_a, local_rows, local_up, grads_one, grads_two, hidden_bias, q_bias
        )
        other_a = across(near_a, 1)
        xs = across(line_f, 2)
        ys = across(line_f, 4)
        grads_one, grads_two = to_rows(grads_one, grads_two, dp_size)

        quarters = rows_one[strip + 1 : strip + 3, : 2 * strip].astype(jnp.int32).reshape(4, strip)

        def quarter(at):
            return lax.dynamic_index_in_dim(quarters, at, 0, keepdims=False)

        own_segments = jnp.concatenate([quarter(2 * core + parity), quarter(2 * core + 1 - parity)])
        far_segments = jnp.concatenate([quarter(2 - 2 * core + parity), quarter(3 - 2 * core - parity)])
        seg_q = own_segments[None, :]
        seg_k = jnp.concatenate([own_segments, far_segments])[:, None]

        normed_one, queries, own_kv, weights = project(
            place,
            rows_one,
            rows_two,
            row(first_gain),
            row(first_shift),
            local_rows,
            near_a,
            other_a,
            q_bias,
            v_bias,
        )
        flat_weights = weights.reshape(-1, width)
        xs, ys, own_kv, line_f, seg_q, seg_k, grads_one, grads_two = tie(
            xs, ys, own_kv, line_f, seg_q, seg_k, grads_one, grads_two
        )
        grads_in = jnp.concatenate([grads_one, grads_two], axis=0)
        far_kv = across(own_kv, 1)
        du = across(xs[0], 4)
        dd = across(ys[1], 2)
        line_far = across(line_f, 1)
        xs_far = across(xs, 1)
        ys_far = across(ys, 1)
        far_kv, line_far, grads_in, xs_far, ys_far = tie(far_kv, line_far, grads_in, xs_far, ys_far)
        heads = (queries, own_kv, far_kv)
        context, log_total, mid_rows, normed_two = attend(
            *heads,
            seg_q,
            seg_k,
            flat_weights,
            rows_one,
            rows_two,
            row(out_bias),
            row(second_gain),
            row(second_shift),
        )
        du, dd, normed_two = tie(du, dd, normed_two)
        du_far = across(du, 1)
        dd_far = across(dd, 1)
        local_up = local_up.reshape(8, piece, width)
        local_down = down_weight.reshape(8, piece, width)
        both = (line_f, line_far, xs, xs_far, ys, ys_far, du, du_far, dd, dd_far)
        active, slope, final_rows = expand(
            place, normed_two, mid_rows, hidden_bias, local_up, local_down, both, row(down_bias)
        )

        back_one, back_two = from_rows(final_rows[:strip], final_rows[strip:], dp_size)
        up_other, down_other, normed_grad, bias_other = expand_back(
            1, place, grads_in, normed_two, active, slope, local_up, local_down, both[1::2], None
        )
        up_got = across(up_other, 1)
        down_got = across(down_other, 1)
        up_own, down_own, normed_grad, bias_own = expand_back(
            0, place, grads_in, normed_two, active, slope, local_up, local_down, both[0::2], normed_grad
        )
        up_got, down_got, normed_grad = tie(up_got, down_got, normed_grad)
        up_sent = add(up_own[1], up_got[1])
        down_sent = add(down_own[1], down_got[1])
        up_sent, down_sent, normed_grad = tie(up_sent, down_sent, normed_grad)
        up_sent = across(up_sent, 4)
        down_sent = across(down_sent, 2)
        grad_mid, grad_attn, grad_context, sums_two = settle(
            normed_grad, mid_rows, grads_in, row(second_gain), flat_weights
        )
        up_kept = add(up_own[0], up_got[0])
        down_kept = add(down_own[0], down_got[0])
        up_kept, down_kept, grad_context = tie(up_kept, down_kept, grad_context)
        inputs = heads + (grad_context, context, log_total, seg_q, seg_k)
        dq, own_grad, far_grad = attend_back(*inputs)
        up_sent, down_sent, far_grad, back_one, back_two = tie(up_sent, down_sent, far_grad, back_one, back_two)
        got_kv = across(far_grad, 1)
        up_second = add(up_kept[1], up_sent[1])
        down_second = add(down_kept[1], down_sent[1])
        up_second, down_second, got_kv, grad_mid, up_kept, down_kept = tie(
            up_second, down_second, got_kv, grad_mid, up_kept, down_kept
        )
        up_second = across(up_second, 2)
        down_second = across(down_second, 4)
        out_one, out_two, sums_one = finish(
            dq, own_grad, got_kv, weights, rows_one, rows_two, row(first_gain), grad_mid
        )
        out_one, out_two, got_kv, sums_one = tie(out_one, out_two, got_kv, sums_one)
        start_one, start_two = from_rows(out_one, out_two, dp_size)
        attention_other = weigh(1, place, dq, own_grad, got_kv, context, normed_one, grad_attn, None)
        attention_got = across(attention_other, 1)
        up_kept = add(up_kept[0], up_sent[0])
        down_kept = add(down_kept[0], down_sent[0])
        up_second, down_second, attention_got, up_kept, down_kept = tie(
            up_second, down_second, attention_got, up_kept, down_kept
        )
        attention_grad = weigh(0, place, dq, own_grad, got_kv, context, normed_one, grad_attn, attention_got)
        start_one, start_two, attention_grad, up_kept = tie(start_one, start_two, attention_grad, up_kept)
        attention_grad = plane_scatter(attention_grad, dp_size)
        pair, pair_sent = merge(up_kept, up_second, down_kept, down_second)
        pair_sent = swap_mp(pair_sent, 1)

        def placed(values):
            values = jnp.stack([values[i] for i in (0, 2, 1, 3)]).reshape(2, 2, -1)
            for axis, bit in ((0, mp_at // 2), (1, mp_at % 2)):
                values = jnp.where(bit == 1, jnp.flip(values, axis), values)
            return values.reshape(4, -1)

        hidden_sum = jnp.concatenate([bias_own, bias_other]).reshape(2, 2, 2, 4, piece)
        hidden_sum = turn(hidden_sum.transpose(3, 0, 1, 2, 4), (1, 2, 3)).reshape(4, width)
        qv_sum = jnp.concatenate([sums_one[3].reshape(4, -1), sums_one[4].reshape(4, -1)], axis=1)
        small = jnp.concatenate(
            [sums_one[:3], sums_two[:4], placed(qv_sum).reshape(2, width), placed(hidden_sum)], axis=0
        )
        bits = [1 << n for n in range(dp_size.bit_length() - 1)]
        small = small + across(small, 1)
        pair_sent, small = tie(pair_sent, small)
        pair = add(pair, pair_sent)
        small = small + swap_mp(small, 1)
        pair_sent = swap_mp(pair[1], 2)
        activations = jnp.where(
            parity == 0, jnp.stack([back_one, back_two]), jnp.stack([back_two, back_one])
        )
        grad_start = jnp.where(
            parity == 0, jnp.stack([start_one, start_two]), jnp.stack([start_two, start_one])
        )
        tokens_grad = jnp.where((mask_flags == 1)[:, :, None], 0.0, grad_start.astype(F32))

        def lift(value):
            for bit in bits[3:]:
                value = value + across(value, bit)
            return value

        small, activations, tokens_grad = tie(small, activations, tokens_grad)
        small = small + swap_mp(small, 2)
        small = jnp.pad(lift(small), ((0, EXTRA - small.shape[0]), (0, 0)))
        small_high = small.astype(BF)
        small_low = (small - small_high.astype(F32)).astype(BF)
        attention_grad, pair, pair_sent, small_high, small_low = tie(
            attention_grad, pair, pair_sent, small_high, small_low
        )
        attention_sent = swap_mp(attention_grad[2:], 1)
        pair = lift(add(pair[0], pair_sent)).reshape(2 * piece, width)
        pair = plane_gather(jnp.concatenate([pair, small_high, small_low], axis=0), dp_size)
        attention_grad = add(attention_grad[:2], attention_sent)
        attention_sent = swap_mp(attention_grad[1], 2)
        attention_sent, pair = tie(attention_sent, pair)
        attention_grad = lift(add(attention_grad[0], attention_sent))
        attention_grad = plane_gather(attention_grad, dp_size)
        up_weight_grad, down_weight_grad, small = close_pair(place, pair, across(pair, 1))
        attention_grad, up_weight_grad, down_weight_grad, small = tie(
            attention_grad, up_weight_grad, down_weight_grad, small
        )
        w_qkv_grad, w_out_grad = close_attention(place, attention_grad, across(attention_grad, 1))
        w_qkv_grad = w_qkv_grad.transpose(0, 2, 1)
        qv_bias_grad = lax.dynamic_index_in_dim(small[7:9].reshape(4, 2, -1), mp_at, 0, keepdims=False)
        up_bias_grad = lax.dynamic_index_in_dim(small[9:13], mp_at, 0, keepdims=False)
        return (
            activations,
            tokens_grad,
            small[0],
            small[1],
            small[2],
            w_qkv_grad,
            qv_bias_grad,
            w_out_grad,
            small[3],
            small[4],
            small[5],
            up_weight_grad,
            up_bias_grad,
            down_weight_grad,
            small[6],
        )

    return body


def solution(mesh):
    in_specs = (
        P("dp", "mp", None),
        P("dp", None),
        P("dp", "mp"),
        P(),
        P(),
        P(),
        P(None, None, "mp"),
        P(None, "mp"),
        P("mp", None),
        P(),
        P(),
        P(),
        P(None, "mp"),
        P("mp"),
        P("mp", None),
        P(),
        P("dp", "mp", None),
    )
    out_specs = (
        P("dp", "mp", None),
        P("dp", "mp", None),
        P(),
        P(),
        P(),
        P(None, None, "mp"),
        P(None, "mp"),
        P("mp", None),
        P(),
        P(),
        P(),
        P(None, "mp"),
        P("mp"),
        P("mp", None),
        P(),
    )
    return jax.shard_map(
        make_body(mesh.shape["dp"]), mesh=mesh, in_specs=in_specs, out_specs=out_specs, check_vma=False
    )
```

```python
import jax
import jax.numpy as jnp
from jax import lax
from jax.experimental import pallas as pl
from jax.experimental.pallas import tpu as pltpu
from jax.sharding import PartitionSpec as P

HD = 64
EPSILON = 1e-06
NEG_FILL = -1e30
BF = jnp.bfloat16
F32 = jnp.float32
BOTH = ("dp", "mp")
BLOCK_ORDER = (0, 2, 1, 3)
NT = (((1,), (1,)), ((), ()))
NN = (((1,), (0,)), ((), ()))
TN = (((0,), (0,)), ((), ()))


def dot(left, right, dims):
    return lax.dot_general(left, right, dims, preferred_element_type=F32)


def swap_dp(value, bit, dp_size):
    return lax.ppermute(value, "dp", [(i, i ^ bit) for i in range(dp_size)])


def swap_mp(value, bit):
    return lax.ppermute(value, "mp", [(i, i ^ bit) for i in range(4)])


def row_routes(dp_size):
    first, second = [], []
    for pair in range(dp_size // 2):
        for core in range(2):
            for place in range(4):
                source = (2 * pair + core) * 4 + place
                for row in range(2):
                    target = (2 * pair + place // 2) * 4 + 2 * core + row
                    (first if row == place % 2 else second).append((source, target))
    return first, second


def to_rows(first, second, dp_size):
    routes = row_routes(dp_size)
    return (lax.ppermute(first, BOTH, routes[0]), lax.ppermute(second, BOTH, routes[1]))


def from_rows(first, second, dp_size):
    back = [[(target, source) for source, target in route] for route in row_routes(dp_size)]
    return (lax.ppermute(first, BOTH, back[0]), lax.ppermute(second, BOTH, back[1]))


EXTRA = 16
SLOTS = 32
MIB_ATTEND = 18
COST = pl.CostEstimate(flops=1000000, transcendentals=0, bytes_accessed=1000)


def plane_groups(dp_size):
    return [[base * 8 + core + 2 * k for k in range(4)] for base in range(dp_size // 8) for core in range(2)]


def plane_gather(value, dp_size):
    spread = jnp.broadcast_to(value[None], (4,) + value.shape)
    return lax.all_to_all(spread, "dp", 0, 0, tiled=True, axis_index_groups=plane_groups(dp_size))


def plane_scatter(value, dp_size):
    pieces = lax.all_to_all(value, "dp", 0, 0, tiled=True, axis_index_groups=plane_groups(dp_size))
    return jnp.sum(pieces.astype(F32), axis=0).astype(BF)


def tie(*values):
    return lax.optimization_barrier(values)


def add(left, right):
    return (left.astype(F32) + right.astype(F32)).astype(BF)


def whole(value):
    rank = value.ndim
    return pl.BlockSpec(value.shape, lambda *i: (0,) * rank, pipeline_mode=pl.Buffered(1))


def scalars():
    return pl.BlockSpec(memory_space=pltpu.SMEM)


def call(kernel, name, mib, grid, in_specs, out_specs, out_shape, scratch, flops, moved, args):
    return pl.pallas_call(
        kernel,
        grid=grid,
        in_specs=in_specs,
        out_specs=out_specs,
        out_shape=out_shape,
        scratch_shapes=scratch,
        compiler_params=pltpu.CompilerParams(vmem_limit_bytes=mib << 20),
        cost_estimate=COST,
        name=name,
    )(*args)


def centre(rows):
    row_mean = jnp.mean(rows, axis=-1, keepdims=True)
    centred = rows - row_mean
    variance = jnp.mean(centred * centred, axis=-1, keepdims=True)
    inv_scale = lax.rsqrt(variance + EPSILON)
    return (centred * inv_scale, inv_scale)


def centre_back(incoming, unit_rows, inv_scale, gain):
    scaled = incoming * gain
    inner_one = jnp.mean(scaled, axis=-1, keepdims=True)
    inner_two = jnp.mean(scaled * unit_rows, axis=-1, keepdims=True)
    return inv_scale * (scaled - inner_one - unit_rows * inner_two)


def project_kernel(place, one, two, gain, shift, local, near, other, q_bias, v_bias, normed, q, kv, weights):
    strip = normed.shape[0] // 2
    for i, rows in enumerate((one, two)):
        unit, _ = centre(rows[:strip].astype(F32))
        normed[i * strip : (i + 1) * strip] = (unit * gain[...] + shift[...]).astype(BF)
    core = place[0]
    weights[:, 0] = local[...]
    for k in range(4):
        weights[2 * core + k // 2, 1:4, k % 2] = near[k]
        weights[2 - 2 * core + k // 2, 1:4, k % 2] = other[k]
    width = one.shape[1]
    rows = normed[...]
    q[...] = (dot(rows, weights[0].reshape(width, width), NT) + q_bias[...]).astype(BF)
    kv[0] = dot(rows, weights[1].reshape(width, width), NT).astype(BF)
    kv[1] = (dot(rows, weights[2].reshape(width, width), NT) + v_bias[...]).astype(BF)


def project(place, one, two, gain, shift, local, near, other, q_bias, v_bias):
    width = one.shape[1]
    tokens = 2 * (one.shape[0] - EXTRA)
    args = (place, one, two, gain, shift, local, near, other, q_bias, v_bias)
    shapes = [
        jax.ShapeDtypeStruct((tokens, width), BF),
        jax.ShapeDtypeStruct((tokens, width), BF),
        jax.ShapeDtypeStruct((2, tokens, width), BF),
        jax.ShapeDtypeStruct((4, 4, 2, width // 8, width), BF),
    ]
    return call(
        project_kernel,
        "project",
        20,
        (1,),
        [scalars()] + [whole(x) for x in args[1:]],
        [whole(x) for x in shapes],
        shapes,
        [],
        6 * tokens * width * width,
        12 * width * width,
        args,
    )


def spare_base(head):
    return 0 if head else HD


def head_lanes(shape, head):
    lanes = lax.broadcasted_iota(jnp.int32, shape, 1)
    return (lanes >= HD) if head else (lanes < HD)


def upright(line):
    return jnp.broadcast_to(line, (128, line.shape[1])).T


def prepare_lanes(segk_ref, segq_ref, key_extra, query_extra):
    for segments, extra, is_key in ((segk_ref, key_extra, True), (segq_ref, query_extra, False)):
        ids = upright(segments[...])
        for head in range(2):
            lanes = lax.broadcasted_iota(jnp.int32, ids.shape, 1) - spare_base(head)
            inside = (lanes >= 0) & (lanes < 4)
            if is_key:
                values = jnp.where(inside & (ids != lanes), NEG_FILL, 0.0)
            else:
                values = jnp.where(inside & (ids == lanes), 1.0, 0.0)
            extra[head] = values.astype(BF)


def attend_kernel(
    q_ref, own_ref, far_ref, segq_ref, segk_ref, weights, one, two, o_bias, gain, shift,
    ctx_ref, lse_ref, mid_ref, normed_ref, keys, values_t, key_extra, query_extra, total,
):
    half = own_ref.shape[1]
    step = pl.program_id(0)

    @pl.when(step == 0)
    def _():
        prepare_lanes(segk_ref, segq_ref, key_extra, query_extra)
        for head in range(2):
            values_t[head, HD:] = jnp.ones_like(values_t[head, HD:])

    for i, ref in enumerate((own_ref, far_ref)):
        span = slice(i * half, (i + 1) * half)
        part = ref[0]
        turned = ref[1].T
        for head in range(2):
            keys[head, span] = jnp.where(head_lanes(part.shape, head), part, key_extra[head, span])
            values_t[head, :HD, span] = turned[head * HD : (head + 1) * HD]
    tokens = q_ref.shape[0]
    block = tokens
    for start in range(0, tokens, block):
        span = slice(start, start + block)
        query = q_ref[span, :] * jnp.asarray(HD**-0.5, BF)
        heads = range(2)
        owns = [jnp.where(head_lanes(query.shape, h), query, query_extra[h, span]) for h in heads]
        scores = [dot(keys[h], owns[h], NT) for h in heads]
        maxima = [jnp.max(v, axis=0, keepdims=True) for v in scores]
        powers = [jnp.exp(v - m).astype(BF) for v, m in zip(scores, maxima)]
        parts = [dot(values_t[h], powers[h], NN) for h in heads]
        pieces = [v[:HD] / v[HD : HD + 1] for v in parts]
        sums = [m + jnp.log(v[HD : HD + 1]) for m, v in zip(maxima, parts)]
        context = jnp.concatenate(pieces, axis=0).T.astype(BF)
        ctx_ref[span, :] = context
        for h in heads:
            lse_ref[0, h : h + 1, span] = sums[h]
        mixed = dot(context, weights[...], NN)

        @pl.when(step == 0)
        def _():
            total[span, :] = mixed

        @pl.when(step > 0)
        def _():
            total[span, :] += mixed

    @pl.when(step == pl.num_programs(0) - 1)
    def _():
        strip = tokens // 2
        for i, rows in enumerate((one, two)):
            span = slice(i * strip, (i + 1) * strip)
            mid = rows[:strip].astype(F32) + total[span, :] + o_bias[...]
            mid_ref[span, :] = mid
            unit, _ = centre(mid)
            normed_ref[span, :] = (unit * gain[...] + shift[...]).astype(BF)


def attend(q, own, far, seg_q, seg_k, weights, one, two, o_bias, gain, shift):
    rows, width = q.shape
    pairs = width // 128
    half = own.shape[1]
    args = (q, own, far, seg_q, seg_k, weights, one, two, o_bias, gain, shift)
    head_block = pl.BlockSpec((rows, 128), lambda i: (0, i))
    key_block = pl.BlockSpec((2, half, 128), lambda i: (0, 0, i))
    shapes = [
        jax.ShapeDtypeStruct((rows, width), BF),
        jax.ShapeDtypeStruct((pairs, 2, rows), F32),
        jax.ShapeDtypeStruct((rows, width), F32),
        jax.ShapeDtypeStruct((rows, width), BF),
    ]
    specs = [head_block, key_block, key_block, whole(seg_q), whole(seg_k)]
    specs.append(pl.BlockSpec((128, width), lambda i: (3 * pairs + i, 0)))
    return call(
        attend_kernel,
        "attend",
        20,
        (pairs,),
        specs + [whole(x) for x in args[6:]],
        [head_block, pl.BlockSpec((1, 2, rows), lambda i: (i, 0, 0)), whole(shapes[2]), whole(shapes[3])],
        shapes,
        [
            pltpu.VMEM((2, 2 * half, 128), BF),
            pltpu.VMEM((2, HD + 16, 2 * half), BF),
            pltpu.VMEM((2, 2 * half, 128), BF),
            pltpu.VMEM((2, rows, 128), BF),
            pltpu.VMEM((rows, width), F32),
        ],
        0,
        0,
        args,
    )


def load_block(place, flip, at_y, mat, local, pieces, block):
    core = place[0] if not flip else 1 - place[0]
    line, along_x, along_y, diagonal = pieces
    for x in range(2):
        spot = place[1 + 2 * at_y + x]
        block[x, 0] = local[core * 4 + spot]
        if at_y and x:
            block[x, 1:4] = diagonal[...]
        else:
            block[x, 1:4] = (along_y if at_y else along_x if x else line)[mat]


def expand_kernel(
    place, normed, mid, bias, local_up, local_down, line, line_far, xs, xs_far, ys, ys_far, du, du_far, dd, dd_far,
    d_bias, active, slope, out, up, down, total,
):
    step = pl.program_id(0)
    for j in range(4):

        @pl.when(step == j)
        def _():
            flip = j // 2
            three = (line_far, xs_far, ys_far) if flip else (line, xs, ys)
            load_block(place, flip, j % 2, 0, local_up, three + ((du_far if flip else du),), up)
            load_block(place, flip, j % 2, 1, local_down, three + ((dd_far if flip else dd),), down)

    width = normed.shape[1]
    hidden = dot(normed[...], up[...].reshape(width, width), NT) + bias[0]
    cdf = 0.5 * (1.0 + lax.erf(hidden * (0.5**0.5)))
    pulled = cdf + hidden * jnp.exp(-0.5 * hidden * hidden) * 0.3989422804014327
    slope[...] = pulled.astype(BF)
    active[...] = (hidden * cdf).astype(BF)
    part = dot(active[...], down[...].reshape(width, width), NN)

    @pl.when(step == 0)
    def _():
        total[...] = mid[...] + d_bias[...] + part

    @pl.when((step > 0) & (step < 3))
    def _():
        total[...] += part

    @pl.when(step == 3)
    def _():
        out[...] = (total[...] + part).astype(BF)


def expand(place, normed, mid, bias, local_up, local_down, pieces, d_bias):
    tokens, width = normed.shape
    piece = width // 8
    args = (place, normed, mid, bias, local_up, local_down, *pieces, d_bias)
    hidden = pl.BlockSpec((tokens, width), lambda j: (0, j))
    shapes = [
        jax.ShapeDtypeStruct((tokens, 4 * width), BF),
        jax.ShapeDtypeStruct((tokens, 4 * width), BF),
        jax.ShapeDtypeStruct((tokens, width), BF),
    ]
    specs = [scalars()] + [whole(x) for x in args[1:]]
    specs[3] = pl.BlockSpec((1, 1, width), lambda j: (j, 0, 0))
    return call(
        expand_kernel,
        "expand",
        28,
        (4,),
        specs,
        [hidden, hidden, whole(shapes[2])],
        shapes,
        [pltpu.VMEM((2, 4, piece, width), BF)] * 2 + [pltpu.VMEM((tokens, width), F32)],
        16 * tokens * width * width,
        20 * width * width,
        args,
    )


def expand_back_kernel(
    flip, place, grad_one, grad_two, normed, active, slope, local_up, local_down, line, xs, ys, du, dd, before,
    up_grad, down_grad, normed_grad, bias_grad, up, down,
):
    step = pl.program_id(0)
    for j in range(2):

        @pl.when(step == j)
        def _():
            load_block(place, flip, j, 0, local_up, (line, xs, ys, du), up)
            load_block(place, flip, j, 1, local_down, (line, xs, ys, dd), down)

    width = normed.shape[1]
    wide = up.shape
    grad = jnp.concatenate([grad_one[...], grad_two[...]], axis=0)
    incoming = dot(grad, down[...].reshape(width, width), NT)
    grad_hidden = (incoming * slope[...].astype(F32)).astype(BF)
    hidden_sum = jnp.sum(grad_hidden.astype(F32), axis=0, keepdims=True)
    piece = wide[2]
    core = place[0] if not flip else 1 - place[0]

    @pl.when(step == 0)
    def _():
        bias_grad[...] = jnp.zeros_like(bias_grad)

    for x in range(2):
        spot = jnp.where(step == 0, place[1 + x], place[3 + x])
        for i, distance in enumerate(BLOCK_ORDER):
            at = (4 * x + i) * piece
            entry = place[5 + distance] * 8 + core * 4 + spot
            bias_grad[pl.ds(entry, 1), :piece] = hidden_sum[:, at : at + piece]
    down_grad[...] = dot(active[...], grad, TN).astype(BF).reshape(2, 1, *wide[1:])
    up_grad[0] = dot(grad_hidden, normed[...], TN).astype(BF).reshape(wide)
    part = dot(grad_hidden, up[...].reshape(width, width), NN)

    @pl.when(step == 0)
    def _():
        if before is None:
            normed_grad[...] = part
        else:
            normed_grad[...] = before[...] + part

    @pl.when(step > 0)
    def _():
        normed_grad[...] += part


def expand_back(flip, place, grad, normed, active, slope, local_up, local_down, pieces, before):
    tokens, width = normed.shape
    piece = width // 8
    args = (place, *grad, normed, active, slope, local_up, local_down, *pieces)
    if before is not None:
        args = args + (before,)

    def kernel(*refs):
        if before is None:
            refs = refs[:13] + (None,) + refs[13:]
        return expand_back_kernel(flip, *refs)

    hidden = pl.BlockSpec((tokens, width), lambda j: (0, j + 2 * flip))
    shapes = [
        jax.ShapeDtypeStruct((2, 2, 4, piece, width), BF),
        jax.ShapeDtypeStruct((2, 2, 4, piece, width), BF),
        jax.ShapeDtypeStruct((tokens, width), F32),
        jax.ShapeDtypeStruct((SLOTS, 128), F32),
    ]
    specs = [scalars()] + [whole(x) for x in args[1:]]
    specs[4] = specs[5] = hidden
    return call(
        kernel,
        "expand_back_other" if flip else "expand_back_own",
        26,
        (2,),
        specs,
        [
            pl.BlockSpec((1, 2, 4, piece, width), lambda j: (j, 0, 0, 0, 0)),
            pl.BlockSpec((2, 1, 4, piece, width), lambda j: (0, j, 0, 0, 0)),
            whole(shapes[2]),
            whole(shapes[3]),
        ],
        shapes,
        [pltpu.VMEM((2, 4, piece, width), BF)] * 2,
        20 * tokens * width * width,
        16 * width * width,
        args,
    )


def settle_kernel(incoming, mid, grad_one, grad_two, gain, wo, grad_mid, grad_attn, grad_context, sums):
    strip = grad_one.shape[0]
    parts = None
    for at in range(0, mid.shape[0], strip):
        span = slice(at, at + strip)
        unit, inv_scale = centre(mid[span, :])
        given = incoming[span, :]
        outer = (grad_two if at else grad_one)[...].astype(F32)
        made = outer + centre_back(given, unit, inv_scale, gain[...])
        grad_mid[span, :] = made
        grad_attn[span, :] = made.astype(BF)
        grad_context[span, :] = dot(made.astype(BF), wo[...], NT).astype(BF)
        rows = [jnp.sum(v, axis=0, keepdims=True) for v in (made, given * unit, given, outer)]
        parts = rows if parts is None else [a + b for a, b in zip(parts, rows)]
    for i, row in enumerate(parts):
        sums[i : i + 1, :] = row


def settle(incoming, mid, grad, gain, weights):
    tokens, width = mid.shape
    args = (incoming, mid, *grad, gain, weights)
    specs = [whole(x) for x in args]
    specs[5] = pl.BlockSpec((width, width), lambda i: (3, 0))
    shapes = [
        jax.ShapeDtypeStruct((tokens, width), F32),
        jax.ShapeDtypeStruct((tokens, width), BF),
        jax.ShapeDtypeStruct((tokens, width), BF),
        jax.ShapeDtypeStruct((8, width), F32),
    ]
    return call(
        settle_kernel,
        "settle",
        13,
        (1,),
        specs,
        [whole(x) for x in shapes],
        shapes,
        [],
        2 * tokens * width * width,
        14 * tokens * width,
        args,
    )


def quarter_block(value, at):
    rank = value.ndim
    shape = (1,) * len(at) + value.shape[len(at) :]
    return pl.BlockSpec(shape, lambda *i: at + (0,) * (rank - len(at)), pipeline_mode=pl.Buffered(1))


def onward_kernel(*refs):
    for i in range(2):
        own, got, sent = (ref[...].astype(F32) for ref in refs[3 * i : 3 * i + 3])
        refs[6 + i][...] = (own[0, 0] + got[0, 0] + sent[0]).astype(BF)


def onward(up, down):
    args = up + down
    shape = jax.ShapeDtypeStruct(up[0].shape[2:], BF)
    return call(
        onward_kernel,
        "onward",
        12,
        (1,),
        [quarter_block(x, (0, 1) if x.ndim == 5 else (1,)) for x in args],
        [whole(shape)] * 2,
        [shape] * 2,
        [],
        0,
        0,
        args,
    )


def merge_kernel(*refs):
    kept, passed = refs[8:]
    for i in range(2):
        own, got, sent, second = refs[4 * i : 4 * i + 4]
        for part, out in ((slice(0, 2), kept), (slice(2, 4), passed)):
            total = own[0, 0, part].astype(F32) + got[0, 0, part].astype(F32)
            total = total + sent[0, part].astype(F32) + second[part].astype(F32)
            out[:, i] = total.astype(BF)


def merge(up, down):
    args = up + down
    shapes = [jax.ShapeDtypeStruct((2, 2) + up[0].shape[3:], BF)] * 2
    specs = [
        quarter_block(x, (0, 0)) if x.ndim == 5 else quarter_block(x, (0,)) if x.ndim == 4 else whole(x) for x in args
    ]
    return call(merge_kernel, "merge", 12, (1,), specs, [whole(x) for x in shapes], shapes, [], 0, 0, args)


def close_pair_kernel(place, near, other, up_grad, down_grad, vectors, up_bias, qv_bias):
    width = near.shape[2]
    piece = width // 8
    for c in range(2):
        for ref, core in ((near, place[0]), (other, 1 - place[0])):

            @pl.when(core == c)
            def _():
                for k in range(4):
                    at = (4 * c + k) * piece
                    down_grad[at : at + piece, :] = ref[k, piece : 2 * piece].astype(F32)
                rows = jnp.concatenate([ref[k, :piece] for k in range(4)], axis=0)
                up_grad[:, 4 * c * piece : 4 * (c + 1) * piece] = rows.astype(F32).T

    total = None
    for k in range(4):
        for at in (2 * piece, 2 * piece + EXTRA):
            part = near[k, at : at + EXTRA].astype(F32)
            total = part if total is None else total + part
    vectors[...] = total[:8]

    def slot(entry):
        r, g = 7 + entry // 6, entry % 6
        return total[r : r + 1, 128 * g : 128 * g + piece]

    for z in range(4):

        @pl.when(place[5] == z)
        def _():
            for k in range(8):
                up_bias[:, k * piece : (k + 1) * piece] = slot(8 * z + k)
            for i in range(2):
                for half in range(2):
                    qv_bias[i : i + 1, half * piece : (half + 1) * piece] = slot(32 + 8 * i + 2 * z + half)


def close_pair(place, near, other):
    width = near.shape[2]
    args = (place, near, other)
    shapes = [
        jax.ShapeDtypeStruct((width, width), F32),
        jax.ShapeDtypeStruct((width, width), F32),
        jax.ShapeDtypeStruct((8, width), F32),
        jax.ShapeDtypeStruct((1, width), F32),
        jax.ShapeDtypeStruct((2, width // 4), F32),
    ]
    return call(
        close_pair_kernel,
        "close_pair",
        12,
        (1,),
        [scalars(), whole(near), whole(other)],
        [whole(x) for x in shapes],
        shapes,
        [],
        0,
        0,
        args,
    )


def close_attention_kernel(place, near, other, qkv_grad, out_grad):
    piece = near.shape[1]
    for c in range(2):
        for ref, core in ((near, place[0]), (other, 1 - place[0])):

            @pl.when(core == c)
            def _():
                for k in range(4):
                    span = slice(k % 2 * piece, (k % 2 + 1) * piece)
                    part = ref[k].astype(F32)
                    if 2 * c + k // 2 < 3:
                        qkv_grad[2 * c + k // 2, span, :] = part
                    else:
                        out_grad[span, :] = part


def close_attention(place, near, other):
    piece, width = near.shape[1:]
    args = (place, near, other)
    shapes = [
        jax.ShapeDtypeStruct((3, 2 * piece, width), F32),
        jax.ShapeDtypeStruct((2 * piece, width), F32),
    ]
    return call(
        close_attention_kernel,
        "close_attention",
        6,
        (1,),
        [scalars(), whole(near), whole(other)],
        [whole(x) for x in shapes],
        shapes,
        [],
        0,
        0,
        args,
    )


def flip_kernel(value, out):
    out[...] = value[...].T


def flip(value):
    shape = jax.ShapeDtypeStruct(value.shape[::-1], value.dtype)
    return call(flip_kernel, "flip", 4, (1,), [whole(value)], whole(shape), shape, [], 0, 0, (value,))


def weigh_kernel(flip, place, dq, mine, got, context, normed, grad, before, out, left, right):
    core = place[0] if not flip else 1 - place[0]
    width = dq.shape[1]
    piece = width // 8

    @pl.when(core == 0)
    def _():
        left[0] = dq[...]
        left[1] = (mine[0].astype(F32) + got[0].astype(F32)).astype(BF)
        right[...] = normed[...]

    @pl.when(core == 1)
    def _():
        left[0] = (mine[1].astype(F32) + got[1].astype(F32)).astype(BF)
        left[1] = context[...]
        right[...] = grad[...]

    for i in range(2):
        rows = normed[...] if i == 0 else right[...]
        made = dot(left[i], rows, TN).reshape(4, 2, piece, width)
        for k in range(2):
            part = made[:, k]
            if before is not None:
                part = part + before[2 * i + k].astype(F32)
            out[2 * i + k] = part.astype(BF)


def weigh(flip, place, dq, mine, got, context, normed, grad, before):
    tokens, width = dq.shape
    args = (place, dq, mine, got, context, normed, grad)
    if before is not None:
        args = args + (before,)

    def kernel(*refs):
        if before is None:
            refs = refs[:7] + (None,) + refs[7:]
        return weigh_kernel(flip, *refs)

    shape = jax.ShapeDtypeStruct((4, 4, width // 8, width), BF)
    return call(
        kernel,
        "weigh_other" if flip else "weigh_own",
        18,
        (1,),
        [scalars()] + [whole(x) for x in args[1:]],
        whole(shape),
        shape,
        [pltpu.VMEM((2, tokens, width), BF), pltpu.VMEM((tokens, width), BF)],
        4 * tokens * width * width,
        8 * width * width,
        args,
    )


def finish_kernel(
    place, dq, mine, got, weights, one, two, gain, grad_mid, sums_two, bias_own, bias_other,
    out_one, out_two, small, total,
):
    width = dq.shape[1]
    keys = (mine[0].astype(F32) + got[0].astype(F32)).astype(BF)
    values = (mine[1].astype(F32) + got[1].astype(F32)).astype(BF)
    total[...] = dot(dq[...], weights[0].reshape(width, width), NN)
    total[...] += dot(keys, weights[1].reshape(width, width), NN)
    total[...] += dot(values, weights[2].reshape(width, width), NN)
    strip = dq.shape[0] // 2
    gathered = None
    for i, rows in enumerate((one, two)):
        span = slice(i * strip, (i + 1) * strip)
        unit, inv_scale = centre(rows[:strip].astype(F32))
        incoming = total[span, :]
        grad_start = grad_mid[span, :] + centre_back(incoming, unit, inv_scale, gain[...])
        high = grad_start.astype(BF)
        (out_two if i else out_one)[...] = high
        low = (grad_start - high.astype(F32)).astype(BF)
        flags = rows[strip : strip + 16, :strip]
        masked = (dot(flags, high, NN) + dot(flags, low, NN))[:1]
        parts = [masked] + [jnp.sum(v, axis=0, keepdims=True) for v in (incoming * unit, incoming)]
        gathered = parts if gathered is None else [a + b for a, b in zip(gathered, parts)]
    small[...] = jnp.zeros_like(small)
    gathered += [sums_two[i : i + 1, :] for i in range(4)]
    for r, line in enumerate(gathered):
        for g in range(width // 128):
            small[16 * g + r : 16 * g + r + 1, :] = line[:, 128 * g : 128 * g + 128]
    hidden = bias_own[...] + bias_other[...]
    for entry in range(32):
        at = 16 * (entry % 6) + 7 + entry // 6
        small[at : at + 1, :] = hidden[entry : entry + 1, :]
    piece = width // 8
    for i, value in enumerate((dq[...], values)):
        line = jnp.sum(value.astype(F32), axis=0, keepdims=True)
        for j, distance in enumerate(BLOCK_ORDER):
            for half in range(2):
                entry = 32 + 8 * i + place[5 + distance] * 2 + half
                at = 16 * lax.rem(entry, 6) + 7 + entry // 6
                span = slice((2 * j + half) * piece, (2 * j + half + 1) * piece)
                small[pl.ds(at, 1), :piece] = line[:, span]


def finish(place, dq, mine, got, weights, one, two, gain, grad_mid, sums_two, bias_own, bias_other):
    tokens, width = dq.shape
    args = (place, dq, mine, got, weights, one, two, gain, grad_mid, sums_two, bias_own, bias_other)
    specs = [scalars()] + [whole(x) for x in args[1:]]
    specs[4] = pl.BlockSpec((3,) + weights.shape[1:], lambda i: (0,) * 5, pipeline_mode=pl.Buffered(1))
    shapes = [
        jax.ShapeDtypeStruct((tokens // 2, width), BF),
        jax.ShapeDtypeStruct((tokens // 2, width), BF),
        jax.ShapeDtypeStruct((96, 128), F32),
    ]
    return call(
        finish_kernel,
        "finish",
        17,
        (1,),
        specs,
        [whole(x) for x in shapes],
        shapes,
        [pltpu.VMEM((tokens, width), F32)],
        0,
        0,
        args,
    )


def pack_kernel(kept, got, small, out):
    piece, width = kept.shape[2:]
    for i in range(2):
        out[i * piece : (i + 1) * piece, :] = (kept[0, i].astype(F32) + got[i].astype(F32)).astype(BF)
    for g in range(width // 128):
        lanes = slice(128 * g, 128 * g + 128)
        value = small[16 * g : 16 * g + 16, :]
        high = value.astype(BF)
        out[2 * piece : 2 * piece + 16, lanes] = high
        out[2 * piece + 16 :, lanes] = (value - high.astype(F32)).astype(BF)


def pack(kept, got, small):
    piece, width = kept.shape[2:]
    args = (kept, got, small)
    shape = jax.ShapeDtypeStruct((2 * piece + 32, width), BF)
    specs = [quarter_block(kept, (0,)), whole(got), whole(small)]
    return call(pack_kernel, "pack", 4, (1,), specs, whole(shape), shape, [], 0, 0, args)


def attend_back_kernel(
    q_ref,
    own_ref,
    far_ref,
    g_ref,
    ctx_ref,
    lse_ref,
    segq_ref,
    segk_ref,
    dq_ref,
    own_grad_ref,
    far_grad_ref,
    keys,
    keys_t,
    values,
    dk_total,
    dv_total,
    key_ids,
):
    half = own_ref.shape[1]

    @pl.when(pl.program_id(0) == 0)
    def _():
        key_ids[...] = upright(segk_ref[...])

    keys[:half] = own_ref[0]
    keys[half:] = far_ref[0]
    keys_t[:, :half] = own_ref[0].T
    keys_t[:, half:] = far_ref[0].T
    values[:half] = own_ref[1]
    values[half:] = far_ref[1]
    total = q_ref.shape[0]
    block = 256
    scale = jnp.asarray(HD**-0.5, BF)
    for start in range(0, total, block):
        span = slice(start, start + block)
        same = key_ids[:, 0:1] == segq_ref[:, span]
        query = q_ref[span, :] * scale
        grad = g_ref[span, :]
        product = (grad.astype(F32) * ctx_ref[span, :].astype(F32)).T
        lanes = lax.broadcasted_iota(jnp.int32, query.shape, 1)
        pieces = []
        for head in range(2):
            own = (lanes >= HD) if head else (lanes < HD)
            query_own = jnp.where(own, query, jnp.zeros_like(query))
            grad_own = jnp.where(own, grad, jnp.zeros_like(grad))
            scores = dot(keys[...], query_own, NT)
            probs = jnp.exp(jnp.where(same, scores, NEG_FILL) - lse_ref[0, head : head + 1, span])
            grad_probs = dot(values[...], grad_own, NT)
            row_dot = jnp.sum(product[head * HD : (head + 1) * HD, :], axis=0, keepdims=True)
            grad_scores = (probs * (grad_probs - row_dot)).astype(BF)
            dv = dot(probs.astype(BF), grad_own, NN)
            dk = dot(grad_scores, query_own, NN)
            if start == 0 and head == 0:
                dv_total[...] = dv
                dk_total[...] = dk
            else:
                dv_total[...] += dv
                dk_total[...] += dk
            pieces.append(dot(keys_t[head * HD : (head + 1) * HD, :], grad_scores, NN))
        dq_ref[span, :] = (jnp.concatenate(pieces, axis=0).T * HD**-0.5).astype(BF)
    own_grad_ref[0] = dk_total[:half].astype(BF)
    far_grad_ref[0] = dk_total[half:].astype(BF)
    own_grad_ref[1] = dv_total[:half].astype(BF)
    far_grad_ref[1] = dv_total[half:].astype(BF)


def attend_back(q, own, far, grad, ctx, lse, seg_q, seg_k):
    rows, width = q.shape
    pairs = width // 128
    half = own.shape[1]
    args = (q, own, far, grad, ctx, lse, seg_q, seg_k)
    head_block = pl.BlockSpec((rows, 128), lambda i: (0, i))
    key_block = pl.BlockSpec((2, half, 128), lambda i: (0, 0, i))
    lse_block = pl.BlockSpec((1, 2, rows), lambda i: (i, 0, 0))
    shapes = [jax.ShapeDtypeStruct((rows, width), BF)] + [jax.ShapeDtypeStruct((2, half, width), BF)] * 2
    return call(
        attend_back_kernel,
        "attend_back",
        13,
        (pairs,),
        [head_block, key_block, key_block, head_block, head_block, lse_block, whole(seg_q), whole(seg_k)],
        [head_block, key_block, key_block],
        shapes,
        [
            pltpu.VMEM((2 * half, 128), BF),
            pltpu.VMEM((128, 2 * half), BF),
            pltpu.VMEM((2 * half, 128), BF),
            pltpu.VMEM((2 * half, 128), F32),
            pltpu.VMEM((2 * half, 128), F32),
            pltpu.VMEM((2 * half, 128), jnp.int32),
        ],
        0,
        0,
        args,
    )


def make_body(dp_size):
    def body(
        tokens,
        segment_ids,
        mask_flags,
        mask_embed,
        first_gain,
        first_shift,
        query_key_value_weight,
        qv_bias,
        output_weight,
        out_bias,
        second_gain,
        second_shift,
        up_weight,
        expand_bias,
        down_weight,
        down_bias,
        out_grad,
    ):
        dp_at = lax.axis_index("dp")
        mp_at = lax.axis_index("mp")
        core = dp_at % 2
        spot = (dp_at // 2) % 4
        parity = mp_at % 2
        width = tokens.shape[2]
        strip = tokens.shape[1]
        piece = width // 8
        place = jnp.stack([core] + [spot ^ r for r in range(4)] + [mp_at ^ d for d in range(4)]).astype(jnp.int32)

        def across(value, bit):
            return swap_dp(value, bit, dp_size)

        def pick(values):
            return (
                lax.dynamic_index_in_dim(values, parity, 0, keepdims=False),
                lax.dynamic_index_in_dim(values, 1 - parity, 0, keepdims=False),
            )

        def row(vector):
            return vector.reshape(1, -1)

        local_attention = jnp.concatenate(
            [query_key_value_weight.transpose(0, 2, 1).reshape(-1, width), output_weight], axis=0
        )
        offset = (core * 4 + spot) * piece
        vectors = jnp.concatenate([qv_bias.reshape(-1), expand_bias])
        vector_high = vectors.astype(BF)
        vector_low = (vectors - vector_high.astype(F32)).astype(BF)
        vector_rows = jnp.concatenate([vector_high, vector_low]).reshape(-1, width)
        share_a = jnp.concatenate(
            [
                lax.dynamic_slice_in_dim(local_attention, offset, piece, 0),
                jnp.pad(vector_rows, ((0, EXTRA - vector_rows.shape[0]), (0, 0))),
            ],
            axis=0,
        )
        local_up = flip(up_weight)
        share_f = jnp.stack(
            [
                lax.dynamic_slice_in_dim(local_up, offset, piece, 0),
                lax.dynamic_slice_in_dim(down_weight, offset, piece, 0),
            ]
        )
        start_rows = jnp.where((mask_flags == 1)[:, :, None], mask_embed.astype(BF), tokens)
        flag_rows = jnp.pad(mask_flags.astype(BF)[:, None, :], ((0, 0), (0, 0), (0, width - strip)))
        segment_rows = segment_ids.astype(BF).reshape(segment_ids.shape[0], 2, -1)
        segment_rows = jnp.pad(segment_rows, ((0, 0), (0, EXTRA - 3), (0, width - segment_rows.shape[2])))
        messages = jnp.concatenate([start_rows, flag_rows, segment_rows], axis=1)
        rows_one, rows_two = pick(messages)
        grads_one, grads_two = pick(out_grad)

        def line_of(share, far):
            near = swap_mp(jnp.stack([share, far]), 1)
            return jnp.stack([far, near[0], near[1]])

        far_a = swap_mp(share_a, 2)
        far_a, share_f = tie(far_a, share_f)
        line_a = line_of(share_a, far_a)
        far_f = swap_mp(share_f, 2)
        line_a, far_f, rows_one, rows_two = tie(line_a, far_f, rows_one, rows_two)
        near_a = plane_gather(line_a[:, :piece], dp_size)
        rows_one, rows_two = to_rows(rows_one, rows_two, dp_size)
        near_f = swap_mp(jnp.stack([share_f, far_f]), 1)
        line_f = jnp.stack([far_f, near_f[0], near_f[1]], axis=1)
        got = line_a[:, piece : piece + vector_rows.shape[0]].astype(F32).reshape(3, 2, -1)
        vectors = jnp.concatenate([vectors[None], got[:, 0] + got[:, 1]])
        q_width = qv_bias.shape[1]
        q_bias = vectors[:, :q_width].reshape(1, -1)
        v_bias = vectors[:, q_width : 2 * q_width].reshape(1, -1)

        def turn(values, axes):
            for axis, bit in zip(axes, (core, spot // 2, spot % 2)):
                values = jnp.where(bit == 1, jnp.flip(values, axis), values)
            return values

        hidden_bias = turn(vectors[:, 2 * q_width :].reshape(4, 2, 2, 2, piece), (1, 2, 3))
        hidden_bias = hidden_bias.transpose(1, 2, 3, 0, 4).reshape(4, 1, width)

        local_rows = local_attention.reshape(4, 2, piece, width)
        rows_one, rows_two, line_f, near_a, local_rows, local_up, grads_one, grads_two, hidden_bias, q_bias = tie(
            rows_one, rows_two, line_f, near_a, local_rows, local_up, grads_one, grads_two, hidden_bias, q_bias
        )
        other_a = across(near_a, 1)
        xs = across(line_f, 2)
        ys = across(line_f, 4)
        grads_one, grads_two = to_rows(grads_one, grads_two, dp_size)

        quarters = rows_one[strip + 1 : strip + 3, : 2 * strip].astype(jnp.int32).reshape(4, strip)

        def quarter(at):
            return lax.dynamic_index_in_dim(quarters, at, 0, keepdims=False)

        own_segments = jnp.concatenate([quarter(2 * core + parity), quarter(2 * core + 1 - parity)])
        far_segments = jnp.concatenate([quarter(2 - 2 * core + parity), quarter(3 - 2 * core - parity)])
        seg_q = own_segments[None, :]
        seg_k = jnp.concatenate([own_segments, far_segments])[None, :]

        normed_one, queries, own_kv, weights = project(
            place,
            rows_one,
            rows_two,
            row(first_gain),
            row(first_shift),
            local_rows,
            near_a,
            other_a,
            q_bias,
            v_bias,
        )
        flat_weights = weights.reshape(-1, width)
        xs, ys, own_kv, line_f, seg_q, seg_k, grads_one, grads_two = tie(
            xs, ys, own_kv, line_f, seg_q, seg_k, grads_one, grads_two
        )
        grads_in = (grads_one, grads_two)
        far_kv = across(own_kv, 1)
        du = across(xs[0], 4)
        dd = across(ys[1], 2)
        line_far = across(line_f, 1)
        xs_far = across(xs, 1)
        ys_far = across(ys, 1)
        far_kv, line_far, xs_far, ys_far = tie(far_kv, line_far, xs_far, ys_far)
        heads = (queries, own_kv, far_kv)
        context, log_total, mid_rows, normed_two = attend(
            *heads,
            seg_q,
            seg_k,
            flat_weights,
            rows_one,
            rows_two,
            row(out_bias),
            row(second_gain),
            row(second_shift),
        )
        du, dd, normed_two = tie(du, dd, normed_two)
        du_far = across(du, 1)
        dd_far = across(dd, 1)
        local_up = local_up.reshape(8, piece, width)
        local_down = down_weight.reshape(8, piece, width)
        both = (line_f, line_far, xs, xs_far, ys, ys_far, du, du_far, dd, dd_far)
        active, slope, final_rows = expand(
            place, normed_two, mid_rows, hidden_bias, local_up, local_down, both, row(down_bias)
        )

        back_one, back_two = from_rows(final_rows[:strip], final_rows[strip:], dp_size)
        up_other, down_other, normed_grad, bias_other = expand_back(
            1, place, grads_in, normed_two, active, slope, local_up, local_down, both[1::2], None
        )
        up_got = across(up_other, 1)
        down_got = across(down_other, 1)
        up_own, down_own, normed_grad, bias_own = expand_back(
            0, place, grads_in, normed_two, active, slope, local_up, local_down, both[0::2], normed_grad
        )
        up_got, down_got, normed_grad = tie(up_got, down_got, normed_grad)
        up_sent = add(up_own[1], up_got[1])
        down_sent = add(down_own[1], down_got[1])
        up_sent, down_sent, normed_grad = tie(up_sent, down_sent, normed_grad)
        up_sent = across(up_sent, 4)
        down_sent = across(down_sent, 2)
        grad_mid, grad_attn, grad_context, sums_two = settle(
            normed_grad, mid_rows, grads_in, row(second_gain), flat_weights
        )
        inputs = heads + (grad_context, context, log_total, seg_q, seg_k)
        dq, own_grad, far_grad = attend_back(*inputs)
        up_sent, down_sent, far_grad, back_one, back_two = tie(up_sent, down_sent, far_grad, back_one, back_two)
        got_kv = across(far_grad, 1)
        up_second, down_second = onward((up_own, up_got, up_sent), (down_own, down_got, down_sent))
        up_second, down_second, got_kv, grad_mid = tie(up_second, down_second, got_kv, grad_mid)
        up_second = across(up_second, 2)
        down_second = across(down_second, 4)
        attention_other = weigh(1, place, dq, own_grad, got_kv, context, normed_one, grad_attn, None)
        attention_got = across(attention_other, 1)
        attention_other, grad_mid = tie(attention_other, grad_mid)
        out_one, out_two, small = finish(
            place,
            dq,
            own_grad,
            got_kv,
            weights,
            rows_one,
            rows_two,
            row(first_gain),
            grad_mid,
            sums_two,
            bias_own,
            bias_other,
        )
        back_routes = [[(target, source) for source, target in route] for route in row_routes(dp_size)]
        out_one, out_two, attention_got = tie(out_one, out_two, attention_got)
        start_one = lax.ppermute(out_one, BOTH, back_routes[0])
        attention_grad = weigh(0, place, dq, own_grad, got_kv, context, normed_one, grad_attn, attention_got)
        attention_grad, start_one, up_second, down_second, out_two, small = tie(
            attention_grad, start_one, up_second, down_second, out_two, small
        )
        attention_grad = plane_scatter(attention_grad, dp_size)
        pair, pair_sent = merge((up_own, up_got, up_sent, up_second), (down_own, down_got, down_sent, down_second))
        small = small + across(small, 1)
        pair_sent, small = tie(pair_sent, small)
        small_got = swap_mp(small, 1)
        pair_sent = swap_mp(pair_sent, 1)
        pair_sent, small_got, out_two = tie(pair_sent, small_got, out_two)
        start_two = lax.ppermute(out_two, BOTH, back_routes[1])

        bits = [1 << n for n in range(dp_size.bit_length() - 1)]
        small = small + small_got
        pair = add(pair, pair_sent)
        pair_sent = swap_mp(pair[1], 2)
        small = small + swap_mp(small, 2)
        activations = jnp.where(
            parity == 0, jnp.stack([back_one, back_two]), jnp.stack([back_two, back_one])
        )

        def lift(value):
            for bit in bits[3:]:
                value = value + across(value, bit)
            return value

        small = lift(small)
        attention_sent = swap_mp(attention_grad[2:], 1)
        pair, pair_sent, activations, _ = tie(pair, pair_sent, activations, attention_sent)
        if dp_size > 8:
            pair_sent = lift(add(pair[0], pair_sent))
            pair = jnp.zeros_like(pair)
        pair = plane_gather(pack(pair, pair_sent, small), dp_size)
        attention_grad = add(attention_grad[:2], attention_sent)
        attention_sent = swap_mp(attention_grad[1], 2)
        attention_sent, pair, start_two = tie(attention_sent, pair, start_two)
        attention_grad = lift(add(attention_grad[0], attention_sent))
        grad_start = jnp.where(
            parity == 0, jnp.stack([start_one, start_two]), jnp.stack([start_two, start_one])
        )
        tokens_grad = jnp.where((mask_flags == 1)[:, :, None], 0.0, grad_start.astype(F32))
        attention_grad = plane_gather(attention_grad, dp_size)
        up_weight_grad, down_weight_grad, small, up_bias_grad, qv_bias_grad = close_pair(place, pair, across(pair, 1))
        attention_grad, up_weight_grad, down_weight_grad, small = tie(
            attention_grad, up_weight_grad, down_weight_grad, small
        )
        w_qkv_grad, w_out_grad = close_attention(place, attention_grad, across(attention_grad, 1))
        w_qkv_grad = w_qkv_grad.transpose(0, 2, 1)
        up_bias_grad = up_bias_grad.reshape(-1)
        return (
            activations,
            tokens_grad,
            small[0],
            small[1],
            small[2],
            w_qkv_grad,
            qv_bias_grad,
            w_out_grad,
            small[3],
            small[4],
            small[5],
            up_weight_grad,
            up_bias_grad,
            down_weight_grad,
            small[6],
        )

    return body


def solution(mesh):
    in_specs = (
        P("dp", "mp", None),
        P("dp", None),
        P("dp", "mp"),
        P(),
        P(),
        P(),
        P(None, None, "mp"),
        P(None, "mp"),
        P("mp", None),
        P(),
        P(),
        P(),
        P(None, "mp"),
        P("mp"),
        P("mp", None),
        P(),
        P("dp", "mp", None),
    )
    out_specs = (
        P("dp", "mp", None),
        P("dp", "mp", None),
        P(),
        P(),
        P(),
        P(None, None, "mp"),
        P(None, "mp"),
        P("mp", None),
        P(),
        P(),
        P(),
        P(None, "mp"),
        P("mp"),
        P("mp", None),
        P(),
    )
    return jax.shard_map(
        make_body(mesh.shape["dp"]), mesh=mesh, in_specs=in_specs, out_specs=out_specs, check_vma=False
    )
```

```python
import jax
import jax.numpy as jnp
from jax import lax
from jax.experimental import pallas as pl
from jax.experimental.pallas import tpu as pltpu
from jax.sharding import PartitionSpec as P

HD = 64
EPSILON = 1e-06
NEG_FILL = -1e30
BF = jnp.bfloat16
F32 = jnp.float32
BOTH = ("dp", "mp")
BLOCK_ORDER = (0, 2, 1, 3)
NT = (((1,), (1,)), ((), ()))
NN = (((1,), (0,)), ((), ()))
TN = (((0,), (0,)), ((), ()))


def dot(left, right, dims):
    return lax.dot_general(left, right, dims, preferred_element_type=F32)


def swap_dp(value, bit, dp_size):
    return lax.ppermute(value, "dp", [(i, i ^ bit) for i in range(dp_size)])


def swap_mp(value, bit):
    return lax.ppermute(value, "mp", [(i, i ^ bit) for i in range(4)])


def row_routes(dp_size):
    first, second = [], []
    for pair in range(dp_size // 2):
        for core in range(2):
            for place in range(4):
                source = (2 * pair + core) * 4 + place
                for row in range(2):
                    target = (2 * pair + place // 2) * 4 + 2 * core + row
                    (first if row == place % 2 else second).append((source, target))
    return first, second


def to_rows(first, second, dp_size):
    routes = row_routes(dp_size)
    return (lax.ppermute(first, BOTH, routes[0]), lax.ppermute(second, BOTH, routes[1]))


def from_rows(first, second, dp_size):
    back = [[(target, source) for source, target in route] for route in row_routes(dp_size)]
    return (lax.ppermute(first, BOTH, back[0]), lax.ppermute(second, BOTH, back[1]))


EXTRA = 16
SLOTS = 32
MIB_ATTEND = 18
COST = pl.CostEstimate(flops=1000000, transcendentals=0, bytes_accessed=1000)


def plane_groups(dp_size):
    return [[base * 8 + core + 2 * k for k in range(4)] for base in range(dp_size // 8) for core in range(2)]


def plane_gather(value, dp_size):
    spread = jnp.broadcast_to(value[None], (4,) + value.shape)
    return lax.all_to_all(spread, "dp", 0, 0, tiled=True, axis_index_groups=plane_groups(dp_size))


def plane_scatter(value, dp_size):
    pieces = lax.all_to_all(value, "dp", 0, 0, tiled=True, axis_index_groups=plane_groups(dp_size))
    return jnp.sum(pieces.astype(F32), axis=0).astype(BF)


def tie(*values):
    return lax.optimization_barrier(values)


def add(left, right):
    return (left.astype(F32) + right.astype(F32)).astype(BF)


def whole(value):
    rank = value.ndim
    return pl.BlockSpec(value.shape, lambda *i: (0,) * rank, pipeline_mode=pl.Buffered(1))


def scalars():
    return pl.BlockSpec(memory_space=pltpu.SMEM)


def call(kernel, name, mib, grid, in_specs, out_specs, out_shape, scratch, flops, moved, args):
    return pl.pallas_call(
        kernel,
        grid=grid,
        in_specs=in_specs,
        out_specs=out_specs,
        out_shape=out_shape,
        scratch_shapes=scratch,
        compiler_params=pltpu.CompilerParams(vmem_limit_bytes=mib << 20),
        cost_estimate=COST,
        name=name,
    )(*args)


def centre(rows):
    row_mean = jnp.mean(rows, axis=-1, keepdims=True)
    centred = rows - row_mean
    variance = jnp.mean(centred * centred, axis=-1, keepdims=True)
    inv_scale = lax.rsqrt(variance + EPSILON)
    return (centred * inv_scale, inv_scale)


def centre_back(incoming, unit_rows, inv_scale, gain):
    scaled = incoming * gain
    inner_one = jnp.mean(scaled, axis=-1, keepdims=True)
    inner_two = jnp.mean(scaled * unit_rows, axis=-1, keepdims=True)
    return inv_scale * (scaled - inner_one - unit_rows * inner_two)


def project_kernel(place, one, two, gain, shift, local, near, other, q_bias, v_bias, normed, q, kv, weights):
    strip = normed.shape[0] // 2
    for i, rows in enumerate((one, two)):
        unit, _ = centre(rows[:strip].astype(F32))
        normed[i * strip : (i + 1) * strip] = (unit * gain[...] + shift[...]).astype(BF)
    core = place[0]
    weights[:, 0] = local[...]
    for k in range(4):
        weights[2 * core + k // 2, 1:4, k % 2] = near[k]
        weights[2 - 2 * core + k // 2, 1:4, k % 2] = other[k]
    width = one.shape[1]
    rows = normed[...]
    q[...] = (dot(rows, weights[0].reshape(width, width), NT) + q_bias[...]).astype(BF)
    kv[0] = dot(rows, weights[1].reshape(width, width), NT).astype(BF)
    kv[1] = (dot(rows, weights[2].reshape(width, width), NT) + v_bias[...]).astype(BF)


def project(place, one, two, gain, shift, local, near, other, q_bias, v_bias):
    width = one.shape[1]
    tokens = 2 * (one.shape[0] - EXTRA)
    args = (place, one, two, gain, shift, local, near, other, q_bias, v_bias)
    shapes = [
        jax.ShapeDtypeStruct((tokens, width), BF),
        jax.ShapeDtypeStruct((tokens, width), BF),
        jax.ShapeDtypeStruct((2, tokens, width), BF),
        jax.ShapeDtypeStruct((4, 4, 2, width // 8, width), BF),
    ]
    return call(
        project_kernel,
        "project",
        20,
        (1,),
        [scalars()] + [whole(x) for x in args[1:]],
        [whole(x) for x in shapes],
        shapes,
        [],
        6 * tokens * width * width,
        12 * width * width,
        args,
    )


def spare_base(head):
    return 0 if head else HD


def head_lanes(shape, head):
    lanes = lax.broadcasted_iota(jnp.int32, shape, 1)
    return (lanes >= HD) if head else (lanes < HD)


def upright(line):
    return jnp.broadcast_to(line, (128, line.shape[1])).T


def prepare_lanes(segk_ref, segq_ref, key_extra, query_extra):
    for segments, extra, is_key in ((segk_ref, key_extra, True), (segq_ref, query_extra, False)):
        ids = upright(segments[...])
        for head in range(2):
            lanes = lax.broadcasted_iota(jnp.int32, ids.shape, 1) - spare_base(head)
            inside = (lanes >= 0) & (lanes < 4)
            if is_key:
                values = jnp.where(inside & (ids != lanes), NEG_FILL, 0.0)
            else:
                values = jnp.where(inside & (ids == lanes), 1.0, 0.0)
            extra[head] = values.astype(BF)


def attend_kernel(
    q_ref, own_ref, far_ref, segq_ref, segk_ref, weights, one, two, o_bias, gain, shift,
    ctx_ref, lse_ref, mid_ref, normed_ref, keys, values_t, key_extra, query_extra, total,
):
    half = own_ref.shape[1]
    step = pl.program_id(0)

    @pl.when(step == 0)
    def _():
        prepare_lanes(segk_ref, segq_ref, key_extra, query_extra)
        for head in range(2):
            values_t[head, HD:] = jnp.ones_like(values_t[head, HD:])

    for i, ref in enumerate((own_ref, far_ref)):
        span = slice(i * half, (i + 1) * half)
        part = ref[0]
        turned = ref[1].T
        for head in range(2):
            keys[head, span] = jnp.where(head_lanes(part.shape, head), part, key_extra[head, span])
            values_t[head, :HD, span] = turned[head * HD : (head + 1) * HD]
    tokens = q_ref.shape[0]
    block = tokens
    for start in range(0, tokens, block):
        span = slice(start, start + block)
        query = q_ref[span, :] * jnp.asarray(HD**-0.5, BF)
        heads = range(2)
        owns = [jnp.where(head_lanes(query.shape, h), query, query_extra[h, span]) for h in heads]
        scores = [dot(keys[h], owns[h], NT) for h in heads]
        maxima = [jnp.max(v, axis=0, keepdims=True) for v in scores]
        powers = [jnp.exp(v - m).astype(BF) for v, m in zip(scores, maxima)]
        parts = [dot(values_t[h], powers[h], NN) for h in heads]
        pieces = [v[:HD] / v[HD : HD + 1] for v in parts]
        sums = [m + jnp.log(v[HD : HD + 1]) for m, v in zip(maxima, parts)]
        context = jnp.concatenate(pieces, axis=0).T.astype(BF)
        ctx_ref[span, :] = context
        for h in heads:
            lse_ref[0, h : h + 1, span] = sums[h]
        mixed = dot(context, weights[...], NN)

        @pl.when(step == 0)
        def _():
            total[span, :] = mixed

        @pl.when(step > 0)
        def _():
            total[span, :] += mixed

    @pl.when(step == pl.num_programs(0) - 1)
    def _():
        strip = tokens // 2
        for i, rows in enumerate((one, two)):
            span = slice(i * strip, (i + 1) * strip)
            mid = rows[:strip].astype(F32) + total[span, :] + o_bias[...]
            mid_ref[span, :] = mid
            unit, _ = centre(mid)
            normed_ref[span, :] = (unit * gain[...] + shift[...]).astype(BF)


def attend(q, own, far, seg_q, seg_k, weights, one, two, o_bias, gain, shift):
    rows, width = q.shape
    pairs = width // 128
    half = own.shape[1]
    args = (q, own, far, seg_q, seg_k, weights, one, two, o_bias, gain, shift)
    head_block = pl.BlockSpec((rows, 128), lambda i: (0, i))
    key_block = pl.BlockSpec((2, half, 128), lambda i: (0, 0, i))
    shapes = [
        jax.ShapeDtypeStruct((rows, width), BF),
        jax.ShapeDtypeStruct((pairs, 2, rows), F32),
        jax.ShapeDtypeStruct((rows, width), F32),
        jax.ShapeDtypeStruct((rows, width), BF),
    ]
    specs = [head_block, key_block, key_block, whole(seg_q), whole(seg_k)]
    specs.append(pl.BlockSpec((128, width), lambda i: (3 * pairs + i, 0)))
    return call(
        attend_kernel,
        "attend",
        20,
        (pairs,),
        specs + [whole(x) for x in args[6:]],
        [head_block, pl.BlockSpec((1, 2, rows), lambda i: (i, 0, 0)), whole(shapes[2]), whole(shapes[3])],
        shapes,
        [
            pltpu.VMEM((2, 2 * half, 128), BF),
            pltpu.VMEM((2, HD + 16, 2 * half), BF),
            pltpu.VMEM((2, 2 * half, 128), BF),
            pltpu.VMEM((2, rows, 128), BF),
            pltpu.VMEM((rows, width), F32),
        ],
        0,
        0,
        args,
    )


def load_block(place, flip, at_y, mat, local, pieces, block):
    core = place[0] if not flip else 1 - place[0]
    line, along_x, along_y, diagonal = pieces
    for x in range(2):
        spot = place[1 + 2 * at_y + x]
        block[x, 0] = local[core * 4 + spot]
        if at_y and x:
            block[x, 1:4] = diagonal[...]
        else:
            block[x, 1:4] = (along_y if at_y else along_x if x else line)[mat]


def expand_kernel(
    place, normed, mid, bias, local_up, local_down, line, line_far, xs, xs_far, ys, ys_far, du, du_far, dd, dd_far,
    d_bias, active, slope, out, up, down, total,
):
    step = pl.program_id(0)
    for j in range(4):

        @pl.when(step == j)
        def _():
            flip = j // 2
            three = (line_far, xs_far, ys_far) if flip else (line, xs, ys)
            load_block(place, flip, j % 2, 0, local_up, three + ((du_far if flip else du),), up)
            load_block(place, flip, j % 2, 1, local_down, three + ((dd_far if flip else dd),), down)

    width = normed.shape[1]
    hidden = dot(normed[...], up[...].reshape(width, width), NT) + bias[0]
    cdf = 0.5 * (1.0 + lax.erf(hidden * (0.5**0.5)))
    pulled = cdf + hidden * jnp.exp(-0.5 * hidden * hidden) * 0.3989422804014327
    slope[...] = pulled.astype(BF)
    active[...] = (hidden * cdf).astype(BF)
    part = dot(active[...], down[...].reshape(width, width), NN)

    @pl.when(step == 0)
    def _():
        total[...] = mid[...] + d_bias[...] + part

    @pl.when((step > 0) & (step < 3))
    def _():
        total[...] += part

    @pl.when(step == 3)
    def _():
        out[...] = (total[...] + part).astype(BF)


def expand(place, normed, mid, bias, local_up, local_down, pieces, d_bias):
    tokens, width = normed.shape
    piece = width // 8
    args = (place, normed, mid, bias, local_up, local_down, *pieces, d_bias)
    hidden = pl.BlockSpec((tokens, width), lambda j: (0, j))
    shapes = [
        jax.ShapeDtypeStruct((tokens, 4 * width), BF),
        jax.ShapeDtypeStruct((tokens, 4 * width), BF),
        jax.ShapeDtypeStruct((tokens, width), BF),
    ]
    specs = [scalars()] + [whole(x) for x in args[1:]]
    specs[3] = pl.BlockSpec((1, 1, width), lambda j: (j, 0, 0))
    return call(
        expand_kernel,
        "expand",
        28,
        (4,),
        specs,
        [hidden, hidden, whole(shapes[2])],
        shapes,
        [pltpu.VMEM((2, 4, piece, width), BF)] * 2 + [pltpu.VMEM((tokens, width), F32)],
        16 * tokens * width * width,
        20 * width * width,
        args,
    )


def expand_back_kernel(
    flip, place, grad_one, grad_two, normed, active, slope, local_up, local_down, line, xs, ys, du, dd, before,
    up_grad, down_grad, normed_grad, bias_grad, up, down,
):
    step = pl.program_id(0)
    for j in range(2):

        @pl.when(step == j)
        def _():
            load_block(place, flip, j, 0, local_up, (line, xs, ys, du), up)
            load_block(place, flip, j, 1, local_down, (line, xs, ys, dd), down)

    width = normed.shape[1]
    wide = up.shape
    grad = jnp.concatenate([grad_one[...], grad_two[...]], axis=0)
    incoming = dot(grad, down[...].reshape(width, width), NT)
    grad_hidden = (incoming * slope[...].astype(F32)).astype(BF)
    hidden_sum = jnp.sum(grad_hidden.astype(F32), axis=0, keepdims=True)
    piece = wide[2]
    core = place[0] if not flip else 1 - place[0]

    @pl.when(step == 0)
    def _():
        bias_grad[...] = jnp.zeros_like(bias_grad)

    for x in range(2):
        spot = jnp.where(step == 0, place[1 + x], place[3 + x])
        for i, distance in enumerate(BLOCK_ORDER):
            at = (4 * x + i) * piece
            entry = place[5 + distance] * 8 + core * 4 + spot
            bias_grad[pl.ds(entry, 1), :piece] = hidden_sum[:, at : at + piece]
    down_grad[...] = dot(active[...], grad, TN).astype(BF).reshape(2, 1, *wide[1:])
    up_grad[0] = dot(grad_hidden, normed[...], TN).astype(BF).reshape(wide)
    part = dot(grad_hidden, up[...].reshape(width, width), NN)

    @pl.when(step == 0)
    def _():
        if before is None:
            normed_grad[...] = part
        else:
            normed_grad[...] = before[...] + part

    @pl.when(step > 0)
    def _():
        normed_grad[...] += part


def expand_back(flip, place, grad, normed, active, slope, local_up, local_down, pieces, before):
    tokens, width = normed.shape
    piece = width // 8
    args = (place, *grad, normed, active, slope, local_up, local_down, *pieces)
    if before is not None:
        args = args + (before,)

    def kernel(*refs):
        if before is None:
            refs = refs[:13] + (None,) + refs[13:]
        return expand_back_kernel(flip, *refs)

    hidden = pl.BlockSpec((tokens, width), lambda j: (0, j + 2 * flip))
    shapes = [
        jax.ShapeDtypeStruct((2, 2, 4, piece, width), BF),
        jax.ShapeDtypeStruct((2, 2, 4, piece, width), BF),
        jax.ShapeDtypeStruct((tokens, width), F32),
        jax.ShapeDtypeStruct((SLOTS, 128), F32),
    ]
    specs = [scalars()] + [whole(x) for x in args[1:]]
    specs[4] = specs[5] = hidden
    return call(
        kernel,
        "expand_back_other" if flip else "expand_back_own",
        26,
        (2,),
        specs,
        [
            pl.BlockSpec((1, 2, 4, piece, width), lambda j: (j, 0, 0, 0, 0)),
            pl.BlockSpec((2, 1, 4, piece, width), lambda j: (0, j, 0, 0, 0)),
            whole(shapes[2]),
            whole(shapes[3]),
        ],
        shapes,
        [pltpu.VMEM((2, 4, piece, width), BF)] * 2,
        20 * tokens * width * width,
        16 * width * width,
        args,
    )


def settle_kernel(incoming, mid, grad_one, grad_two, gain, wo, grad_mid, grad_attn, grad_context, sums):
    strip = grad_one.shape[0]
    parts = None
    for at in range(0, mid.shape[0], strip):
        span = slice(at, at + strip)
        unit, inv_scale = centre(mid[span, :])
        given = incoming[span, :]
        outer = (grad_two if at else grad_one)[...].astype(F32)
        made = outer + centre_back(given, unit, inv_scale, gain[...])
        grad_mid[span, :] = made
        grad_attn[span, :] = made.astype(BF)
        grad_context[span, :] = dot(made.astype(BF), wo[...], NT).astype(BF)
        rows = [jnp.sum(v, axis=0, keepdims=True) for v in (made, given * unit, given, outer)]
        parts = rows if parts is None else [a + b for a, b in zip(parts, rows)]
    for i, row in enumerate(parts):
        sums[i : i + 1, :] = row


def settle(incoming, mid, grad, gain, weights):
    tokens, width = mid.shape
    args = (incoming, mid, *grad, gain, weights)
    specs = [whole(x) for x in args]
    specs[5] = pl.BlockSpec((width, width), lambda i: (3, 0))
    shapes = [
        jax.ShapeDtypeStruct((tokens, width), F32),
        jax.ShapeDtypeStruct((tokens, width), BF),
        jax.ShapeDtypeStruct((tokens, width), BF),
        jax.ShapeDtypeStruct((8, width), F32),
    ]
    return call(
        settle_kernel,
        "settle",
        13,
        (1,),
        specs,
        [whole(x) for x in shapes],
        shapes,
        [],
        2 * tokens * width * width,
        14 * tokens * width,
        args,
    )


def quarter_block(value, at):
    rank = value.ndim
    shape = (1,) * len(at) + value.shape[len(at) :]
    return pl.BlockSpec(shape, lambda *i: at + (0,) * (rank - len(at)), pipeline_mode=pl.Buffered(1))


def onward_kernel(*refs):
    for i in range(2):
        own, got, sent = (ref[...].astype(F32) for ref in refs[3 * i : 3 * i + 3])
        refs[6 + i][...] = (own[0, 0] + got[0, 0] + sent[0]).astype(BF)


def onward(up, down):
    args = up + down
    shape = jax.ShapeDtypeStruct(up[0].shape[2:], BF)
    return call(
        onward_kernel,
        "onward",
        12,
        (1,),
        [quarter_block(x, (0, 1) if x.ndim == 5 else (1,)) for x in args],
        [whole(shape)] * 2,
        [shape] * 2,
        [],
        0,
        0,
        args,
    )


def merge_kernel(*refs):
    kept, passed = refs[8:]
    for i in range(2):
        own, got, sent, second = refs[4 * i : 4 * i + 4]
        for part, out in ((slice(0, 2), kept), (slice(2, 4), passed)):
            total = own[0, 0, part].astype(F32) + got[0, 0, part].astype(F32)
            total = total + sent[0, part].astype(F32) + second[part].astype(F32)
            out[:, i] = total.astype(BF)


def merge(up, down):
    args = up + down
    shapes = [jax.ShapeDtypeStruct((2, 2) + up[0].shape[3:], BF)] * 2
    specs = [
        quarter_block(x, (0, 0)) if x.ndim == 5 else quarter_block(x, (0,)) if x.ndim == 4 else whole(x) for x in args
    ]
    return call(merge_kernel, "merge", 60, (1,), specs, [whole(x) for x in shapes], shapes, [], 0, 0, args)


def close_pair_kernel(place, near, other, up_grad, down_grad, vectors, up_bias, qv_bias):
    width = near.shape[2]
    piece = width // 8
    for c in range(2):
        for ref, core in ((near, place[0]), (other, 1 - place[0])):

            @pl.when(core == c)
            def _():
                for k in range(4):
                    at = (4 * c + k) * piece
                    down_grad[at : at + piece, :] = ref[k, piece : 2 * piece].astype(F32)
                rows = jnp.concatenate([ref[k, :piece] for k in range(4)], axis=0)
                up_grad[:, 4 * c * piece : 4 * (c + 1) * piece] = rows.astype(F32).T

    total = None
    for k in range(4):
        for at in (2 * piece, 2 * piece + EXTRA):
            part = near[k, at : at + EXTRA].astype(F32)
            total = part if total is None else total + part
    vectors[...] = total[:8]

    def slot(entry):
        r, g = 7 + entry // 6, entry % 6
        return total[r : r + 1, 128 * g : 128 * g + piece]

    for z in range(4):

        @pl.when(place[5] == z)
        def _():
            for k in range(8):
                up_bias[:, k * piece : (k + 1) * piece] = slot(8 * z + k)
            for i in range(2):
                for half in range(2):
                    qv_bias[i : i + 1, half * piece : (half + 1) * piece] = slot(32 + 8 * i + 2 * z + half)


def close_pair(place, near, other):
    width = near.shape[2]
    args = (place, near, other)
    shapes = [
        jax.ShapeDtypeStruct((width, width), F32),
        jax.ShapeDtypeStruct((width, width), F32),
        jax.ShapeDtypeStruct((8, width), F32),
        jax.ShapeDtypeStruct((1, width), F32),
        jax.ShapeDtypeStruct((2, width // 4), F32),
    ]
    return call(
        close_pair_kernel,
        "close_pair",
        12,
        (1,),
        [scalars(), whole(near), whole(other)],
        [whole(x) for x in shapes],
        shapes,
        [],
        0,
        0,
        args,
    )


def close_attention_kernel(place, near, other, qkv_grad, out_grad):
    piece = near.shape[1]
    for c in range(2):
        for ref, core in ((near, place[0]), (other, 1 - place[0])):

            @pl.when(core == c)
            def _():
                for k in range(4):
                    span = slice(k % 2 * piece, (k % 2 + 1) * piece)
                    part = ref[k].astype(F32)
                    if 2 * c + k // 2 < 3:
                        qkv_grad[2 * c + k // 2, span, :] = part
                    else:
                        out_grad[span, :] = part


def close_attention(place, near, other):
    piece, width = near.shape[1:]
    args = (place, near, other)
    shapes = [
        jax.ShapeDtypeStruct((3, 2 * piece, width), F32),
        jax.ShapeDtypeStruct((2 * piece, width), F32),
    ]
    return call(
        close_attention_kernel,
        "close_attention",
        6,
        (1,),
        [scalars(), whole(near), whole(other)],
        [whole(x) for x in shapes],
        shapes,
        [],
        0,
        0,
        args,
    )


def flip_kernel(value, out):
    out[...] = value[...].T


def flip(value):
    shape = jax.ShapeDtypeStruct(value.shape[::-1], value.dtype)
    return call(flip_kernel, "flip", 4, (1,), [whole(value)], whole(shape), shape, [], 0, 0, (value,))


def weigh_kernel(flip, place, dq, mine, got, context, normed, grad, before, out, left, right):
    core = place[0] if not flip else 1 - place[0]
    width = dq.shape[1]
    piece = width // 8

    @pl.when(core == 0)
    def _():
        left[0] = dq[...]
        left[1] = (mine[0].astype(F32) + got[0].astype(F32)).astype(BF)
        right[...] = normed[...]

    @pl.when(core == 1)
    def _():
        left[0] = (mine[1].astype(F32) + got[1].astype(F32)).astype(BF)
        left[1] = context[...]
        right[...] = grad[...]

    for i in range(2):
        rows = normed[...] if i == 0 else right[...]
        made = dot(left[i], rows, TN).reshape(4, 2, piece, width)
        for k in range(2):
            part = made[:, k]
            if before is not None:
                part = part + before[2 * i + k].astype(F32)
            out[2 * i + k] = part.astype(BF)


def weigh(flip, place, dq, mine, got, context, normed, grad, before):
    tokens, width = dq.shape
    args = (place, dq, mine, got, context, normed, grad)
    if before is not None:
        args = args + (before,)

    def kernel(*refs):
        if before is None:
            refs = refs[:7] + (None,) + refs[7:]
        return weigh_kernel(flip, *refs)

    shape = jax.ShapeDtypeStruct((4, 4, width // 8, width), BF)
    return call(
        kernel,
        "weigh_other" if flip else "weigh_own",
        18,
        (1,),
        [scalars()] + [whole(x) for x in args[1:]],
        whole(shape),
        shape,
        [pltpu.VMEM((2, tokens, width), BF), pltpu.VMEM((tokens, width), BF)],
        4 * tokens * width * width,
        8 * width * width,
        args,
    )


def finish_kernel(
    place, dq, mine, got, weights, one, two, gain, grad_mid, sums_two, bias_own, bias_other,
    out_one, out_two, small, total,
):
    width = dq.shape[1]
    keys = (mine[0].astype(F32) + got[0].astype(F32)).astype(BF)
    values = (mine[1].astype(F32) + got[1].astype(F32)).astype(BF)
    total[...] = dot(dq[...], weights[0].reshape(width, width), NN)
    total[...] += dot(keys, weights[1].reshape(width, width), NN)
    total[...] += dot(values, weights[2].reshape(width, width), NN)
    strip = dq.shape[0] // 2
    gathered = None
    for i, rows in enumerate((one, two)):
        span = slice(i * strip, (i + 1) * strip)
        unit, inv_scale = centre(rows[:strip].astype(F32))
        incoming = total[span, :]
        grad_start = grad_mid[span, :] + centre_back(incoming, unit, inv_scale, gain[...])
        high = grad_start.astype(BF)
        (out_two if i else out_one)[...] = high
        low = (grad_start - high.astype(F32)).astype(BF)
        flags = rows[strip : strip + 16, :strip]
        masked = (dot(flags, high, NN) + dot(flags, low, NN))[:1]
        parts = [masked] + [jnp.sum(v, axis=0, keepdims=True) for v in (incoming * unit, incoming)]
        gathered = parts if gathered is None else [a + b for a, b in zip(gathered, parts)]
    small[...] = jnp.zeros_like(small)
    gathered += [sums_two[i : i + 1, :] for i in range(4)]
    for r, line in enumerate(gathered):
        for g in range(width // 128):
            small[16 * g + r : 16 * g + r + 1, :] = line[:, 128 * g : 128 * g + 128]
    hidden = bias_own[...] + bias_other[...]
    for entry in range(32):
        at = 16 * (entry % 6) + 7 + entry // 6
        small[at : at + 1, :] = hidden[entry : entry + 1, :]
    piece = width // 8
    for i, value in enumerate((dq[...], values)):
        line = jnp.sum(value.astype(F32), axis=0, keepdims=True)
        for j, distance in enumerate(BLOCK_ORDER):
            for half in range(2):
                entry = 32 + 8 * i + place[5 + distance] * 2 + half
                at = 16 * lax.rem(entry, 6) + 7 + entry // 6
                span = slice((2 * j + half) * piece, (2 * j + half + 1) * piece)
                small[pl.ds(at, 1), :piece] = line[:, span]


def finish(place, dq, mine, got, weights, one, two, gain, grad_mid, sums_two, bias_own, bias_other):
    tokens, width = dq.shape
    args = (place, dq, mine, got, weights, one, two, gain, grad_mid, sums_two, bias_own, bias_other)
    specs = [scalars()] + [whole(x) for x in args[1:]]
    specs[4] = pl.BlockSpec((3,) + weights.shape[1:], lambda i: (0,) * 5, pipeline_mode=pl.Buffered(1))
    shapes = [
        jax.ShapeDtypeStruct((tokens // 2, width), BF),
        jax.ShapeDtypeStruct((tokens // 2, width), BF),
        jax.ShapeDtypeStruct((96, 128), F32),
    ]
    return call(
        finish_kernel,
        "finish",
        17,
        (1,),
        specs,
        [whole(x) for x in shapes],
        shapes,
        [pltpu.VMEM((tokens, width), F32)],
        0,
        0,
        args,
    )


def pack_kernel(kept, got, small, out):
    piece, width = kept.shape[2:]
    for i in range(2):
        out[i * piece : (i + 1) * piece, :] = (kept[0, i].astype(F32) + got[i].astype(F32)).astype(BF)
    for g in range(width // 128):
        lanes = slice(128 * g, 128 * g + 128)
        value = small[16 * g : 16 * g + 16, :]
        high = value.astype(BF)
        out[2 * piece : 2 * piece + 16, lanes] = high
        out[2 * piece + 16 :, lanes] = (value - high.astype(F32)).astype(BF)


def pack(kept, got, small):
    piece, width = kept.shape[2:]
    args = (kept, got, small)
    shape = jax.ShapeDtypeStruct((2 * piece + 32, width), BF)
    specs = [quarter_block(kept, (0,)), whole(got), whole(small)]
    return call(pack_kernel, "pack", 4, (1,), specs, whole(shape), shape, [], 0, 0, args)


def attend_back_kernel(
    q_ref,
    own_ref,
    far_ref,
    g_ref,
    ctx_ref,
    lse_ref,
    segq_ref,
    segk_ref,
    dq_ref,
    own_grad_ref,
    far_grad_ref,
    keys,
    keys_t,
    values,
    dk_total,
    dv_total,
    key_ids,
):
    half = own_ref.shape[1]

    @pl.when(pl.program_id(0) == 0)
    def _():
        key_ids[...] = upright(segk_ref[...])

    keys[:half] = own_ref[0]
    keys[half:] = far_ref[0]
    keys_t[:, :half] = own_ref[0].T
    keys_t[:, half:] = far_ref[0].T
    values[:half] = own_ref[1]
    values[half:] = far_ref[1]
    total = q_ref.shape[0]
    block = 256
    scale = jnp.asarray(HD**-0.5, BF)
    for start in range(0, total, block):
        span = slice(start, start + block)
        same = key_ids[:, 0:1] == segq_ref[:, span]
        query = q_ref[span, :] * scale
        grad = g_ref[span, :]
        product = (grad.astype(F32) * ctx_ref[span, :].astype(F32)).T
        lanes = lax.broadcasted_iota(jnp.int32, query.shape, 1)
        pieces = []
        for head in range(2):
            own = (lanes >= HD) if head else (lanes < HD)
            query_own = jnp.where(own, query, jnp.zeros_like(query))
            grad_own = jnp.where(own, grad, jnp.zeros_like(grad))
            scores = dot(keys[...], query_own, NT)
            probs = jnp.exp(jnp.where(same, scores, NEG_FILL) - lse_ref[0, head : head + 1, span])
            grad_probs = dot(values[...], grad_own, NT)
            row_dot = jnp.sum(product[head * HD : (head + 1) * HD, :], axis=0, keepdims=True)
            grad_scores = (probs * (grad_probs - row_dot)).astype(BF)
            dv = dot(probs.astype(BF), grad_own, NN)
            dk = dot(grad_scores, query_own, NN)
            if start == 0 and head == 0:
                dv_total[...] = dv
                dk_total[...] = dk
            else:
                dv_total[...] += dv
                dk_total[...] += dk
            pieces.append(dot(keys_t[head * HD : (head + 1) * HD, :], grad_scores, NN))
        dq_ref[span, :] = (jnp.concatenate(pieces, axis=0).T * HD**-0.5).astype(BF)
    own_grad_ref[0] = dk_total[:half].astype(BF)
    far_grad_ref[0] = dk_total[half:].astype(BF)
    own_grad_ref[1] = dv_total[:half].astype(BF)
    far_grad_ref[1] = dv_total[half:].astype(BF)


def attend_back(q, own, far, grad, ctx, lse, seg_q, seg_k):
    rows, width = q.shape
    pairs = width // 128
    half = own.shape[1]
    args = (q, own, far, grad, ctx, lse, seg_q, seg_k)
    head_block = pl.BlockSpec((rows, 128), lambda i: (0, i))
    key_block = pl.BlockSpec((2, half, 128), lambda i: (0, 0, i))
    lse_block = pl.BlockSpec((1, 2, rows), lambda i: (i, 0, 0))
    shapes = [jax.ShapeDtypeStruct((rows, width), BF)] + [jax.ShapeDtypeStruct((2, half, width), BF)] * 2
    return call(
        attend_back_kernel,
        "attend_back",
        13,
        (pairs,),
        [head_block, key_block, key_block, head_block, head_block, lse_block, whole(seg_q), whole(seg_k)],
        [head_block, key_block, key_block],
        shapes,
        [
            pltpu.VMEM((2 * half, 128), BF),
            pltpu.VMEM((128, 2 * half), BF),
            pltpu.VMEM((2 * half, 128), BF),
            pltpu.VMEM((2 * half, 128), F32),
            pltpu.VMEM((2 * half, 128), F32),
            pltpu.VMEM((2 * half, 128), jnp.int32),
        ],
        0,
        0,
        args,
    )


def make_body(dp_size):
    def body(
        tokens,
        segment_ids,
        mask_flags,
        mask_embed,
        first_gain,
        first_shift,
        query_key_value_weight,
        qv_bias,
        output_weight,
        out_bias,
        second_gain,
        second_shift,
        up_weight,
        expand_bias,
        down_weight,
        down_bias,
        out_grad,
    ):
        dp_at = lax.axis_index("dp")
        mp_at = lax.axis_index("mp")
        core = dp_at % 2
        spot = (dp_at // 2) % 4
        parity = mp_at % 2
        width = tokens.shape[2]
        strip = tokens.shape[1]
        piece = width // 8
        place = jnp.stack([core] + [spot ^ r for r in range(4)] + [mp_at ^ d for d in range(4)]).astype(jnp.int32)

        def across(value, bit):
            return swap_dp(value, bit, dp_size)

        def pick(values):
            return (
                lax.dynamic_index_in_dim(values, parity, 0, keepdims=False),
                lax.dynamic_index_in_dim(values, 1 - parity, 0, keepdims=False),
            )

        def row(vector):
            return vector.reshape(1, -1)

        local_attention = jnp.concatenate(
            [query_key_value_weight.transpose(0, 2, 1).reshape(-1, width), output_weight], axis=0
        )
        offset = (core * 4 + spot) * piece
        vectors = jnp.concatenate([qv_bias.reshape(-1), expand_bias])
        vector_high = vectors.astype(BF)
        vector_low = (vectors - vector_high.astype(F32)).astype(BF)
        vector_rows = jnp.concatenate([vector_high, vector_low]).reshape(-1, width)
        share_a = jnp.concatenate(
            [
                lax.dynamic_slice_in_dim(local_attention, offset, piece, 0),
                jnp.pad(vector_rows, ((0, EXTRA - vector_rows.shape[0]), (0, 0))),
            ],
            axis=0,
        )
        local_up = flip(up_weight)
        share_f = jnp.stack(
            [
                lax.dynamic_slice_in_dim(local_up, offset, piece, 0),
                lax.dynamic_slice_in_dim(down_weight, offset, piece, 0),
            ]
        )
        start_rows = jnp.where((mask_flags == 1)[:, :, None], mask_embed.astype(BF), tokens)
        flag_rows = jnp.pad(mask_flags.astype(BF)[:, None, :], ((0, 0), (0, 0), (0, width - strip)))
        segment_rows = segment_ids.astype(BF).reshape(segment_ids.shape[0], 2, -1)
        segment_rows = jnp.pad(segment_rows, ((0, 0), (0, EXTRA - 3), (0, width - segment_rows.shape[2])))
        messages = jnp.concatenate([start_rows, flag_rows, segment_rows], axis=1)
        rows_one, rows_two = pick(messages)
        grads_one, grads_two = pick(out_grad)

        def line_of(share, far):
            near = swap_mp(jnp.stack([share, far]), 1)
            return jnp.stack([far, near[0], near[1]])

        far_a = swap_mp(share_a, 2)
        far_a, share_f = tie(far_a, share_f)
        line_a = line_of(share_a, far_a)
        far_f = swap_mp(share_f, 2)
        line_a, far_f, rows_one, rows_two = tie(line_a, far_f, rows_one, rows_two)
        near_a = plane_gather(line_a[:, :piece], dp_size)
        rows_one, rows_two = to_rows(rows_one, rows_two, dp_size)
        near_f = swap_mp(jnp.stack([share_f, far_f]), 1)
        line_f = jnp.stack([far_f, near_f[0], near_f[1]], axis=1)
        got = line_a[:, piece : piece + vector_rows.shape[0]].astype(F32).reshape(3, 2, -1)
        vectors = jnp.concatenate([vectors[None], got[:, 0] + got[:, 1]])
        q_width = qv_bias.shape[1]
        q_bias = vectors[:, :q_width].reshape(1, -1)
        v_bias = vectors[:, q_width : 2 * q_width].reshape(1, -1)

        def turn(values, axes):
            for axis, bit in zip(axes, (core, spot // 2, spot % 2)):
                values = jnp.where(bit == 1, jnp.flip(values, axis), values)
            return values

        hidden_bias = turn(vectors[:, 2 * q_width :].reshape(4, 2, 2, 2, piece), (1, 2, 3))
        hidden_bias = hidden_bias.transpose(1, 2, 3, 0, 4).reshape(4, 1, width)

        local_rows = local_attention.reshape(4, 2, piece, width)
        rows_one, rows_two, line_f, near_a, local_rows, local_up, grads_one, grads_two, hidden_bias, q_bias = tie(
            rows_one, rows_two, line_f, near_a, local_rows, local_up, grads_one, grads_two, hidden_bias, q_bias
        )
        other_a = across(near_a, 1)
        xs = across(line_f, 2)
        ys = across(line_f, 4)
        grads_one, grads_two = to_rows(grads_one, grads_two, dp_size)

        quarters = rows_one[strip + 1 : strip + 3, : 2 * strip].astype(jnp.int32).reshape(4, strip)

        def quarter(at):
            return lax.dynamic_index_in_dim(quarters, at, 0, keepdims=False)

        own_segments = jnp.concatenate([quarter(2 * core + parity), quarter(2 * core + 1 - parity)])
        far_segments = jnp.concatenate([quarter(2 - 2 * core + parity), quarter(3 - 2 * core - parity)])
        seg_q = own_segments[None, :]
        seg_k = jnp.concatenate([own_segments, far_segments])[None, :]

        normed_one, queries, own_kv, weights = project(
            place,
            rows_one,
            rows_two,
            row(first_gain),
            row(first_shift),
            local_rows,
            near_a,
            other_a,
            q_bias,
            v_bias,
        )
        flat_weights = weights.reshape(-1, width)
        xs, ys, own_kv, line_f, seg_q, seg_k, grads_one, grads_two = tie(
            xs, ys, own_kv, line_f, seg_q, seg_k, grads_one, grads_two
        )
        grads_in = (grads_one, grads_two)
        far_kv = across(own_kv, 1)
        du = across(xs[0], 4)
        dd = across(ys[1], 2)
        line_far = across(line_f, 1)
        xs_far = across(xs, 1)
        ys_far = across(ys, 1)
        far_kv, line_far, xs_far, ys_far = tie(far_kv, line_far, xs_far, ys_far)
        heads = (queries, own_kv, far_kv)
        context, log_total, mid_rows, normed_two = attend(
            *heads,
            seg_q,
            seg_k,
            flat_weights,
            rows_one,
            rows_two,
            row(out_bias),
            row(second_gain),
            row(second_shift),
        )
        du, dd, normed_two = tie(du, dd, normed_two)
        du_far = across(du, 1)
        dd_far = across(dd, 1)
        local_up = local_up.reshape(8, piece, width)
        local_down = down_weight.reshape(8, piece, width)
        both = (line_f, line_far, xs, xs_far, ys, ys_far, du, du_far, dd, dd_far)
        active, slope, final_rows = expand(
            place, normed_two, mid_rows, hidden_bias, local_up, local_down, both, row(down_bias)
        )

        back_one, back_two = from_rows(final_rows[:strip], final_rows[strip:], dp_size)
        up_other, down_other, normed_grad, bias_other = expand_back(
            1, place, grads_in, normed_two, active, slope, local_up, local_down, both[1::2], None
        )
        up_got = across(up_other, 1)
        down_got = across(down_other, 1)
        up_own, down_own, normed_grad, bias_own = expand_back(
            0, place, grads_in, normed_two, active, slope, local_up, local_down, both[0::2], normed_grad
        )
        up_got, down_got, normed_grad = tie(up_got, down_got, normed_grad)
        up_sent = add(up_own[1], up_got[1])
        down_sent = add(down_own[1], down_got[1])
        up_sent, down_sent, normed_grad = tie(up_sent, down_sent, normed_grad)
        up_sent = across(up_sent, 4)
        down_sent = across(down_sent, 2)
        grad_mid, grad_attn, grad_context, sums_two = settle(
            normed_grad, mid_rows, grads_in, row(second_gain), flat_weights
        )
        inputs = heads + (grad_context, context, log_total, seg_q, seg_k)
        dq, own_grad, far_grad = attend_back(*inputs)
        up_sent, down_sent, far_grad, back_one, back_two = tie(up_sent, down_sent, far_grad, back_one, back_two)
        got_kv = across(far_grad, 1)
        up_second, down_second = onward((up_own, up_got, up_sent), (down_own, down_got, down_sent))
        up_second, down_second, got_kv, grad_mid = tie(up_second, down_second, got_kv, grad_mid)
        up_second = across(up_second, 2)
        down_second = across(down_second, 4)
        attention_other = weigh(1, place, dq, own_grad, got_kv, context, normed_one, grad_attn, None)
        attention_got = across(attention_other, 1)
        attention_other, grad_mid = tie(attention_other, grad_mid)
        out_one, out_two, small = finish(
            place,
            dq,
            own_grad,
            got_kv,
            weights,
            rows_one,
            rows_two,
            row(first_gain),
            grad_mid,
            sums_two,
            bias_own,
            bias_other,
        )
        back_routes = [[(target, source) for source, target in route] for route in row_routes(dp_size)]
        out_one, out_two, attention_got = tie(out_one, out_two, attention_got)
        start_one = lax.ppermute(out_one, BOTH, back_routes[0])
        attention_grad = weigh(0, place, dq, own_grad, got_kv, context, normed_one, grad_attn, attention_got)
        attention_grad, start_one, up_second, down_second, out_two, small = tie(
            attention_grad, start_one, up_second, down_second, out_two, small
        )
        attention_grad = plane_scatter(attention_grad, dp_size)
        pair, pair_sent = merge((up_own, up_got, up_sent, up_second), (down_own, down_got, down_sent, down_second))
        small = small + across(small, 1)
        small_got = swap_mp(small, 1)
        pair_sent = swap_mp(pair_sent, 1)
        pair_sent, small_got = tie(pair_sent, small_got)

        bits = [1 << n for n in range(dp_size.bit_length() - 1)]
        small = small + small_got
        pair = add(pair, pair_sent)
        pair_sent = swap_mp(pair[1], 2)
        small_far = swap_mp(small, 2)
        attention_grad, small_far = tie(attention_grad, small_far)
        small = small + small_far
        activations = jnp.where(
            parity == 0, jnp.stack([back_one, back_two]), jnp.stack([back_two, back_one])
        )

        def lift(value):
            for bit in bits[3:]:
                value = value + across(value, bit)
            return value

        small = lift(small)
        attention_sent = swap_mp(attention_grad[2:], 1)
        pair, pair_sent, activations, _ = tie(pair, pair_sent, activations, attention_sent)
        if dp_size > 8:
            pair_sent = lift(add(pair[0], pair_sent))
            pair = jnp.zeros_like(pair)
        pair = plane_gather(pack(pair, pair_sent, small), dp_size)
        attention_sent, out_two = tie(attention_sent, out_two)
        half = strip // 2
        start_two = jnp.concatenate(
            [
                lax.ppermute(out_two[:half], BOTH, back_routes[1]),
                lax.ppermute(out_two[half:], BOTH, back_routes[1]),
            ],
            axis=0,
        )
        attention_grad = add(attention_grad[:2], attention_sent)
        attention_sent = swap_mp(attention_grad[1], 2)
        attention_sent, pair, start_two = tie(attention_sent, pair, start_two)
        grad_start = jnp.where(
            parity == 0, jnp.stack([start_one, start_two]), jnp.stack([start_two, start_one])
        )
        tokens_grad = jnp.where((mask_flags == 1)[:, :, None], 0.0, grad_start.astype(F32))
        attention_grad = lift(add(attention_grad[0], attention_sent))
        attention_grad = plane_gather(attention_grad, dp_size)
        up_weight_grad, down_weight_grad, small, up_bias_grad, qv_bias_grad = close_pair(place, pair, across(pair, 1))
        attention_grad, up_weight_grad, down_weight_grad, small = tie(
            attention_grad, up_weight_grad, down_weight_grad, small
        )
        w_qkv_grad, w_out_grad = close_attention(place, attention_grad, across(attention_grad, 1))
        w_qkv_grad = w_qkv_grad.transpose(0, 2, 1)
        up_bias_grad = up_bias_grad.reshape(-1)
        return (
            activations,
            tokens_grad,
            small[0],
            small[1],
            small[2],
            w_qkv_grad,
            qv_bias_grad,
            w_out_grad,
            small[3],
            small[4],
            small[5],
            up_weight_grad,
            up_bias_grad,
            down_weight_grad,
            small[6],
        )

    return body


def solution(mesh):
    in_specs = (
        P("dp", "mp", None),
        P("dp", None),
        P("dp", "mp"),
        P(),
        P(),
        P(),
        P(None, None, "mp"),
        P(None, "mp"),
        P("mp", None),
        P(),
        P(),
        P(),
        P(None, "mp"),
        P("mp"),
        P("mp", None),
        P(),
        P("dp", "mp", None),
    )
    out_specs = (
        P("dp", "mp", None),
        P("dp", "mp", None),
        P(),
        P(),
        P(),
        P(None, None, "mp"),
        P(None, "mp"),
        P("mp", None),
        P(),
        P(),
        P(),
        P(None, "mp"),
        P("mp"),
        P("mp", None),
        P(),
    )
    return jax.shard_map(
        make_body(mesh.shape["dp"]), mesh=mesh, in_specs=in_specs, out_specs=out_specs, check_vma=False
    )
```

```python
import jax
import jax.numpy as jnp
from jax import lax
from jax.experimental import pallas as pl
from jax.experimental.pallas import tpu as pltpu
from jax.sharding import PartitionSpec as P

HD = 64
EPSILON = 1e-06
NEG_FILL = -1e30
BF = jnp.bfloat16
F32 = jnp.float32
BOTH = ("dp", "mp")
BLOCK_ORDER = (0, 2, 1, 3)
NT = (((1,), (1,)), ((), ()))
NN = (((1,), (0,)), ((), ()))
TN = (((0,), (0,)), ((), ()))


def dot(left, right, dims):
    return lax.dot_general(left, right, dims, preferred_element_type=F32)


def swap_dp(value, bit, dp_size):
    return lax.ppermute(value, "dp", [(i, i ^ bit) for i in range(dp_size)])


def swap_mp(value, bit):
    return lax.ppermute(value, "mp", [(i, i ^ bit) for i in range(4)])


def row_routes(dp_size):
    first, second = [], []
    for pair in range(dp_size // 2):
        for core in range(2):
            for place in range(4):
                source = (2 * pair + core) * 4 + place
                for row in range(2):
                    target = (2 * pair + place // 2) * 4 + 2 * core + row
                    (first if row == place % 2 else second).append((source, target))
    return first, second


def to_rows(first, second, dp_size):
    routes = row_routes(dp_size)
    return (lax.ppermute(first, BOTH, routes[0]), lax.ppermute(second, BOTH, routes[1]))


def from_rows(first, second, dp_size):
    back = [[(target, source) for source, target in route] for route in row_routes(dp_size)]
    return (lax.ppermute(first, BOTH, back[0]), lax.ppermute(second, BOTH, back[1]))


EXTRA = 16
MIB_ATTEND = 18
COST = pl.CostEstimate(flops=1000000, transcendentals=0, bytes_accessed=1000)


def plane_groups(dp_size):
    return [[base * 8 + core + 2 * k for k in range(4)] for base in range(dp_size // 8) for core in range(2)]


def plane_gather(value, dp_size):
    spread = jnp.broadcast_to(value[None], (4,) + value.shape)
    return lax.all_to_all(spread, "dp", 0, 0, tiled=True, axis_index_groups=plane_groups(dp_size))


def plane_scatter(value, dp_size):
    pieces = lax.all_to_all(value, "dp", 0, 0, tiled=True, axis_index_groups=plane_groups(dp_size))
    return jnp.sum(pieces.astype(F32), axis=0).astype(BF)


def tie(*values):
    return lax.optimization_barrier(values)


def add(left, right):
    return (left.astype(F32) + right.astype(F32)).astype(BF)


def whole(value):
    rank = value.ndim
    return pl.BlockSpec(value.shape, lambda *i: (0,) * rank, pipeline_mode=pl.Buffered(1))


def scalars():
    return pl.BlockSpec(memory_space=pltpu.SMEM)


def call(kernel, name, mib, grid, in_specs, out_specs, out_shape, scratch, flops, moved, args):
    return pl.pallas_call(
        kernel,
        grid=grid,
        in_specs=in_specs,
        out_specs=out_specs,
        out_shape=out_shape,
        scratch_shapes=scratch,
        compiler_params=pltpu.CompilerParams(vmem_limit_bytes=mib << 20),
        cost_estimate=COST,
        name=name,
    )(*args)


def centre(rows):
    row_mean = jnp.mean(rows, axis=-1, keepdims=True)
    centred = rows - row_mean
    variance = jnp.mean(centred * centred, axis=-1, keepdims=True)
    inv_scale = lax.rsqrt(variance + EPSILON)
    return (centred * inv_scale, inv_scale)


def centre_back(incoming, unit_rows, inv_scale, gain):
    scaled = incoming * gain
    inner_one = jnp.mean(scaled, axis=-1, keepdims=True)
    inner_two = jnp.mean(scaled * unit_rows, axis=-1, keepdims=True)
    return inv_scale * (scaled - inner_one - unit_rows * inner_two)


def project_kernel(place, one, two, gain, shift, local, near, other, q_bias, v_bias, normed, q, kv, weights):
    strip = normed.shape[0] // 2
    for i, rows in enumerate((one, two)):
        unit, _ = centre(rows[:strip].astype(F32))
        normed[i * strip : (i + 1) * strip] = (unit * gain[...] + shift[...]).astype(BF)
    core = place[0]
    weights[:, 0] = local[...]
    for k in range(4):
        weights[2 * core + k // 2, 1:4, k % 2] = near[k]
        weights[2 - 2 * core + k // 2, 1:4, k % 2] = other[k]
    width = one.shape[1]
    rows = normed[...]
    q[...] = (dot(rows, weights[0].reshape(width, width), NT) + q_bias[...]).astype(BF)
    kv[0] = dot(rows, weights[1].reshape(width, width), NT).astype(BF)
    kv[1] = (dot(rows, weights[2].reshape(width, width), NT) + v_bias[...]).astype(BF)


def project(place, one, two, gain, shift, local, near, other, q_bias, v_bias):
    width = one.shape[1]
    tokens = 2 * (one.shape[0] - EXTRA)
    args = (place, one, two, gain, shift, local, near, other, q_bias, v_bias)
    shapes = [
        jax.ShapeDtypeStruct((tokens, width), BF),
        jax.ShapeDtypeStruct((tokens, width), BF),
        jax.ShapeDtypeStruct((2, tokens, width), BF),
        jax.ShapeDtypeStruct((4, 4, 2, width // 8, width), BF),
    ]
    return call(
        project_kernel,
        "project",
        20,
        (1,),
        [scalars()] + [whole(x) for x in args[1:]],
        [whole(x) for x in shapes],
        shapes,
        [],
        6 * tokens * width * width,
        12 * width * width,
        args,
    )


def spare_base(head):
    return 0 if head else HD


def head_lanes(shape, head):
    lanes = lax.broadcasted_iota(jnp.int32, shape, 1)
    return (lanes >= HD) if head else (lanes < HD)


def upright(line):
    return jnp.broadcast_to(line, (128, line.shape[1])).T


def prepare_lanes(segk_ref, segq_ref, key_extra, query_extra):
    for segments, extra, is_key in ((segk_ref, key_extra, True), (segq_ref, query_extra, False)):
        ids = upright(segments[...])
        for head in range(2):
            lanes = lax.broadcasted_iota(jnp.int32, ids.shape, 1) - spare_base(head)
            inside = (lanes >= 0) & (lanes < 4)
            if is_key:
                values = jnp.where(inside & (ids != lanes), NEG_FILL, 0.0)
            else:
                values = jnp.where(inside & (ids == lanes), 1.0, 0.0)
            extra[head] = values.astype(BF)


def attend_kernel(
    q_ref, own_ref, far_ref, segq_ref, segk_ref, weights, one, two, o_bias, gain, shift,
    ctx_ref, lse_ref, mid_ref, normed_ref, keys, values_t, key_extra, query_extra, total,
):
    half = own_ref.shape[1]
    step = pl.program_id(0)

    @pl.when(step == 0)
    def _():
        prepare_lanes(segk_ref, segq_ref, key_extra, query_extra)
        for head in range(2):
            values_t[head, HD:] = jnp.ones_like(values_t[head, HD:])

    for i, ref in enumerate((own_ref, far_ref)):
        span = slice(i * half, (i + 1) * half)
        part = ref[0]
        turned = ref[1].T
        for head in range(2):
            keys[head, span] = jnp.where(head_lanes(part.shape, head), part, key_extra[head, span])
            values_t[head, :HD, span] = turned[head * HD : (head + 1) * HD]
    tokens = q_ref.shape[0]
    block = tokens
    for start in range(0, tokens, block):
        span = slice(start, start + block)
        query = q_ref[span, :] * jnp.asarray(HD**-0.5, BF)
        heads = range(2)
        owns = [jnp.where(head_lanes(query.shape, h), query, query_extra[h, span]) for h in heads]
        scores = [dot(keys[h], owns[h], NT) for h in heads]
        maxima = [jnp.max(v, axis=0, keepdims=True) for v in scores]
        powers = [jnp.exp(v - m).astype(BF) for v, m in zip(scores, maxima)]
        parts = [dot(values_t[h], powers[h], NN) for h in heads]
        pieces = [v[:HD] / v[HD : HD + 1] for v in parts]
        sums = [m + jnp.log(v[HD : HD + 1]) for m, v in zip(maxima, parts)]
        context = jnp.concatenate(pieces, axis=0).T.astype(BF)
        ctx_ref[span, :] = context
        for h in heads:
            lse_ref[0, h : h + 1, span] = sums[h]
        mixed = dot(context, weights[...], NN)

        @pl.when(step == 0)
        def _():
            total[span, :] = mixed

        @pl.when(step > 0)
        def _():
            total[span, :] += mixed

    @pl.when(step == pl.num_programs(0) - 1)
    def _():
        strip = tokens // 2
        for i, rows in enumerate((one, two)):
            span = slice(i * strip, (i + 1) * strip)
            mid = rows[:strip].astype(F32) + total[span, :] + o_bias[...]
            mid_ref[span, :] = mid
            unit, _ = centre(mid)
            normed_ref[span, :] = (unit * gain[...] + shift[...]).astype(BF)


def attend(q, own, far, seg_q, seg_k, weights, one, two, o_bias, gain, shift):
    rows, width = q.shape
    pairs = width // 128
    half = own.shape[1]
    args = (q, own, far, seg_q, seg_k, weights, one, two, o_bias, gain, shift)
    head_block = pl.BlockSpec((rows, 128), lambda i: (0, i))
    key_block = pl.BlockSpec((2, half, 128), lambda i: (0, 0, i))
    shapes = [
        jax.ShapeDtypeStruct((rows, width), BF),
        jax.ShapeDtypeStruct((pairs, 2, rows), F32),
        jax.ShapeDtypeStruct((rows, width), F32),
        jax.ShapeDtypeStruct((rows, width), BF),
    ]
    specs = [head_block, key_block, key_block, whole(seg_q), whole(seg_k)]
    specs.append(pl.BlockSpec((128, width), lambda i: (3 * pairs + i, 0)))
    return call(
        attend_kernel,
        "attend",
        20,
        (pairs,),
        specs + [whole(x) for x in args[6:]],
        [head_block, pl.BlockSpec((1, 2, rows), lambda i: (i, 0, 0)), whole(shapes[2]), whole(shapes[3])],
        shapes,
        [
            pltpu.VMEM((2, 2 * half, 128), BF),
            pltpu.VMEM((2, HD + 16, 2 * half), BF),
            pltpu.VMEM((2, 2 * half, 128), BF),
            pltpu.VMEM((2, rows, 128), BF),
            pltpu.VMEM((rows, width), F32),
        ],
        0,
        0,
        args,
    )


def load_block(place, flip, at_y, mat, local, pieces, block):
    core = place[0] if not flip else 1 - place[0]
    line, along_x, along_y, diagonal = pieces
    for x in range(2):
        spot = place[1 + 2 * at_y + x]
        block[x, 0] = local[core * 4 + spot]
        if at_y and x:
            block[x, 1:4] = diagonal[...]
        else:
            block[x, 1:4] = (along_y if at_y else along_x if x else line)[mat]


def expand_kernel(
    place, normed, mid, bias, local_up, local_down, line, line_far, xs, xs_far, ys, ys_far, du, du_far, dd, dd_far,
    d_bias, active, slope, out, up, down, total,
):
    step = pl.program_id(0)
    for j in range(4):

        @pl.when(step == j)
        def _():
            flip = j // 2
            three = (line_far, xs_far, ys_far) if flip else (line, xs, ys)
            load_block(place, flip, j % 2, 0, local_up, three + ((du_far if flip else du),), up)
            load_block(place, flip, j % 2, 1, local_down, three + ((dd_far if flip else dd),), down)

    width = normed.shape[1]
    hidden = dot(normed[...], up[...].reshape(width, width), NT) + bias[0]
    cdf = 0.5 * (1.0 + lax.erf(hidden * (0.5**0.5)))
    pulled = cdf + hidden * jnp.exp(-0.5 * hidden * hidden) * 0.3989422804014327
    slope[...] = pulled.astype(BF)
    active[...] = (hidden * cdf).astype(BF)
    part = dot(active[...], down[...].reshape(width, width), NN)

    @pl.when(step == 0)
    def _():
        total[...] = mid[...] + d_bias[...] + part

    @pl.when((step > 0) & (step < 3))
    def _():
        total[...] += part

    @pl.when(step == 3)
    def _():
        out[...] = (total[...] + part).astype(BF)


def expand(place, normed, mid, bias, local_up, local_down, pieces, d_bias):
    tokens, width = normed.shape
    piece = width // 8
    args = (place, normed, mid, bias, local_up, local_down, *pieces, d_bias)
    hidden = pl.BlockSpec((tokens, width), lambda j: (0, j))
    shapes = [
        jax.ShapeDtypeStruct((tokens, 4 * width), BF),
        jax.ShapeDtypeStruct((tokens, 4 * width), BF),
        jax.ShapeDtypeStruct((tokens, width), BF),
    ]
    specs = [scalars()] + [whole(x) for x in args[1:]]
    specs[3] = pl.BlockSpec((1, 1, width), lambda j: (j, 0, 0))
    return call(
        expand_kernel,
        "expand",
        28,
        (4,),
        specs,
        [hidden, hidden, whole(shapes[2])],
        shapes,
        [pltpu.VMEM((2, 4, piece, width), BF)] * 2 + [pltpu.VMEM((tokens, width), F32)],
        16 * tokens * width * width,
        20 * width * width,
        args,
    )


def expand_back_kernel(
    flip, place, grad_one, grad_two, normed, active, slope, local_up, local_down, line, xs, ys, du, dd, before,
    up_grad, down_grad, normed_grad, bias_grad, up, down,
):
    step = pl.program_id(0)
    for j in range(2):

        @pl.when(step == j)
        def _():
            load_block(place, flip, j, 0, local_up, (line, xs, ys, du), up)
            load_block(place, flip, j, 1, local_down, (line, xs, ys, dd), down)

    width = normed.shape[1]
    wide = up.shape
    grad = jnp.concatenate([grad_one[...], grad_two[...]], axis=0)
    incoming = dot(grad, down[...].reshape(width, width), NT)
    grad_hidden = (incoming * slope[...].astype(F32)).astype(BF)
    bias_grad[0] = jnp.sum(grad_hidden.astype(F32), axis=0, keepdims=True)
    down_grad[...] = dot(active[...], grad, TN).astype(BF).reshape(2, 1, *wide[1:])
    up_grad[0] = dot(grad_hidden, normed[...], TN).astype(BF).reshape(wide)
    part = dot(grad_hidden, up[...].reshape(width, width), NN)

    @pl.when(step == 0)
    def _():
        if before is None:
            normed_grad[...] = part
        else:
            normed_grad[...] = before[...] + part

    @pl.when(step > 0)
    def _():
        normed_grad[...] += part


def expand_back(flip, place, grad, normed, active, slope, local_up, local_down, pieces, before):
    tokens, width = normed.shape
    piece = width // 8
    args = (place, *grad, normed, active, slope, local_up, local_down, *pieces)
    if before is not None:
        args = args + (before,)

    def kernel(*refs):
        if before is None:
            refs = refs[:13] + (None,) + refs[13:]
        return expand_back_kernel(flip, *refs)

    hidden = pl.BlockSpec((tokens, width), lambda j: (0, j + 2 * flip))
    shapes = [
        jax.ShapeDtypeStruct((2, 2, 4, piece, width), BF),
        jax.ShapeDtypeStruct((2, 2, 4, piece, width), BF),
        jax.ShapeDtypeStruct((tokens, width), F32),
        jax.ShapeDtypeStruct((2, 1, width), F32),
    ]
    specs = [scalars()] + [whole(x) for x in args[1:]]
    specs[4] = specs[5] = hidden
    return call(
        kernel,
        "expand_back_other" if flip else "expand_back_own",
        22,
        (2,),
        specs,
        [
            pl.BlockSpec((1, 2, 4, piece, width), lambda j: (j, 0, 0, 0, 0)),
            pl.BlockSpec((2, 1, 4, piece, width), lambda j: (0, j, 0, 0, 0)),
            whole(shapes[2]),
            pl.BlockSpec((1, 1, width), lambda j: (j, 0, 0)),
        ],
        shapes,
        [pltpu.VMEM((2, 4, piece, width), BF)] * 2,
        20 * tokens * width * width,
        16 * width * width,
        args,
    )


def settle_kernel(incoming, mid, grad_one, grad_two, gain, wo, grad_mid, grad_attn, grad_context, sums):
    strip = grad_one.shape[0]
    parts = None
    for at in range(0, mid.shape[0], strip):
        span = slice(at, at + strip)
        unit, inv_scale = centre(mid[span, :])
        given = incoming[span, :]
        outer = (grad_two if at else grad_one)[...].astype(F32)
        made = outer + centre_back(given, unit, inv_scale, gain[...])
        grad_mid[span, :] = made
        grad_attn[span, :] = made.astype(BF)
        grad_context[span, :] = dot(made.astype(BF), wo[...], NT).astype(BF)
        rows = [jnp.sum(v, axis=0, keepdims=True) for v in (made, given * unit, given, outer)]
        parts = rows if parts is None else [a + b for a, b in zip(parts, rows)]
    for i, row in enumerate(parts):
        sums[i : i + 1, :] = row


def settle(incoming, mid, grad, gain, weights):
    tokens, width = mid.shape
    args = (incoming, mid, *grad, gain, weights)
    specs = [whole(x) for x in args]
    specs[5] = pl.BlockSpec((width, width), lambda i: (3, 0))
    shapes = [
        jax.ShapeDtypeStruct((tokens, width), F32),
        jax.ShapeDtypeStruct((tokens, width), BF),
        jax.ShapeDtypeStruct((tokens, width), BF),
        jax.ShapeDtypeStruct((8, width), F32),
    ]
    return call(
        settle_kernel,
        "settle",
        13,
        (1,),
        specs,
        [whole(x) for x in shapes],
        shapes,
        [],
        2 * tokens * width * width,
        14 * tokens * width,
        args,
    )


def quarter_block(value, at):
    rank = value.ndim
    shape = (1,) * len(at) + value.shape[len(at) :]
    return pl.BlockSpec(shape, lambda *i: at + (0,) * (rank - len(at)), pipeline_mode=pl.Buffered(1))


def onward_kernel(*refs):
    for i in range(2):
        own, got, sent = (ref[...].astype(F32) for ref in refs[3 * i : 3 * i + 3])
        refs[6 + i][...] = (own[0, 0] + got[0, 0] + sent[0]).astype(BF)


def onward(up, down):
    args = up + down
    shape = jax.ShapeDtypeStruct(up[0].shape[2:], BF)
    return call(
        onward_kernel,
        "onward",
        12,
        (1,),
        [quarter_block(x, (0, 1) if x.ndim == 5 else (1,)) for x in args],
        [whole(shape)] * 2,
        [shape] * 2,
        [],
        0,
        0,
        args,
    )


def merge_kernel(*refs):
    kept, passed = refs[8:]
    for i in range(2):
        own, got, sent, second = refs[4 * i : 4 * i + 4]
        for part, out in ((slice(0, 2), kept), (slice(2, 4), passed)):
            total = own[0, 0, part].astype(F32) + got[0, 0, part].astype(F32)
            total = total + sent[0, part].astype(F32) + second[part].astype(F32)
            out[:, i] = total.astype(BF)


def merge(up, down):
    args = up + down
    shapes = [jax.ShapeDtypeStruct((2, 2) + up[0].shape[3:], BF)] * 2
    specs = [
        quarter_block(x, (0, 0)) if x.ndim == 5 else quarter_block(x, (0,)) if x.ndim == 4 else whole(x) for x in args
    ]
    return call(merge_kernel, "merge", 60, (1,), specs, [whole(x) for x in shapes], shapes, [], 0, 0, args)


def close_pair_kernel(place, near, other, up_grad, down_grad, vectors, up_bias, qv_bias):
    width = near.shape[2]
    piece = width // 8
    for c in range(2):
        for ref, core in ((near, place[0]), (other, 1 - place[0])):

            @pl.when(core == c)
            def _():
                for k in range(4):
                    at = (4 * c + k) * piece
                    down_grad[at : at + piece, :] = ref[k, piece : 2 * piece].astype(F32)
                rows = jnp.concatenate([ref[k, :piece] for k in range(4)], axis=0)
                up_grad[:, 4 * c * piece : 4 * (c + 1) * piece] = rows.astype(F32).T

    total = None
    for k in range(4):
        for at in (2 * piece, 2 * piece + EXTRA):
            part = near[k, at : at + EXTRA].astype(F32)
            total = part if total is None else total + part
    vectors[...] = total[:8]

    def slot(entry):
        r, g = 7 + entry // 6, entry % 6
        return total[r : r + 1, 128 * g : 128 * g + piece]

    for z in range(4):

        @pl.when(place[5] == z)
        def _():
            for k in range(8):
                up_bias[:, k * piece : (k + 1) * piece] = slot(8 * z + k)
            for i in range(2):
                for half in range(2):
                    qv_bias[i : i + 1, half * piece : (half + 1) * piece] = slot(32 + 8 * i + 2 * z + half)


def close_pair(place, near, other):
    width = near.shape[2]
    args = (place, near, other)
    shapes = [
        jax.ShapeDtypeStruct((width, width), F32),
        jax.ShapeDtypeStruct((width, width), F32),
        jax.ShapeDtypeStruct((8, width), F32),
        jax.ShapeDtypeStruct((1, width), F32),
        jax.ShapeDtypeStruct((2, width // 4), F32),
    ]
    return call(
        close_pair_kernel,
        "close_pair",
        12,
        (1,),
        [scalars(), whole(near), whole(other)],
        [whole(x) for x in shapes],
        shapes,
        [],
        0,
        0,
        args,
    )


def close_attention_kernel(place, near, other, qkv_grad, out_grad):
    piece = near.shape[1]
    for c in range(2):
        for ref, core in ((near, place[0]), (other, 1 - place[0])):

            @pl.when(core == c)
            def _():
                for k in range(4):
                    span = slice(k % 2 * piece, (k % 2 + 1) * piece)
                    part = ref[k].astype(F32)
                    if 2 * c + k // 2 < 3:
                        qkv_grad[2 * c + k // 2, span, :] = part
                    else:
                        out_grad[span, :] = part


def close_attention(place, near, other):
    piece, width = near.shape[1:]
    args = (place, near, other)
    shapes = [
        jax.ShapeDtypeStruct((3, 2 * piece, width), F32),
        jax.ShapeDtypeStruct((2 * piece, width), F32),
    ]
    return call(
        close_attention_kernel,
        "close_attention",
        6,
        (1,),
        [scalars(), whole(near), whole(other)],
        [whole(x) for x in shapes],
        shapes,
        [],
        0,
        0,
        args,
    )


def flip_kernel(value, out):
    out[...] = value[...].T


def flip(value):
    shape = jax.ShapeDtypeStruct(value.shape[::-1], value.dtype)
    return call(flip_kernel, "flip", 4, (1,), [whole(value)], whole(shape), shape, [], 0, 0, (value,))


def weigh_kernel(flip, place, dq, mine, got, context, normed, grad, before, out, left, right):
    core = place[0] if not flip else 1 - place[0]
    width = dq.shape[1]
    piece = width // 8

    @pl.when(core == 0)
    def _():
        left[0] = dq[...]
        left[1] = (mine[0].astype(F32) + got[0].astype(F32)).astype(BF)
        right[...] = normed[...]

    @pl.when(core == 1)
    def _():
        left[0] = (mine[1].astype(F32) + got[1].astype(F32)).astype(BF)
        left[1] = context[...]
        right[...] = grad[...]

    for i in range(2):
        rows = normed[...] if i == 0 else right[...]
        made = dot(left[i], rows, TN).reshape(4, 2, piece, width)
        for k in range(2):
            part = made[:, k]
            if before is not None:
                part = part + before[2 * i + k].astype(F32)
            out[2 * i + k] = part.astype(BF)


def weigh(flip, place, dq, mine, got, context, normed, grad, before):
    tokens, width = dq.shape
    args = (place, dq, mine, got, context, normed, grad)
    if before is not None:
        args = args + (before,)

    def kernel(*refs):
        if before is None:
            refs = refs[:7] + (None,) + refs[7:]
        return weigh_kernel(flip, *refs)

    shape = jax.ShapeDtypeStruct((4, 4, width // 8, width), BF)
    return call(
        kernel,
        "weigh_other" if flip else "weigh_own",
        14,
        (1,),
        [scalars()] + [whole(x) for x in args[1:]],
        whole(shape),
        shape,
        [pltpu.VMEM((2, tokens, width), BF), pltpu.VMEM((tokens, width), BF)],
        4 * tokens * width * width,
        8 * width * width,
        args,
    )


def finish_kernel(
    place, dq, mine, got, weights, one, two, gain, grad_mid, sums_two,
    out_one, out_two, small, total,
):
    width = dq.shape[1]
    keys = (mine[0].astype(F32) + got[0].astype(F32)).astype(BF)
    values = (mine[1].astype(F32) + got[1].astype(F32)).astype(BF)
    total[...] = dot(dq[...], weights[0].reshape(width, width), NN)
    total[...] += dot(keys, weights[1].reshape(width, width), NN)
    total[...] += dot(values, weights[2].reshape(width, width), NN)
    strip = dq.shape[0] // 2
    gathered = None
    for i, rows in enumerate((one, two)):
        span = slice(i * strip, (i + 1) * strip)
        unit, inv_scale = centre(rows[:strip].astype(F32))
        incoming = total[span, :]
        grad_start = grad_mid[span, :] + centre_back(incoming, unit, inv_scale, gain[...])
        high = grad_start.astype(BF)
        (out_two if i else out_one)[...] = high
        low = (grad_start - high.astype(F32)).astype(BF)
        flags = rows[strip : strip + 16, :strip]
        masked = (dot(flags, high, NN) + dot(flags, low, NN))[:1]
        parts = [masked] + [jnp.sum(v, axis=0, keepdims=True) for v in (incoming * unit, incoming)]
        gathered = parts if gathered is None else [a + b for a, b in zip(gathered, parts)]
    small[...] = jnp.zeros_like(small)
    gathered += [sums_two[i : i + 1, :] for i in range(4)]
    for r, line in enumerate(gathered):
        for g in range(width // 128):
            small[16 * g + r : 16 * g + r + 1, :] = line[:, 128 * g : 128 * g + 128]
    piece = width // 8
    for i, value in enumerate((dq[...], values)):
        line = jnp.sum(value.astype(F32), axis=0, keepdims=True)
        for j, distance in enumerate(BLOCK_ORDER):
            for half in range(2):
                entry = 32 + 8 * i + place[5 + distance] * 2 + half
                at = 16 * lax.rem(entry, 6) + 7 + entry // 6
                span = slice((2 * j + half) * piece, (2 * j + half + 1) * piece)
                small[pl.ds(at, 1), :piece] = line[:, span]


def finish(place, dq, mine, got, weights, one, two, gain, grad_mid, sums_two):
    tokens, width = dq.shape
    args = (place, dq, mine, got, weights, one, two, gain, grad_mid, sums_two)
    specs = [scalars()] + [whole(x) for x in args[1:]]
    specs[4] = pl.BlockSpec((3,) + weights.shape[1:], lambda i: (0,) * 5, pipeline_mode=pl.Buffered(1))
    shapes = [
        jax.ShapeDtypeStruct((tokens // 2, width), BF),
        jax.ShapeDtypeStruct((tokens // 2, width), BF),
        jax.ShapeDtypeStruct((96, 128), F32),
    ]
    return call(
        finish_kernel,
        "finish",
        15,
        (1,),
        specs,
        [whole(x) for x in shapes],
        shapes,
        [pltpu.VMEM((tokens, width), F32)],
        0,
        0,
        args,
    )


def tally_kernel(place, table, own, other, out):
    out[...] = table[...]
    width = own.shape[2]
    piece = width // 8
    for flip, sums in enumerate((own, other)):
        core = place[0] if not flip else 1 - place[0]
        for y in range(2):
            line = sums[y]
            for x in range(2):
                spot = place[1 + 2 * y + x]
                for i, distance in enumerate(BLOCK_ORDER):
                    entry = place[5 + distance] * 8 + core * 4 + spot
                    at = 16 * lax.rem(entry, 6) + 7 + entry // 6
                    span = slice((4 * x + i) * piece, (4 * x + i + 1) * piece)
                    out[pl.ds(at, 1), :piece] = line[:, span]


def tally(place, table, own, other):
    args = (place, table, own, other)
    shape = jax.ShapeDtypeStruct(table.shape, F32)
    specs = [scalars()] + [whole(x) for x in args[1:]]
    return call(tally_kernel, "tally", 4, (1,), specs, whole(shape), shape, [], 0, 0, args)


def pack_kernel(kept, got, small, out):
    piece, width = kept.shape[2:]
    for i in range(2):
        out[i * piece : (i + 1) * piece, :] = (kept[0, i].astype(F32) + got[i].astype(F32)).astype(BF)
    for g in range(width // 128):
        lanes = slice(128 * g, 128 * g + 128)
        value = small[16 * g : 16 * g + 16, :]
        high = value.astype(BF)
        out[2 * piece : 2 * piece + 16, lanes] = high
        out[2 * piece + 16 :, lanes] = (value - high.astype(F32)).astype(BF)


def pack(kept, got, small):
    piece, width = kept.shape[2:]
    args = (kept, got, small)
    shape = jax.ShapeDtypeStruct((2 * piece + 32, width), BF)
    specs = [quarter_block(kept, (0,)), whole(got), whole(small)]
    return call(pack_kernel, "pack", 4, (1,), specs, whole(shape), shape, [], 0, 0, args)


def attend_back_kernel(
    q_ref,
    own_ref,
    far_ref,
    g_ref,
    ctx_ref,
    lse_ref,
    segq_ref,
    segk_ref,
    dq_ref,
    own_grad_ref,
    far_grad_ref,
    keys,
    keys_t,
    values,
    dk_total,
    dv_total,
    key_ids,
):
    half = own_ref.shape[1]

    @pl.when(pl.program_id(0) == 0)
    def _():
        key_ids[...] = upright(segk_ref[...])

    keys[:half] = own_ref[0]
    keys[half:] = far_ref[0]
    keys_t[:, :half] = own_ref[0].T
    keys_t[:, half:] = far_ref[0].T
    values[:half] = own_ref[1]
    values[half:] = far_ref[1]
    total = q_ref.shape[0]
    block = 256
    scale = jnp.asarray(HD**-0.5, BF)
    for start in range(0, total, block):
        span = slice(start, start + block)
        same = key_ids[:, 0:1] == segq_ref[:, span]
        query = q_ref[span, :] * scale
        grad = g_ref[span, :]
        product = (grad.astype(F32) * ctx_ref[span, :].astype(F32)).T
        lanes = lax.broadcasted_iota(jnp.int32, query.shape, 1)
        pieces = []
        for head in range(2):
            own = (lanes >= HD) if head else (lanes < HD)
            query_own = jnp.where(own, query, jnp.zeros_like(query))
            grad_own = jnp.where(own, grad, jnp.zeros_like(grad))
            scores = dot(keys[...], query_own, NT)
            probs = jnp.exp(jnp.where(same, scores, NEG_FILL) - lse_ref[0, head : head + 1, span])
            grad_probs = dot(values[...], grad_own, NT)
            row_dot = jnp.sum(product[head * HD : (head + 1) * HD, :], axis=0, keepdims=True)
            grad_scores = (probs * (grad_probs - row_dot)).astype(BF)
            dv = dot(probs.astype(BF), grad_own, NN)
            dk = dot(grad_scores, query_own, NN)
            if start == 0 and head == 0:
                dv_total[...] = dv
                dk_total[...] = dk
            else:
                dv_total[...] += dv
                dk_total[...] += dk
            pieces.append(dot(keys_t[head * HD : (head + 1) * HD, :], grad_scores, NN))
        dq_ref[span, :] = (jnp.concatenate(pieces, axis=0).T * HD**-0.5).astype(BF)
    own_grad_ref[0] = dk_total[:half].astype(BF)
    far_grad_ref[0] = dk_total[half:].astype(BF)
    own_grad_ref[1] = dv_total[:half].astype(BF)
    far_grad_ref[1] = dv_total[half:].astype(BF)


def attend_back(q, own, far, grad, ctx, lse, seg_q, seg_k):
    rows, width = q.shape
    pairs = width // 128
    half = own.shape[1]
    args = (q, own, far, grad, ctx, lse, seg_q, seg_k)
    head_block = pl.BlockSpec((rows, 128), lambda i: (0, i))
    key_block = pl.BlockSpec((2, half, 128), lambda i: (0, 0, i))
    lse_block = pl.BlockSpec((1, 2, rows), lambda i: (i, 0, 0))
    shapes = [jax.ShapeDtypeStruct((rows, width), BF)] + [jax.ShapeDtypeStruct((2, half, width), BF)] * 2
    return call(
        attend_back_kernel,
        "attend_back",
        13,
        (pairs,),
        [head_block, key_block, key_block, head_block, head_block, lse_block, whole(seg_q), whole(seg_k)],
        [head_block, key_block, key_block],
        shapes,
        [
            pltpu.VMEM((2 * half, 128), BF),
            pltpu.VMEM((128, 2 * half), BF),
            pltpu.VMEM((2 * half, 128), BF),
            pltpu.VMEM((2 * half, 128), F32),
            pltpu.VMEM((2 * half, 128), F32),
            pltpu.VMEM((2 * half, 128), jnp.int32),
        ],
        0,
        0,
        args,
    )


def make_body(dp_size):
    def body(
        tokens,
        segment_ids,
        mask_flags,
        mask_embed,
        first_gain,
        first_shift,
        query_key_value_weight,
        qv_bias,
        output_weight,
        out_bias,
        second_gain,
        second_shift,
        up_weight,
        expand_bias,
        down_weight,
        down_bias,
        out_grad,
    ):
        dp_at = lax.axis_index("dp")
        mp_at = lax.axis_index("mp")
        core = dp_at % 2
        spot = (dp_at // 2) % 4
        parity = mp_at % 2
        width = tokens.shape[2]
        strip = tokens.shape[1]
        piece = width // 8
        place = jnp.stack([core] + [spot ^ r for r in range(4)] + [mp_at ^ d for d in range(4)]).astype(jnp.int32)

        def across(value, bit):
            return swap_dp(value, bit, dp_size)

        def pick(values):
            return (
                lax.dynamic_index_in_dim(values, parity, 0, keepdims=False),
                lax.dynamic_index_in_dim(values, 1 - parity, 0, keepdims=False),
            )

        def row(vector):
            return vector.reshape(1, -1)

        local_attention = jnp.concatenate(
            [query_key_value_weight.transpose(0, 2, 1).reshape(-1, width), output_weight], axis=0
        )
        offset = (core * 4 + spot) * piece
        vectors = jnp.concatenate([qv_bias.reshape(-1), expand_bias])
        vector_high = vectors.astype(BF)
        vector_low = (vectors - vector_high.astype(F32)).astype(BF)
        vector_rows = jnp.concatenate([vector_high, vector_low]).reshape(-1, width)
        share_a = jnp.concatenate(
            [
                lax.dynamic_slice_in_dim(local_attention, offset, piece, 0),
                jnp.pad(vector_rows, ((0, EXTRA - vector_rows.shape[0]), (0, 0))),
            ],
            axis=0,
        )
        local_up = flip(up_weight)
        share_f = jnp.stack(
            [
                lax.dynamic_slice_in_dim(local_up, offset, piece, 0),
                lax.dynamic_slice_in_dim(down_weight, offset, piece, 0),
            ]
        )
        start_rows = jnp.where((mask_flags == 1)[:, :, None], mask_embed.astype(BF), tokens)
        flag_rows = jnp.pad(mask_flags.astype(BF)[:, None, :], ((0, 0), (0, 0), (0, width - strip)))
        segment_rows = segment_ids.astype(BF).reshape(segment_ids.shape[0], 2, -1)
        segment_rows = jnp.pad(segment_rows, ((0, 0), (0, EXTRA - 3), (0, width - segment_rows.shape[2])))
        messages = jnp.concatenate([start_rows, flag_rows, segment_rows], axis=1)
        rows_one, rows_two = pick(messages)
        grads_one, grads_two = pick(out_grad)

        def line_of(share, far):
            near = swap_mp(jnp.stack([share, far]), 1)
            return jnp.stack([far, near[0], near[1]])

        far_a = swap_mp(share_a, 2)
        far_a, share_f = tie(far_a, share_f)
        line_a = line_of(share_a, far_a)
        far_f = swap_mp(share_f, 2)
        line_a, far_f, rows_one, rows_two = tie(line_a, far_f, rows_one, rows_two)
        near_a = plane_gather(line_a[:, :piece], dp_size)
        rows_one, rows_two = to_rows(rows_one, rows_two, dp_size)
        near_f = swap_mp(jnp.stack([share_f, far_f]), 1)
        line_f = jnp.stack([far_f, near_f[0], near_f[1]], axis=1)
        got = line_a[:, piece : piece + vector_rows.shape[0]].astype(F32).reshape(3, 2, -1)
        vectors = jnp.concatenate([vectors[None], got[:, 0] + got[:, 1]])
        q_width = qv_bias.shape[1]
        q_bias = vectors[:, :q_width].reshape(1, -1)
        v_bias = vectors[:, q_width : 2 * q_width].reshape(1, -1)

        def turn(values, axes):
            for axis, bit in zip(axes, (core, spot // 2, spot % 2)):
                values = jnp.where(bit == 1, jnp.flip(values, axis), values)
            return values

        hidden_bias = turn(vectors[:, 2 * q_width :].reshape(4, 2, 2, 2, piece), (1, 2, 3))
        hidden_bias = hidden_bias.transpose(1, 2, 3, 0, 4).reshape(4, 1, width)

        local_rows = local_attention.reshape(4, 2, piece, width)
        rows_one, rows_two, line_f, near_a, local_rows, local_up, grads_one, grads_two, hidden_bias, q_bias = tie(
            rows_one, rows_two, line_f, near_a, local_rows, local_up, grads_one, grads_two, hidden_bias, q_bias
        )
        other_a = across(near_a, 1)
        xs = across(line_f, 2)
        ys = across(line_f, 4)
        grads_one, grads_two = to_rows(grads_one, grads_two, dp_size)

        quarters = rows_one[strip + 1 : strip + 3, : 2 * strip].astype(jnp.int32).reshape(4, strip)

        def quarter(at):
            return lax.dynamic_index_in_dim(quarters, at, 0, keepdims=False)

        own_segments = jnp.concatenate([quarter(2 * core + parity), quarter(2 * core + 1 - parity)])
        far_segments = jnp.concatenate([quarter(2 - 2 * core + parity), quarter(3 - 2 * core - parity)])
        seg_q = own_segments[None, :]
        seg_k = jnp.concatenate([own_segments, far_segments])[None, :]

        normed_one, queries, own_kv, weights = project(
            place,
            rows_one,
            rows_two,
            row(first_gain),
            row(first_shift),
            local_rows,
            near_a,
            other_a,
            q_bias,
            v_bias,
        )
        flat_weights = weights.reshape(-1, width)
        xs, ys, own_kv, line_f, seg_q, seg_k, grads_one, grads_two = tie(
            xs, ys, own_kv, line_f, seg_q, seg_k, grads_one, grads_two
        )
        grads_in = (grads_one, grads_two)
        far_kv = across(own_kv, 1)
        du = across(xs[0], 4)
        dd = across(ys[1], 2)
        line_far = across(line_f, 1)
        xs_far = across(xs, 1)
        ys_far = across(ys, 1)
        far_kv, line_far, xs_far, ys_far = tie(far_kv, line_far, xs_far, ys_far)
        heads = (queries, own_kv, far_kv)
        context, log_total, mid_rows, normed_two = attend(
            *heads,
            seg_q,
            seg_k,
            flat_weights,
            rows_one,
            rows_two,
            row(out_bias),
            row(second_gain),
            row(second_shift),
        )
        du, dd, normed_two = tie(du, dd, normed_two)
        du_far = across(du, 1)
        dd_far = across(dd, 1)
        local_up = local_up.reshape(8, piece, width)
        local_down = down_weight.reshape(8, piece, width)
        both = (line_f, line_far, xs, xs_far, ys, ys_far, du, du_far, dd, dd_far)
        active, slope, final_rows = expand(
            place, normed_two, mid_rows, hidden_bias, local_up, local_down, both, row(down_bias)
        )

        back_one, back_two = from_rows(final_rows[:strip], final_rows[strip:], dp_size)
        up_other, down_other, normed_grad, bias_other = expand_back(
            1, place, grads_in, normed_two, active, slope, local_up, local_down, both[1::2], None
        )
        up_got = across(up_other, 1)
        down_got = across(down_other, 1)
        up_own, down_own, normed_grad, bias_own = expand_back(
            0, place, grads_in, normed_two, active, slope, local_up, local_down, both[0::2], normed_grad
        )
        up_got, down_got, normed_grad = tie(up_got, down_got, normed_grad)
        up_sent = add(up_own[1], up_got[1])
        down_sent = add(down_own[1], down_got[1])
        up_sent, down_sent, normed_grad = tie(up_sent, down_sent, normed_grad)
        up_sent = across(up_sent, 4)
        down_sent = across(down_sent, 2)
        grad_mid, grad_attn, grad_context, sums_two = settle(
            normed_grad, mid_rows, grads_in, row(second_gain), flat_weights
        )
        inputs = heads + (grad_context, context, log_total, seg_q, seg_k)
        dq, own_grad, far_grad = attend_back(*inputs)
        up_sent, down_sent, far_grad, back_one, back_two = tie(up_sent, down_sent, far_grad, back_one, back_two)
        got_kv = across(far_grad, 1)
        up_second, down_second = onward((up_own, up_got, up_sent), (down_own, down_got, down_sent))
        up_second, down_second, got_kv, grad_mid = tie(up_second, down_second, got_kv, grad_mid)
        up_second = across(up_second, 2)
        down_second = across(down_second, 4)
        attention_other = weigh(1, place, dq, own_grad, got_kv, context, normed_one, grad_attn, None)
        attention_got = across(attention_other, 1)
        attention_other, grad_mid = tie(attention_other, grad_mid)
        out_one, out_two, small = finish(
            place,
            dq,
            own_grad,
            got_kv,
            weights,
            rows_one,
            rows_two,
            row(first_gain),
            grad_mid,
            sums_two,
        )
        back_routes = [[(target, source) for source, target in route] for route in row_routes(dp_size)]
        out_one, out_two, attention_got = tie(out_one, out_two, attention_got)
        start_one = lax.ppermute(out_one, BOTH, back_routes[0])
        attention_grad = weigh(0, place, dq, own_grad, got_kv, context, normed_one, grad_attn, attention_got)
        attention_grad, start_one, up_second, down_second, out_two, small = tie(
            attention_grad, start_one, up_second, down_second, out_two, small
        )
        attention_grad = plane_scatter(attention_grad, dp_size)
        pair, pair_sent = merge((up_own, up_got, up_sent, up_second), (down_own, down_got, down_sent, down_second))
        pair_sent, small, bias_own, bias_other = tie(pair_sent, small, bias_own, bias_other)
        small = tally(place, small, bias_own, bias_other)
        small = small + across(small, 1)
        small_got = swap_mp(small, 1)
        pair_sent = swap_mp(pair_sent, 1)
        pair_sent, small_got = tie(pair_sent, small_got)

        bits = [1 << n for n in range(dp_size.bit_length() - 1)]
        small = small + small_got
        pair = add(pair, pair_sent)
        pair_sent = swap_mp(pair[1], 2)
        small_far = swap_mp(small, 2)
        attention_grad, small_far = tie(attention_grad, small_far)
        small = small + small_far
        activations = jnp.where(
            parity == 0, jnp.stack([back_one, back_two]), jnp.stack([back_two, back_one])
        )

        def lift(value):
            for bit in bits[3:]:
                value = value + across(value, bit)
            return value

        small = lift(small)
        attention_sent = swap_mp(attention_grad[2:], 1)
        pair, pair_sent, activations, _ = tie(pair, pair_sent, activations, attention_sent)
        if dp_size > 8:
            pair_sent = lift(add(pair[0], pair_sent))
            pair = jnp.zeros_like(pair)
        pair = plane_gather(pack(pair, pair_sent, small), dp_size)
        attention_sent, out_two = tie(attention_sent, out_two)
        half = strip // 2
        start_two = jnp.concatenate(
            [
                lax.ppermute(out_two[:half], BOTH, back_routes[1]),
                lax.ppermute(out_two[half:], BOTH, back_routes[1]),
            ],
            axis=0,
        )
        attention_grad = add(attention_grad[:2], attention_sent)
        attention_sent = swap_mp(attention_grad[1], 2)
        attention_sent, pair, start_two = tie(attention_sent, pair, start_two)
        grad_start = jnp.where(
            parity == 0, jnp.stack([start_one, start_two]), jnp.stack([start_two, start_one])
        )
        tokens_grad = jnp.where((mask_flags == 1)[:, :, None], 0.0, grad_start.astype(F32))
        attention_grad = lift(add(attention_grad[0], attention_sent))
        attention_grad = plane_gather(attention_grad, dp_size)
        up_weight_grad, down_weight_grad, small, up_bias_grad, qv_bias_grad = close_pair(place, pair, across(pair, 1))
        attention_grad, up_weight_grad, down_weight_grad, small, tokens_grad = tie(
            attention_grad, up_weight_grad, down_weight_grad, small, tokens_grad
        )
        w_qkv_grad, w_out_grad = close_attention(place, attention_grad, across(attention_grad, 1))
        w_qkv_grad = w_qkv_grad.transpose(0, 2, 1)
        up_bias_grad = up_bias_grad.reshape(-1)
        return (
            activations,
            tokens_grad,
            small[0],
            small[1],
            small[2],
            w_qkv_grad,
            qv_bias_grad,
            w_out_grad,
            small[3],
            small[4],
            small[5],
            up_weight_grad,
            up_bias_grad,
            down_weight_grad,
            small[6],
        )

    return body


def solution(mesh):
    in_specs = (
        P("dp", "mp", None),
        P("dp", None),
        P("dp", "mp"),
        P(),
        P(),
        P(),
        P(None, None, "mp"),
        P(None, "mp"),
        P("mp", None),
        P(),
        P(),
        P(),
        P(None, "mp"),
        P("mp"),
        P("mp", None),
        P(),
        P("dp", "mp", None),
    )
    out_specs = (
        P("dp", "mp", None),
        P("dp", "mp", None),
        P(),
        P(),
        P(),
        P(None, None, "mp"),
        P(None, "mp"),
        P("mp", None),
        P(),
        P(),
        P(),
        P(None, "mp"),
        P("mp"),
        P("mp", None),
        P(),
    )
    return jax.shard_map(
        make_body(mesh.shape["dp"]), mesh=mesh, in_specs=in_specs, out_specs=out_specs, check_vma=False
    )
```

```python
import jax
import jax.numpy as jnp
from jax import lax
from jax.experimental import pallas as pl
from jax.experimental.pallas import tpu as pltpu
from jax.sharding import PartitionSpec as P

HD = 64
EPSILON = 1e-06
NEG_FILL = -1e30
BF = jnp.bfloat16
F32 = jnp.float32
BOTH = ("dp", "mp")
BLOCK_ORDER = (0, 2, 1, 3)
NT = (((1,), (1,)), ((), ()))
NN = (((1,), (0,)), ((), ()))
TN = (((0,), (0,)), ((), ()))


def dot(left, right, dims):
    return lax.dot_general(left, right, dims, preferred_element_type=F32)


def swap_dp(value, bit, dp_size):
    return lax.ppermute(value, "dp", [(i, i ^ bit) for i in range(dp_size)])


def swap_mp(value, bit):
    return lax.ppermute(value, "mp", [(i, i ^ bit) for i in range(4)])


def row_routes(dp_size):
    first, second = [], []
    for pair in range(dp_size // 2):
        for core in range(2):
            for place in range(4):
                source = (2 * pair + core) * 4 + place
                for row in range(2):
                    target = (2 * pair + place // 2) * 4 + 2 * core + row
                    (first if row == place % 2 else second).append((source, target))
    return first, second


def to_rows(first, second, dp_size):
    routes = row_routes(dp_size)
    return (lax.ppermute(first, BOTH, routes[0]), lax.ppermute(second, BOTH, routes[1]))


def from_rows(first, second, dp_size):
    back = [[(target, source) for source, target in route] for route in row_routes(dp_size)]
    return (lax.ppermute(first, BOTH, back[0]), lax.ppermute(second, BOTH, back[1]))


EXTRA = 16
MIB_ATTEND = 18
COST = pl.CostEstimate(flops=1000000, transcendentals=0, bytes_accessed=1000)


def plane_groups(dp_size):
    return [[base * 8 + core + 2 * k for k in range(4)] for base in range(dp_size // 8) for core in range(2)]


def plane_gather(value, dp_size):
    spread = jnp.broadcast_to(value[None], (4,) + value.shape)
    return lax.all_to_all(spread, "dp", 0, 0, tiled=True, axis_index_groups=plane_groups(dp_size))


def plane_scatter(value, dp_size):
    pieces = lax.all_to_all(value, "dp", 0, 0, tiled=True, axis_index_groups=plane_groups(dp_size))
    return jnp.sum(pieces.astype(F32), axis=0).astype(BF)


def tie(*values):
    return lax.optimization_barrier(values)


def add(left, right):
    return (left.astype(F32) + right.astype(F32)).astype(BF)


def whole(value):
    rank = value.ndim
    return pl.BlockSpec(value.shape, lambda *i: (0,) * rank, pipeline_mode=pl.Buffered(1))


def scalars():
    return pl.BlockSpec(memory_space=pltpu.SMEM)


def call(kernel, name, mib, grid, in_specs, out_specs, out_shape, scratch, flops, moved, args):
    return pl.pallas_call(
        kernel,
        grid=grid,
        in_specs=in_specs,
        out_specs=out_specs,
        out_shape=out_shape,
        scratch_shapes=scratch,
        compiler_params=pltpu.CompilerParams(vmem_limit_bytes=mib << 20),
        cost_estimate=COST,
        name=name,
    )(*args)


def centre(rows):
    row_mean = jnp.mean(rows, axis=-1, keepdims=True)
    centred = rows - row_mean
    variance = jnp.mean(centred * centred, axis=-1, keepdims=True)
    inv_scale = lax.rsqrt(variance + EPSILON)
    return (centred * inv_scale, inv_scale)


def centre_back(incoming, unit_rows, inv_scale, gain):
    scaled = incoming * gain
    inner_one = jnp.mean(scaled, axis=-1, keepdims=True)
    inner_two = jnp.mean(scaled * unit_rows, axis=-1, keepdims=True)
    return inv_scale * (scaled - inner_one - unit_rows * inner_two)


def project_kernel(place, one, two, gain, shift, local, near, other, q_bias, v_bias, normed, q, kv, weights):
    strip = normed.shape[0] // 2
    for i, rows in enumerate((one, two)):
        unit, _ = centre(rows[:strip].astype(F32))
        normed[i * strip : (i + 1) * strip] = (unit * gain[...] + shift[...]).astype(BF)
    core = place[0]
    weights[:, 0] = local[...]
    for k in range(4):
        weights[2 * core + k // 2, 1:4, k % 2] = near[k]
        weights[2 - 2 * core + k // 2, 1:4, k % 2] = other[k]
    width = one.shape[1]
    rows = normed[...]
    q[...] = (dot(rows, weights[0].reshape(width, width), NT) + q_bias[...]).astype(BF)
    kv[0] = dot(rows, weights[1].reshape(width, width), NT).astype(BF)
    kv[1] = (dot(rows, weights[2].reshape(width, width), NT) + v_bias[...]).astype(BF)


def project(place, one, two, gain, shift, local, near, other, q_bias, v_bias):
    width = one.shape[1]
    tokens = 2 * (one.shape[0] - EXTRA)
    args = (place, one, two, gain, shift, local, near, other, q_bias, v_bias)
    shapes = [
        jax.ShapeDtypeStruct((tokens, width), BF),
        jax.ShapeDtypeStruct((tokens, width), BF),
        jax.ShapeDtypeStruct((2, tokens, width), BF),
        jax.ShapeDtypeStruct((4, 4, 2, width // 8, width), BF),
    ]
    return call(
        project_kernel,
        "project",
        16,
        (1,),
        [scalars()] + [whole(x) for x in args[1:]],
        [whole(x) for x in shapes],
        shapes,
        [],
        6 * tokens * width * width,
        12 * width * width,
        args,
    )


def spare_base(head):
    return 0 if head else HD


def head_lanes(shape, head):
    lanes = lax.broadcasted_iota(jnp.int32, shape, 1)
    return (lanes >= HD) if head else (lanes < HD)


def upright(line):
    return jnp.broadcast_to(line, (128, line.shape[1])).T


def prepare_lanes(segk_ref, segq_ref, key_extra, query_extra):
    for segments, extra, is_key in ((segk_ref, key_extra, True), (segq_ref, query_extra, False)):
        ids = upright(segments[...])
        for head in range(2):
            lanes = lax.broadcasted_iota(jnp.int32, ids.shape, 1) - spare_base(head)
            inside = (lanes >= 0) & (lanes < 4)
            if is_key:
                values = jnp.where(inside & (ids != lanes), NEG_FILL, 0.0)
            else:
                values = jnp.where(inside & (ids == lanes), 1.0, 0.0)
            extra[head] = values.astype(BF)


def attend_kernel(
    q_ref, own_ref, far_ref, segq_ref, segk_ref, weights, one, two, o_bias, gain, shift,
    ctx_ref, lse_ref, mid_ref, normed_ref, keys, values_t, key_extra, query_extra, total,
):
    half = own_ref.shape[1]
    step = pl.program_id(0)

    @pl.when(step == 0)
    def _():
        prepare_lanes(segk_ref, segq_ref, key_extra, query_extra)
        for head in range(2):
            values_t[head, HD:] = jnp.ones_like(values_t[head, HD:])

    for i, ref in enumerate((own_ref, far_ref)):
        span = slice(i * half, (i + 1) * half)
        part = ref[0]
        turned = ref[1].T
        for head in range(2):
            keys[head, span] = jnp.where(head_lanes(part.shape, head), part, key_extra[head, span])
            values_t[head, :HD, span] = turned[head * HD : (head + 1) * HD]
    tokens = q_ref.shape[0]
    block = tokens
    for start in range(0, tokens, block):
        span = slice(start, start + block)
        query = q_ref[span, :] * jnp.asarray(HD**-0.5, BF)
        heads = range(2)
        owns = [jnp.where(head_lanes(query.shape, h), query, query_extra[h, span]) for h in heads]
        scores = [dot(keys[h], owns[h], NT) for h in heads]
        maxima = [jnp.max(v, axis=0, keepdims=True) for v in scores]
        powers = [jnp.exp(v - m).astype(BF) for v, m in zip(scores, maxima)]
        parts = [dot(values_t[h], powers[h], NN) for h in heads]
        pieces = [v[:HD] / v[HD : HD + 1] for v in parts]
        sums = [m + jnp.log(v[HD : HD + 1]) for m, v in zip(maxima, parts)]
        context = jnp.concatenate(pieces, axis=0).T.astype(BF)
        ctx_ref[span, :] = context
        for h in heads:
            lse_ref[0, h : h + 1, span] = sums[h]
        mixed = dot(context, weights[...], NN)

        @pl.when(step == 0)
        def _():
            total[span, :] = mixed

        @pl.when(step > 0)
        def _():
            total[span, :] += mixed

    @pl.when(step == pl.num_programs(0) - 1)
    def _():
        strip = tokens // 2
        for i, rows in enumerate((one, two)):
            span = slice(i * strip, (i + 1) * strip)
            mid = rows[:strip].astype(F32) + total[span, :] + o_bias[...]
            mid_ref[span, :] = mid
            unit, _ = centre(mid)
            normed_ref[span, :] = (unit * gain[...] + shift[...]).astype(BF)


def attend(q, own, far, seg_q, seg_k, weights, one, two, o_bias, gain, shift):
    rows, width = q.shape
    pairs = width // 128
    half = own.shape[1]
    args = (q, own, far, seg_q, seg_k, weights, one, two, o_bias, gain, shift)
    head_block = pl.BlockSpec((rows, 128), lambda i: (0, i))
    key_block = pl.BlockSpec((2, half, 128), lambda i: (0, 0, i))
    shapes = [
        jax.ShapeDtypeStruct((rows, width), BF),
        jax.ShapeDtypeStruct((pairs, 2, rows), F32),
        jax.ShapeDtypeStruct((rows, width), F32),
        jax.ShapeDtypeStruct((rows, width), BF),
    ]
    specs = [head_block, key_block, key_block, whole(seg_q), whole(seg_k)]
    specs.append(pl.BlockSpec((128, width), lambda i: (3 * pairs + i, 0)))
    return call(
        attend_kernel,
        "attend",
        20,
        (pairs,),
        specs + [whole(x) for x in args[6:]],
        [head_block, pl.BlockSpec((1, 2, rows), lambda i: (i, 0, 0)), whole(shapes[2]), whole(shapes[3])],
        shapes,
        [
            pltpu.VMEM((2, 2 * half, 128), BF),
            pltpu.VMEM((2, HD + 16, 2 * half), BF),
            pltpu.VMEM((2, 2 * half, 128), BF),
            pltpu.VMEM((2, rows, 128), BF),
            pltpu.VMEM((rows, width), F32),
        ],
        0,
        0,
        args,
    )


def load_block(place, flip, at_y, mat, local, pieces, block):
    core = place[0] if not flip else 1 - place[0]
    line, along_x, along_y, diagonal = pieces
    for x in range(2):
        spot = place[1 + 2 * at_y + x]
        block[x, 0] = local[core * 4 + spot]
        if at_y and x:
            block[x, 1:4] = diagonal[...]
        else:
            block[x, 1:4] = (along_y if at_y else along_x if x else line)[mat]


def expand_kernel(
    place, normed, mid, bias, local_up, local_down, line, line_far, xs, xs_far, ys, ys_far, du, du_far, dd, dd_far,
    d_bias, active, slope, out, up, down, total,
):
    step = pl.program_id(0)
    for j in range(4):

        @pl.when(step == j)
        def _():
            flip = j // 2
            three = (line_far, xs_far, ys_far) if flip else (line, xs, ys)
            load_block(place, flip, j % 2, 0, local_up, three + ((du_far if flip else du),), up)
            load_block(place, flip, j % 2, 1, local_down, three + ((dd_far if flip else dd),), down)

    width = normed.shape[1]
    hidden = dot(normed[...], up[...].reshape(width, width), NT) + bias[0]
    cdf = 0.5 * (1.0 + lax.erf(hidden * (0.5**0.5)))
    pulled = cdf + hidden * jnp.exp(-0.5 * hidden * hidden) * 0.3989422804014327
    slope[...] = pulled.astype(BF)
    active[...] = (hidden * cdf).astype(BF)
    part = dot(active[...], down[...].reshape(width, width), NN)

    @pl.when(step == 0)
    def _():
        total[...] = mid[...] + d_bias[...] + part

    @pl.when((step > 0) & (step < 3))
    def _():
        total[...] += part

    @pl.when(step == 3)
    def _():
        out[...] = (total[...] + part).astype(BF)


def expand(place, normed, mid, bias, local_up, local_down, pieces, d_bias):
    tokens, width = normed.shape
    piece = width // 8
    args = (place, normed, mid, bias, local_up, local_down, *pieces, d_bias)
    hidden = pl.BlockSpec((tokens, width), lambda j: (0, j))
    shapes = [
        jax.ShapeDtypeStruct((tokens, 4 * width), BF),
        jax.ShapeDtypeStruct((tokens, 4 * width), BF),
        jax.ShapeDtypeStruct((tokens, width), BF),
    ]
    specs = [scalars()] + [whole(x) for x in args[1:]]
    specs[3] = pl.BlockSpec((1, 1, width), lambda j: (j, 0, 0))
    return call(
        expand_kernel,
        "expand",
        26,
        (4,),
        specs,
        [hidden, hidden, whole(shapes[2])],
        shapes,
        [pltpu.VMEM((2, 4, piece, width), BF)] * 2 + [pltpu.VMEM((tokens, width), F32)],
        16 * tokens * width * width,
        20 * width * width,
        args,
    )


def expand_back_kernel(
    flip, place, grad_one, grad_two, normed, active, slope, local_up, local_down, line, xs, ys, du, dd, before,
    up_grad, down_grad, normed_grad, bias_grad, up, down,
):
    step = pl.program_id(0)
    for j in range(2):

        @pl.when(step == j)
        def _():
            load_block(place, flip, j, 0, local_up, (line, xs, ys, du), up)
            load_block(place, flip, j, 1, local_down, (line, xs, ys, dd), down)

    width = normed.shape[1]
    wide = up.shape
    grad = jnp.concatenate([grad_one[...], grad_two[...]], axis=0)
    incoming = dot(grad, down[...].reshape(width, width), NT)
    grad_hidden = (incoming * slope[...].astype(F32)).astype(BF)
    bias_grad[0] = jnp.sum(grad_hidden.astype(F32), axis=0, keepdims=True)
    down_grad[...] = dot(active[...], grad, TN).astype(BF).reshape(2, 1, *wide[1:])
    up_grad[0] = dot(grad_hidden, normed[...], TN).astype(BF).reshape(wide)
    part = dot(grad_hidden, up[...].reshape(width, width), NN)

    @pl.when(step == 0)
    def _():
        if before is None:
            normed_grad[...] = part
        else:
            normed_grad[...] = before[...] + part

    @pl.when(step > 0)
    def _():
        normed_grad[...] += part


def expand_back(flip, place, grad, normed, active, slope, local_up, local_down, pieces, before):
    tokens, width = normed.shape
    piece = width // 8
    args = (place, *grad, normed, active, slope, local_up, local_down, *pieces)
    if before is not None:
        args = args + (before,)

    def kernel(*refs):
        if before is None:
            refs = refs[:13] + (None,) + refs[13:]
        return expand_back_kernel(flip, *refs)

    hidden = pl.BlockSpec((tokens, width), lambda j: (0, j + 2 * flip))
    shapes = [
        jax.ShapeDtypeStruct((2, 2, 4, piece, width), BF),
        jax.ShapeDtypeStruct((2, 2, 4, piece, width), BF),
        jax.ShapeDtypeStruct((tokens, width), F32),
        jax.ShapeDtypeStruct((2, 1, width), F32),
    ]
    specs = [scalars()] + [whole(x) for x in args[1:]]
    specs[4] = specs[5] = hidden
    return call(
        kernel,
        "expand_back_other" if flip else "expand_back_own",
        22,
        (2,),
        specs,
        [
            pl.BlockSpec((1, 2, 4, piece, width), lambda j: (j, 0, 0, 0, 0)),
            pl.BlockSpec((2, 1, 4, piece, width), lambda j: (0, j, 0, 0, 0)),
            whole(shapes[2]),
            pl.BlockSpec((1, 1, width), lambda j: (j, 0, 0)),
        ],
        shapes,
        [pltpu.VMEM((2, 4, piece, width), BF)] * 2,
        20 * tokens * width * width,
        16 * width * width,
        args,
    )


def settle_kernel(incoming, mid, grad_one, grad_two, gain, wo, grad_mid, grad_attn, grad_context, sums):
    strip = grad_one.shape[0]
    parts = None
    for at in range(0, mid.shape[0], strip):
        span = slice(at, at + strip)
        unit, inv_scale = centre(mid[span, :])
        given = incoming[span, :]
        outer = (grad_two if at else grad_one)[...].astype(F32)
        made = outer + centre_back(given, unit, inv_scale, gain[...])
        grad_mid[span, :] = made
        grad_attn[span, :] = made.astype(BF)
        grad_context[span, :] = dot(made.astype(BF), wo[...], NT).astype(BF)
        rows = [jnp.sum(v, axis=0, keepdims=True) for v in (made, given * unit, given, outer)]
        parts = rows if parts is None else [a + b for a, b in zip(parts, rows)]
    for i, row in enumerate(parts):
        sums[i : i + 1, :] = row


def settle(incoming, mid, grad, gain, weights):
    tokens, width = mid.shape
    args = (incoming, mid, *grad, gain, weights)
    specs = [whole(x) for x in args]
    specs[5] = pl.BlockSpec((width, width), lambda i: (3, 0))
    shapes = [
        jax.ShapeDtypeStruct((tokens, width), F32),
        jax.ShapeDtypeStruct((tokens, width), BF),
        jax.ShapeDtypeStruct((tokens, width), BF),
        jax.ShapeDtypeStruct((8, width), F32),
    ]
    return call(
        settle_kernel,
        "settle",
        13,
        (1,),
        specs,
        [whole(x) for x in shapes],
        shapes,
        [],
        2 * tokens * width * width,
        14 * tokens * width,
        args,
    )


def quarter_block(value, at):
    rank = value.ndim
    shape = (1,) * len(at) + value.shape[len(at) :]
    return pl.BlockSpec(shape, lambda *i: at + (0,) * (rank - len(at)), pipeline_mode=pl.Buffered(1))


def onward_kernel(*refs):
    for i in range(2):
        own, got, sent = (ref[...].astype(F32) for ref in refs[3 * i : 3 * i + 3])
        refs[6 + i][...] = (own[0, 0] + got[0, 0] + sent[0]).astype(BF)


def onward(up, down):
    args = up + down
    shape = jax.ShapeDtypeStruct(up[0].shape[2:], BF)
    return call(
        onward_kernel,
        "onward",
        12,
        (1,),
        [quarter_block(x, (0, 1) if x.ndim == 5 else (1,)) for x in args],
        [whole(shape)] * 2,
        [shape] * 2,
        [],
        0,
        0,
        args,
    )


def merge_kernel(*refs):
    kept, passed = refs[8:]
    for i in range(2):
        own, got, sent, second = refs[4 * i : 4 * i + 4]
        for part, out in ((slice(0, 2), kept), (slice(2, 4), passed)):
            total = own[0, 0, part].astype(F32) + got[0, 0, part].astype(F32)
            total = total + sent[0, part].astype(F32) + second[part].astype(F32)
            out[:, i] = total.astype(BF)


def merge(up, down):
    args = up + down
    shapes = [jax.ShapeDtypeStruct((2, 2) + up[0].shape[3:], BF)] * 2
    specs = [
        quarter_block(x, (0, 0)) if x.ndim == 5 else quarter_block(x, (0,)) if x.ndim == 4 else whole(x) for x in args
    ]
    return call(merge_kernel, "merge", 60, (1,), specs, [whole(x) for x in shapes], shapes, [], 0, 0, args)


def close_pair_kernel(place, near, other, up_grad, down_grad, vectors, up_bias, qv_bias):
    width = near.shape[2]
    piece = width // 8
    for c in range(2):
        for ref, core in ((near, place[0]), (other, 1 - place[0])):

            @pl.when(core == c)
            def _():
                for k in range(4):
                    at = (4 * c + k) * piece
                    down_grad[at : at + piece, :] = ref[k, piece : 2 * piece].astype(F32)
                rows = jnp.concatenate([ref[k, :piece] for k in range(4)], axis=0)
                up_grad[:, 4 * c * piece : 4 * (c + 1) * piece] = rows.astype(F32).T

    total = None
    for k in range(4):
        for at in (2 * piece, 2 * piece + EXTRA):
            part = near[k, at : at + EXTRA].astype(F32)
            total = part if total is None else total + part
    vectors[...] = total[:8]

    def slot(entry):
        r, g = 7 + entry // 6, entry % 6
        return total[r : r + 1, 128 * g : 128 * g + piece]

    for z in range(4):

        @pl.when(place[5] == z)
        def _():
            for k in range(8):
                up_bias[:, k * piece : (k + 1) * piece] = slot(8 * z + k)
            for i in range(2):
                for half in range(2):
                    qv_bias[i : i + 1, half * piece : (half + 1) * piece] = slot(32 + 8 * i + 2 * z + half)


def close_pair(place, near, other):
    width = near.shape[2]
    args = (place, near, other)
    shapes = [
        jax.ShapeDtypeStruct((width, width), F32),
        jax.ShapeDtypeStruct((width, width), F32),
        jax.ShapeDtypeStruct((8, width), F32),
        jax.ShapeDtypeStruct((1, width), F32),
        jax.ShapeDtypeStruct((2, width // 4), F32),
    ]
    return call(
        close_pair_kernel,
        "close_pair",
        12,
        (1,),
        [scalars(), whole(near), whole(other)],
        [whole(x) for x in shapes],
        shapes,
        [],
        0,
        0,
        args,
    )


def close_attention_kernel(place, near, other, qkv_grad, out_grad):
    piece = near.shape[1]
    for c in range(2):
        for ref, core in ((near, place[0]), (other, 1 - place[0])):

            @pl.when(core == c)
            def _():
                for k in range(4):
                    span = slice(k % 2 * piece, (k % 2 + 1) * piece)
                    part = ref[k].astype(F32)
                    if 2 * c + k // 2 < 3:
                        qkv_grad[2 * c + k // 2, span, :] = part
                    else:
                        out_grad[span, :] = part


def close_attention(place, near, other):
    piece, width = near.shape[1:]
    args = (place, near, other)
    shapes = [
        jax.ShapeDtypeStruct((3, 2 * piece, width), F32),
        jax.ShapeDtypeStruct((2 * piece, width), F32),
    ]
    return call(
        close_attention_kernel,
        "close_attention",
        6,
        (1,),
        [scalars(), whole(near), whole(other)],
        [whole(x) for x in shapes],
        shapes,
        [],
        0,
        0,
        args,
    )


def flip_kernel(value, out):
    out[...] = value[...].T


def flip(value):
    shape = jax.ShapeDtypeStruct(value.shape[::-1], value.dtype)
    return call(flip_kernel, "flip", 4, (1,), [whole(value)], whole(shape), shape, [], 0, 0, (value,))


def weigh_kernel(flip, place, dq, mine, got, context, normed, grad, before, out, left, right):
    core = place[0] if not flip else 1 - place[0]
    width = dq.shape[1]
    piece = width // 8

    @pl.when(core == 0)
    def _():
        left[0] = dq[...]
        left[1] = (mine[0].astype(F32) + got[0].astype(F32)).astype(BF)
        right[...] = normed[...]

    @pl.when(core == 1)
    def _():
        left[0] = (mine[1].astype(F32) + got[1].astype(F32)).astype(BF)
        left[1] = context[...]
        right[...] = grad[...]

    for i in range(2):
        rows = normed[...] if i == 0 else right[...]
        made = dot(left[i], rows, TN).reshape(4, 2, piece, width)
        for k in range(2):
            part = made[:, k]
            if before is not None:
                part = part + before[2 * i + k].astype(F32)
            out[2 * i + k] = part.astype(BF)


def weigh(flip, place, dq, mine, got, context, normed, grad, before):
    tokens, width = dq.shape
    args = (place, dq, mine, got, context, normed, grad)
    if before is not None:
        args = args + (before,)

    def kernel(*refs):
        if before is None:
            refs = refs[:7] + (None,) + refs[7:]
        return weigh_kernel(flip, *refs)

    shape = jax.ShapeDtypeStruct((4, 4, width // 8, width), BF)
    return call(
        kernel,
        "weigh_other" if flip else "weigh_own",
        14,
        (1,),
        [scalars()] + [whole(x) for x in args[1:]],
        whole(shape),
        shape,
        [pltpu.VMEM((2, tokens, width), BF), pltpu.VMEM((tokens, width), BF)],
        4 * tokens * width * width,
        8 * width * width,
        args,
    )


def finish_kernel(
    place, dq, mine, got, weights, one, two, gain, grad_mid, sums_two,
    out_one, out_two, small, total,
):
    width = dq.shape[1]
    keys = (mine[0].astype(F32) + got[0].astype(F32)).astype(BF)
    values = (mine[1].astype(F32) + got[1].astype(F32)).astype(BF)
    total[...] = dot(dq[...], weights[0].reshape(width, width), NN)
    total[...] += dot(keys, weights[1].reshape(width, width), NN)
    total[...] += dot(values, weights[2].reshape(width, width), NN)
    strip = dq.shape[0] // 2
    gathered = None
    for i, rows in enumerate((one, two)):
        span = slice(i * strip, (i + 1) * strip)
        unit, inv_scale = centre(rows[:strip].astype(F32))
        incoming = total[span, :]
        grad_start = grad_mid[span, :] + centre_back(incoming, unit, inv_scale, gain[...])
        high = grad_start.astype(BF)
        (out_two if i else out_one)[...] = high
        low = (grad_start - high.astype(F32)).astype(BF)
        flags = rows[strip : strip + 16, :strip]
        masked = (dot(flags, high, NN) + dot(flags, low, NN))[:1]
        parts = [masked] + [jnp.sum(v, axis=0, keepdims=True) for v in (incoming * unit, incoming)]
        gathered = parts if gathered is None else [a + b for a, b in zip(gathered, parts)]
    small[...] = jnp.zeros_like(small)
    gathered += [sums_two[i : i + 1, :] for i in range(4)]
    for r, line in enumerate(gathered):
        for g in range(width // 128):
            small[16 * g + r : 16 * g + r + 1, :] = line[:, 128 * g : 128 * g + 128]
    piece = width // 8
    for i, value in enumerate((dq[...], values)):
        line = jnp.sum(value.astype(F32), axis=0, keepdims=True)
        for j, distance in enumerate(BLOCK_ORDER):
            for half in range(2):
                entry = 32 + 8 * i + place[5 + distance] * 2 + half
                at = 16 * lax.rem(entry, 6) + 7 + entry // 6
                span = slice((2 * j + half) * piece, (2 * j + half + 1) * piece)
                small[pl.ds(at, 1), :piece] = line[:, span]


def finish(place, dq, mine, got, weights, one, two, gain, grad_mid, sums_two):
    tokens, width = dq.shape
    args = (place, dq, mine, got, weights, one, two, gain, grad_mid, sums_two)
    specs = [scalars()] + [whole(x) for x in args[1:]]
    specs[4] = pl.BlockSpec((3,) + weights.shape[1:], lambda i: (0,) * 5, pipeline_mode=pl.Buffered(1))
    shapes = [
        jax.ShapeDtypeStruct((tokens // 2, width), BF),
        jax.ShapeDtypeStruct((tokens // 2, width), BF),
        jax.ShapeDtypeStruct((96, 128), F32),
    ]
    return call(
        finish_kernel,
        "finish",
        15,
        (1,),
        specs,
        [whole(x) for x in shapes],
        shapes,
        [pltpu.VMEM((tokens, width), F32)],
        0,
        0,
        args,
    )


def tally_kernel(place, table, own, other, out):
    out[...] = table[...]
    width = own.shape[2]
    piece = width // 8
    for flip, sums in enumerate((own, other)):
        core = place[0] if not flip else 1 - place[0]
        for y in range(2):
            line = sums[y]
            for x in range(2):
                spot = place[1 + 2 * y + x]
                for i, distance in enumerate(BLOCK_ORDER):
                    entry = place[5 + distance] * 8 + core * 4 + spot
                    at = 16 * lax.rem(entry, 6) + 7 + entry // 6
                    span = slice((4 * x + i) * piece, (4 * x + i + 1) * piece)
                    out[pl.ds(at, 1), :piece] = line[:, span]


def tally(place, table, own, other):
    args = (place, table, own, other)
    shape = jax.ShapeDtypeStruct(table.shape, F32)
    specs = [scalars()] + [whole(x) for x in args[1:]]
    return call(tally_kernel, "tally", 4, (1,), specs, whole(shape), shape, [], 0, 0, args)


def pack_kernel(kept, got, small, out):
    piece, width = kept.shape[2:]
    for i in range(2):
        out[i * piece : (i + 1) * piece, :] = (kept[0, i].astype(F32) + got[i].astype(F32)).astype(BF)
    for g in range(width // 128):
        lanes = slice(128 * g, 128 * g + 128)
        value = small[16 * g : 16 * g + 16, :]
        high = value.astype(BF)
        out[2 * piece : 2 * piece + 16, lanes] = high
        out[2 * piece + 16 :, lanes] = (value - high.astype(F32)).astype(BF)


def pack(kept, got, small):
    piece, width = kept.shape[2:]
    args = (kept, got, small)
    shape = jax.ShapeDtypeStruct((2 * piece + 32, width), BF)
    specs = [quarter_block(kept, (0,)), whole(got), whole(small)]
    return call(pack_kernel, "pack", 4, (1,), specs, whole(shape), shape, [], 0, 0, args)


def attend_back_kernel(
    q_ref,
    own_ref,
    far_ref,
    g_ref,
    ctx_ref,
    lse_ref,
    segq_ref,
    segk_ref,
    dq_ref,
    own_grad_ref,
    far_grad_ref,
    keys,
    keys_t,
    values,
    dk_total,
    dv_total,
    key_ids,
):
    half = own_ref.shape[1]

    @pl.when(pl.program_id(0) == 0)
    def _():
        key_ids[...] = upright(segk_ref[...])

    keys[:half] = own_ref[0]
    keys[half:] = far_ref[0]
    keys_t[:, :half] = own_ref[0].T
    keys_t[:, half:] = far_ref[0].T
    values[:half] = own_ref[1]
    values[half:] = far_ref[1]
    total = q_ref.shape[0]
    block = 256
    scale = jnp.asarray(HD**-0.5, BF)
    for start in range(0, total, block):
        span = slice(start, start + block)
        same = key_ids[:, 0:1] == segq_ref[:, span]
        query = q_ref[span, :] * scale
        grad = g_ref[span, :]
        product = (grad.astype(F32) * ctx_ref[span, :].astype(F32)).T
        lanes = lax.broadcasted_iota(jnp.int32, query.shape, 1)
        pieces = []
        for head in range(2):
            own = (lanes >= HD) if head else (lanes < HD)
            query_own = jnp.where(own, query, jnp.zeros_like(query))
            grad_own = jnp.where(own, grad, jnp.zeros_like(grad))
            scores = dot(keys[...], query_own, NT)
            probs = jnp.exp(jnp.where(same, scores, NEG_FILL) - lse_ref[0, head : head + 1, span])
            grad_probs = dot(values[...], grad_own, NT)
            row_dot = jnp.sum(product[head * HD : (head + 1) * HD, :], axis=0, keepdims=True)
            grad_scores = (probs * (grad_probs - row_dot)).astype(BF)
            dv = dot(probs.astype(BF), grad_own, NN)
            dk = dot(grad_scores, query_own, NN)
            if start == 0 and head == 0:
                dv_total[...] = dv
                dk_total[...] = dk
            else:
                dv_total[...] += dv
                dk_total[...] += dk
            pieces.append(dot(keys_t[head * HD : (head + 1) * HD, :], grad_scores, NN))
        dq_ref[span, :] = (jnp.concatenate(pieces, axis=0).T * HD**-0.5).astype(BF)
    own_grad_ref[0] = dk_total[:half].astype(BF)
    far_grad_ref[0] = dk_total[half:].astype(BF)
    own_grad_ref[1] = dv_total[:half].astype(BF)
    far_grad_ref[1] = dv_total[half:].astype(BF)


def attend_back(q, own, far, grad, ctx, lse, seg_q, seg_k):
    rows, width = q.shape
    pairs = width // 128
    half = own.shape[1]
    args = (q, own, far, grad, ctx, lse, seg_q, seg_k)
    head_block = pl.BlockSpec((rows, 128), lambda i: (0, i))
    key_block = pl.BlockSpec((2, half, 128), lambda i: (0, 0, i))
    lse_block = pl.BlockSpec((1, 2, rows), lambda i: (i, 0, 0))
    shapes = [jax.ShapeDtypeStruct((rows, width), BF)] + [jax.ShapeDtypeStruct((2, half, width), BF)] * 2
    return call(
        attend_back_kernel,
        "attend_back",
        13,
        (pairs,),
        [head_block, key_block, key_block, head_block, head_block, lse_block, whole(seg_q), whole(seg_k)],
        [head_block, key_block, key_block],
        shapes,
        [
            pltpu.VMEM((2 * half, 128), BF),
            pltpu.VMEM((128, 2 * half), BF),
            pltpu.VMEM((2 * half, 128), BF),
            pltpu.VMEM((2 * half, 128), F32),
            pltpu.VMEM((2 * half, 128), F32),
            pltpu.VMEM((2 * half, 128), jnp.int32),
        ],
        0,
        0,
        args,
    )


def make_body(dp_size):
    def body(
        tokens,
        segment_ids,
        mask_flags,
        mask_embed,
        first_gain,
        first_shift,
        query_key_value_weight,
        qv_bias,
        output_weight,
        out_bias,
        second_gain,
        second_shift,
        up_weight,
        expand_bias,
        down_weight,
        down_bias,
        out_grad,
    ):
        dp_at = lax.axis_index("dp")
        mp_at = lax.axis_index("mp")
        core = dp_at % 2
        spot = (dp_at // 2) % 4
        parity = mp_at % 2
        width = tokens.shape[2]
        strip = tokens.shape[1]
        piece = width // 8
        place = jnp.stack([core] + [spot ^ r for r in range(4)] + [mp_at ^ d for d in range(4)]).astype(jnp.int32)

        def across(value, bit):
            return swap_dp(value, bit, dp_size)

        def pick(values):
            return (
                lax.dynamic_index_in_dim(values, parity, 0, keepdims=False),
                lax.dynamic_index_in_dim(values, 1 - parity, 0, keepdims=False),
            )

        def row(vector):
            return vector.reshape(1, -1)

        local_attention = jnp.concatenate(
            [query_key_value_weight.transpose(0, 2, 1).reshape(-1, width), output_weight], axis=0
        )
        offset = (core * 4 + spot) * piece
        vectors = jnp.concatenate([qv_bias.reshape(-1), expand_bias])
        vector_high = vectors.astype(BF)
        vector_low = (vectors - vector_high.astype(F32)).astype(BF)
        vector_rows = jnp.concatenate([vector_high, vector_low]).reshape(-1, width)
        share_a = jnp.concatenate(
            [
                lax.dynamic_slice_in_dim(local_attention, offset, piece, 0),
                jnp.pad(vector_rows, ((0, EXTRA - vector_rows.shape[0]), (0, 0))),
            ],
            axis=0,
        )
        local_up = flip(up_weight)
        share_f = jnp.stack(
            [
                lax.dynamic_slice_in_dim(local_up, offset, piece, 0),
                lax.dynamic_slice_in_dim(down_weight, offset, piece, 0),
            ]
        )
        start_rows = jnp.where((mask_flags == 1)[:, :, None], mask_embed.astype(BF), tokens)
        flag_rows = jnp.pad(mask_flags.astype(BF)[:, None, :], ((0, 0), (0, 0), (0, width - strip)))
        segment_rows = segment_ids.astype(BF).reshape(segment_ids.shape[0], 2, -1)
        segment_rows = jnp.pad(segment_rows, ((0, 0), (0, EXTRA - 3), (0, width - segment_rows.shape[2])))
        messages = jnp.concatenate([start_rows, flag_rows, segment_rows], axis=1)
        rows_one, rows_two = pick(messages)
        grads_one, grads_two = pick(out_grad)

        def line_of(share, far):
            near = swap_mp(jnp.stack([share, far]), 1)
            return jnp.stack([far, near[0], near[1]])

        far_a = swap_mp(share_a, 2)
        far_a, share_f = tie(far_a, share_f)
        line_a = line_of(share_a, far_a)
        far_f = swap_mp(share_f, 2)
        line_a, far_f, rows_one, rows_two = tie(line_a, far_f, rows_one, rows_two)
        near_a = plane_gather(line_a[:, :piece], dp_size)
        rows_one, rows_two = to_rows(rows_one, rows_two, dp_size)
        near_f = swap_mp(jnp.stack([share_f, far_f]), 1)
        line_f = jnp.stack([far_f, near_f[0], near_f[1]], axis=1)
        got = line_a[:, piece : piece + vector_rows.shape[0]].astype(F32).reshape(3, 2, -1)
        vectors = jnp.concatenate([vectors[None], got[:, 0] + got[:, 1]])
        q_width = qv_bias.shape[1]
        q_bias = vectors[:, :q_width].reshape(1, -1)
        v_bias = vectors[:, q_width : 2 * q_width].reshape(1, -1)

        def turn(values, axes):
            for axis, bit in zip(axes, (core, spot // 2, spot % 2)):
                values = jnp.where(bit == 1, jnp.flip(values, axis), values)
            return values

        hidden_bias = turn(vectors[:, 2 * q_width :].reshape(4, 2, 2, 2, piece), (1, 2, 3))
        hidden_bias = hidden_bias.transpose(1, 2, 3, 0, 4).reshape(4, 1, width)

        local_rows = local_attention.reshape(4, 2, piece, width)
        rows_one, rows_two, line_f, near_a, local_rows, local_up, grads_one, grads_two, hidden_bias, q_bias = tie(
            rows_one, rows_two, line_f, near_a, local_rows, local_up, grads_one, grads_two, hidden_bias, q_bias
        )
        other_a = across(near_a, 1)
        xs = across(line_f, 2)
        ys = across(line_f, 4)
        grads_one, grads_two = to_rows(grads_one, grads_two, dp_size)

        quarters = rows_one[strip + 1 : strip + 3, : 2 * strip].astype(jnp.int32).reshape(4, strip)

        def quarter(at):
            return lax.dynamic_index_in_dim(quarters, at, 0, keepdims=False)

        own_segments = jnp.concatenate([quarter(2 * core + parity), quarter(2 * core + 1 - parity)])
        far_segments = jnp.concatenate([quarter(2 - 2 * core + parity), quarter(3 - 2 * core - parity)])
        seg_q = own_segments[None, :]
        seg_k = jnp.concatenate([own_segments, far_segments])[None, :]

        normed_one, queries, own_kv, weights = project(
            place,
            rows_one,
            rows_two,
            row(first_gain),
            row(first_shift),
            local_rows,
            near_a,
            other_a,
            q_bias,
            v_bias,
        )
        flat_weights = weights.reshape(-1, width)
        xs, ys, own_kv, line_f, seg_q, seg_k, grads_one, grads_two = tie(
            xs, ys, own_kv, line_f, seg_q, seg_k, grads_one, grads_two
        )
        grads_in = (grads_one, grads_two)
        far_kv = across(own_kv, 1)
        du = across(xs[0], 4)
        dd = across(ys[1], 2)
        line_far = across(line_f, 1)
        xs_far = across(xs, 1)
        ys_far = across(ys, 1)
        far_kv, line_far, xs_far, ys_far = tie(far_kv, line_far, xs_far, ys_far)
        heads = (queries, own_kv, far_kv)
        context, log_total, mid_rows, normed_two = attend(
            *heads,
            seg_q,
            seg_k,
            flat_weights,
            rows_one,
            rows_two,
            row(out_bias),
            row(second_gain),
            row(second_shift),
        )
        du, dd, normed_two = tie(du, dd, normed_two)
        du_far = across(du, 1)
        dd_far = across(dd, 1)
        local_up = local_up.reshape(8, piece, width)
        local_down = down_weight.reshape(8, piece, width)
        both = (line_f, line_far, xs, xs_far, ys, ys_far, du, du_far, dd, dd_far)
        active, slope, final_rows = expand(
            place, normed_two, mid_rows, hidden_bias, local_up, local_down, both, row(down_bias)
        )

        back_one, back_two = from_rows(final_rows[:strip], final_rows[strip:], dp_size)
        up_other, down_other, normed_grad, bias_other = expand_back(
            1, place, grads_in, normed_two, active, slope, local_up, local_down, both[1::2], None
        )
        up_got = across(up_other, 1)
        down_got = across(down_other, 1)
        up_own, down_own, normed_grad, bias_own = expand_back(
            0, place, grads_in, normed_two, active, slope, local_up, local_down, both[0::2], normed_grad
        )
        up_got, down_got, normed_grad = tie(up_got, down_got, normed_grad)
        up_sent = add(up_own[1], up_got[1])
        down_sent = add(down_own[1], down_got[1])
        up_sent, down_sent, normed_grad = tie(up_sent, down_sent, normed_grad)
        up_sent = across(up_sent, 4)
        down_sent = across(down_sent, 2)
        grad_mid, grad_attn, grad_context, sums_two = settle(
            normed_grad, mid_rows, grads_in, row(second_gain), flat_weights
        )
        inputs = heads + (grad_context, context, log_total, seg_q, seg_k)
        dq, own_grad, far_grad = attend_back(*inputs)
        up_sent, down_sent, far_grad, back_one, back_two = tie(up_sent, down_sent, far_grad, back_one, back_two)
        got_kv = across(far_grad, 1)
        up_second, down_second = onward((up_own, up_got, up_sent), (down_own, down_got, down_sent))
        up_second, down_second, got_kv, grad_mid = tie(up_second, down_second, got_kv, grad_mid)
        up_second = across(up_second, 2)
        down_second = across(down_second, 4)
        attention_other = weigh(1, place, dq, own_grad, got_kv, context, normed_one, grad_attn, None)
        attention_got = across(attention_other, 1)
        attention_other, grad_mid = tie(attention_other, grad_mid)
        out_one, out_two, small = finish(
            place,
            dq,
            own_grad,
            got_kv,
            weights,
            rows_one,
            rows_two,
            row(first_gain),
            grad_mid,
            sums_two,
        )
        back_routes = [[(target, source) for source, target in route] for route in row_routes(dp_size)]
        out_one, out_two, attention_got = tie(out_one, out_two, attention_got)
        start_one = lax.ppermute(out_one, BOTH, back_routes[0])
        attention_grad = weigh(0, place, dq, own_grad, got_kv, context, normed_one, grad_attn, attention_got)
        attention_grad, start_one, up_second, down_second, out_two, small = tie(
            attention_grad, start_one, up_second, down_second, out_two, small
        )
        attention_grad = plane_scatter(attention_grad, dp_size)
        pair, pair_sent = merge((up_own, up_got, up_sent, up_second), (down_own, down_got, down_sent, down_second))
        pair_sent, small, bias_own, bias_other = tie(pair_sent, small, bias_own, bias_other)
        small = tally(place, small, bias_own, bias_other)
        small = small + across(small, 1)
        small_got = swap_mp(small, 1)
        pair_sent = swap_mp(pair_sent, 1)
        pair_sent, small_got = tie(pair_sent, small_got)

        bits = [1 << n for n in range(dp_size.bit_length() - 1)]
        small = small + small_got
        pair = add(pair, pair_sent)
        pair_sent = swap_mp(pair[1], 2)
        small_far = swap_mp(small, 2)
        attention_grad, small_far = tie(attention_grad, small_far)
        small = small + small_far
        activations = jnp.where(
            parity == 0, jnp.stack([back_one, back_two]), jnp.stack([back_two, back_one])
        )

        def lift(value):
            for bit in bits[3:]:
                value = value + across(value, bit)
            return value

        small = lift(small)
        attention_sent = swap_mp(attention_grad[2:], 1)
        pair, pair_sent, activations, _ = tie(pair, pair_sent, activations, attention_sent)
        if dp_size > 8:
            pair_sent = lift(add(pair[0], pair_sent))
            pair = jnp.zeros_like(pair)
        pair = plane_gather(pack(pair, pair_sent, small), dp_size)
        attention_sent, out_two = tie(attention_sent, out_two)
        half = strip // 2
        start_two = jnp.concatenate(
            [
                lax.ppermute(out_two[:half], BOTH, back_routes[1]),
                lax.ppermute(out_two[half:], BOTH, back_routes[1]),
            ],
            axis=0,
        )
        attention_grad = add(attention_grad[:2], attention_sent)
        attention_sent = swap_mp(attention_grad[1], 2)
        attention_sent, pair, start_two = tie(attention_sent, pair, start_two)
        grad_start = jnp.where(
            parity == 0, jnp.stack([start_one, start_two]), jnp.stack([start_two, start_one])
        )
        tokens_grad = jnp.where((mask_flags == 1)[:, :, None], 0.0, grad_start.astype(F32))
        attention_grad = lift(add(attention_grad[0], attention_sent))
        attention_grad = plane_gather(attention_grad, dp_size)
        up_weight_grad, down_weight_grad, small, up_bias_grad, qv_bias_grad = close_pair(place, pair, across(pair, 1))
        attention_grad, up_weight_grad, down_weight_grad, small, tokens_grad = tie(
            attention_grad, up_weight_grad, down_weight_grad, small, tokens_grad
        )
        w_qkv_grad, w_out_grad = close_attention(place, attention_grad, across(attention_grad, 1))
        w_qkv_grad = w_qkv_grad.transpose(0, 2, 1)
        up_bias_grad = up_bias_grad.reshape(-1)
        return (
            activations,
            tokens_grad,
            small[0],
            small[1],
            small[2],
            w_qkv_grad,
            qv_bias_grad,
            w_out_grad,
            small[3],
            small[4],
            small[5],
            up_weight_grad,
            up_bias_grad,
            down_weight_grad,
            small[6],
        )

    return body


def solution(mesh):
    in_specs = (
        P("dp", "mp", None),
        P("dp", None),
        P("dp", "mp"),
        P(),
        P(),
        P(),
        P(None, None, "mp"),
        P(None, "mp"),
        P("mp", None),
        P(),
        P(),
        P(),
        P(None, "mp"),
        P("mp"),
        P("mp", None),
        P(),
        P("dp", "mp", None),
    )
    out_specs = (
        P("dp", "mp", None),
        P("dp", "mp", None),
        P(),
        P(),
        P(),
        P(None, None, "mp"),
        P(None, "mp"),
        P("mp", None),
        P(),
        P(),
        P(),
        P(None, "mp"),
        P("mp"),
        P("mp", None),
        P(),
    )
    return jax.shard_map(
        make_body(mesh.shape["dp"]), mesh=mesh, in_specs=in_specs, out_specs=out_specs, check_vma=False
    )
```

```python
import jax
import jax.numpy as jnp
from jax import lax
from jax.experimental import pallas as pl
from jax.experimental.pallas import tpu as pltpu
from jax.sharding import PartitionSpec as P

HD = 64
EPSILON = 1e-06
NEG_FILL = -1e30
BF = jnp.bfloat16
F32 = jnp.float32
BOTH = ("dp", "mp")
BLOCK_ORDER = (0, 2, 1, 3)
NT = (((1,), (1,)), ((), ()))
NN = (((1,), (0,)), ((), ()))
TN = (((0,), (0,)), ((), ()))


def dot(left, right, dims):
    return lax.dot_general(left, right, dims, preferred_element_type=F32)


def swap_dp(value, bit, dp_size):
    return lax.ppermute(value, "dp", [(i, i ^ bit) for i in range(dp_size)])


def swap_mp(value, bit):
    return lax.ppermute(value, "mp", [(i, i ^ bit) for i in range(4)])


def row_routes(dp_size):
    first, second = [], []
    for pair in range(dp_size // 2):
        for core in range(2):
            for place in range(4):
                source = (2 * pair + core) * 4 + place
                for row in range(2):
                    target = (2 * pair + place // 2) * 4 + 2 * core + row
                    (first if row == place % 2 else second).append((source, target))
    return first, second


def to_rows(first, second, dp_size):
    routes = row_routes(dp_size)
    return (lax.ppermute(first, BOTH, routes[0]), lax.ppermute(second, BOTH, routes[1]))


def from_rows(first, second, dp_size):
    back = [[(target, source) for source, target in route] for route in row_routes(dp_size)]
    return (lax.ppermute(first, BOTH, back[0]), lax.ppermute(second, BOTH, back[1]))


EXTRA = 16
MIB_ATTEND = 18
COST = pl.CostEstimate(flops=1000000, transcendentals=0, bytes_accessed=1000)


def plane_groups(dp_size):
    return [[base * 8 + core + 2 * k for k in range(4)] for base in range(dp_size // 8) for core in range(2)]


def plane_gather(value, dp_size):
    spread = jnp.broadcast_to(value[None], (4,) + value.shape)
    return lax.all_to_all(spread, "dp", 0, 0, tiled=True, axis_index_groups=plane_groups(dp_size))


def plane_scatter(value, dp_size):
    pieces = lax.all_to_all(value, "dp", 0, 0, tiled=True, axis_index_groups=plane_groups(dp_size))
    return jnp.sum(pieces.astype(F32), axis=0).astype(BF)


def tie(*values):
    return lax.optimization_barrier(values)


def add(left, right):
    return (left.astype(F32) + right.astype(F32)).astype(BF)


def whole(value):
    rank = value.ndim
    return pl.BlockSpec(value.shape, lambda *i: (0,) * rank, pipeline_mode=pl.Buffered(1))


def scalars():
    return pl.BlockSpec(memory_space=pltpu.SMEM)


def call(kernel, name, mib, grid, in_specs, out_specs, out_shape, scratch, flops, moved, args):
    return pl.pallas_call(
        kernel,
        grid=grid,
        in_specs=in_specs,
        out_specs=out_specs,
        out_shape=out_shape,
        scratch_shapes=scratch,
        compiler_params=pltpu.CompilerParams(vmem_limit_bytes=mib << 20),
        cost_estimate=COST,
        name=name,
    )(*args)


def centre(rows):
    row_mean = jnp.mean(rows, axis=-1, keepdims=True)
    centred = rows - row_mean
    variance = jnp.mean(centred * centred, axis=-1, keepdims=True)
    inv_scale = lax.rsqrt(variance + EPSILON)
    return (centred * inv_scale, inv_scale)


def centre_back(incoming, unit_rows, inv_scale, gain):
    scaled = incoming * gain
    inner_one = jnp.mean(scaled, axis=-1, keepdims=True)
    inner_two = jnp.mean(scaled * unit_rows, axis=-1, keepdims=True)
    return inv_scale * (scaled - inner_one - unit_rows * inner_two)


def project_kernel(place, one, two, gain, shift, local, near, other, q_bias, v_bias, normed, q, kv, weights):
    strip = normed.shape[0] // 2
    for i, rows in enumerate((one, two)):
        unit, _ = centre(rows[:strip].astype(F32))
        normed[i * strip : (i + 1) * strip] = (unit * gain[...] + shift[...]).astype(BF)
    core = place[0]
    weights[:, 0] = local[...]
    for k in range(4):
        weights[2 * core + k // 2, 1:4, k % 2] = near[k]
        weights[2 - 2 * core + k // 2, 1:4, k % 2] = other[k]
    width = one.shape[1]
    rows = normed[...]
    q[...] = (dot(rows, weights[0].reshape(width, width), NT) + q_bias[...]).astype(BF)
    kv[0] = dot(rows, weights[1].reshape(width, width), NT).astype(BF)
    kv[1] = (dot(rows, weights[2].reshape(width, width), NT) + v_bias[...]).astype(BF)


def project(place, one, two, gain, shift, local, near, other, q_bias, v_bias):
    width = one.shape[1]
    tokens = 2 * (one.shape[0] - EXTRA)
    args = (place, one, two, gain, shift, local, near, other, q_bias, v_bias)
    shapes = [
        jax.ShapeDtypeStruct((tokens, width), BF),
        jax.ShapeDtypeStruct((tokens, width), BF),
        jax.ShapeDtypeStruct((2, tokens, width), BF),
        jax.ShapeDtypeStruct((4, 4, 2, width // 8, width), BF),
    ]
    return call(
        project_kernel,
        "project",
        15,
        (1,),
        [scalars()] + [whole(x) for x in args[1:]],
        [whole(x) for x in shapes],
        shapes,
        [],
        6 * tokens * width * width,
        12 * width * width,
        args,
    )


def spare_base(head):
    return 0 if head else HD


def head_lanes(shape, head):
    lanes = lax.broadcasted_iota(jnp.int32, shape, 1)
    return (lanes >= HD) if head else (lanes < HD)


def upright(line):
    return jnp.broadcast_to(line, (128, line.shape[1])).T


def prepare_lanes(segk_ref, segq_ref, key_extra, query_extra):
    for segments, extra, is_key in ((segk_ref, key_extra, True), (segq_ref, query_extra, False)):
        ids = upright(segments[...])
        for head in range(2):
            lanes = lax.broadcasted_iota(jnp.int32, ids.shape, 1) - spare_base(head)
            inside = (lanes >= 0) & (lanes < 4)
            if is_key:
                values = jnp.where(inside & (ids != lanes), NEG_FILL, 0.0)
            else:
                values = jnp.where(inside & (ids == lanes), 1.0, 0.0)
            extra[head] = values.astype(BF)


def attend_kernel(
    q_ref, own_ref, far_ref, segq_ref, segk_ref, weights, one, two, o_bias, gain, shift,
    ctx_ref, lse_ref, mid_ref, normed_ref, keys, values_t, key_extra, query_extra, total,
):
    half = own_ref.shape[1]
    step = pl.program_id(0)

    @pl.when(step == 0)
    def _():
        prepare_lanes(segk_ref, segq_ref, key_extra, query_extra)
        for head in range(2):
            values_t[head, HD:] = jnp.ones_like(values_t[head, HD:])

    for i, ref in enumerate((own_ref, far_ref)):
        span = slice(i * half, (i + 1) * half)
        part = ref[0]
        turned = ref[1].T
        for head in range(2):
            keys[head, span] = jnp.where(head_lanes(part.shape, head), part, key_extra[head, span])
            values_t[head, :HD, span] = turned[head * HD : (head + 1) * HD]
    tokens = q_ref.shape[0]
    block = tokens
    for start in range(0, tokens, block):
        span = slice(start, start + block)
        query = q_ref[span, :] * jnp.asarray(HD**-0.5, BF)
        heads = range(2)
        owns = [jnp.where(head_lanes(query.shape, h), query, query_extra[h, span]) for h in heads]
        scores = [dot(keys[h], owns[h], NT) for h in heads]
        maxima = [jnp.max(v, axis=0, keepdims=True) for v in scores]
        powers = [jnp.exp(v - m).astype(BF) for v, m in zip(scores, maxima)]
        parts = [dot(values_t[h], powers[h], NN) for h in heads]
        pieces = [v[:HD] / v[HD : HD + 1] for v in parts]
        sums = [m + jnp.log(v[HD : HD + 1]) for m, v in zip(maxima, parts)]
        context = jnp.concatenate(pieces, axis=0).T.astype(BF)
        ctx_ref[span, :] = context
        for h in heads:
            lse_ref[0, h : h + 1, span] = sums[h]
        mixed = dot(context, weights[...], NN)

        @pl.when(step == 0)
        def _():
            total[span, :] = mixed

        @pl.when(step > 0)
        def _():
            total[span, :] += mixed

    @pl.when(step == pl.num_programs(0) - 1)
    def _():
        strip = tokens // 2
        for i, rows in enumerate((one, two)):
            span = slice(i * strip, (i + 1) * strip)
            mid = rows[:strip].astype(F32) + total[span, :] + o_bias[...]
            mid_ref[span, :] = mid
            unit, _ = centre(mid)
            normed_ref[span, :] = (unit * gain[...] + shift[...]).astype(BF)


def attend(q, own, far, seg_q, seg_k, weights, one, two, o_bias, gain, shift):
    rows, width = q.shape
    pairs = width // 128
    half = own.shape[1]
    args = (q, own, far, seg_q, seg_k, weights, one, two, o_bias, gain, shift)
    head_block = pl.BlockSpec((rows, 128), lambda i: (0, i))
    key_block = pl.BlockSpec((2, half, 128), lambda i: (0, 0, i))
    shapes = [
        jax.ShapeDtypeStruct((rows, width), BF),
        jax.ShapeDtypeStruct((pairs, 2, rows), F32),
        jax.ShapeDtypeStruct((rows, width), F32),
        jax.ShapeDtypeStruct((rows, width), BF),
    ]
    specs = [head_block, key_block, key_block, whole(seg_q), whole(seg_k)]
    specs.append(pl.BlockSpec((128, width), lambda i: (3 * pairs + i, 0)))
    return call(
        attend_kernel,
        "attend",
        20,
        (pairs,),
        specs + [whole(x) for x in args[6:]],
        [head_block, pl.BlockSpec((1, 2, rows), lambda i: (i, 0, 0)), whole(shapes[2]), whole(shapes[3])],
        shapes,
        [
            pltpu.VMEM((2, 2 * half, 128), BF),
            pltpu.VMEM((2, HD + 16, 2 * half), BF),
            pltpu.VMEM((2, 2 * half, 128), BF),
            pltpu.VMEM((2, rows, 128), BF),
            pltpu.VMEM((rows, width), F32),
        ],
        0,
        0,
        args,
    )


def load_block(place, flip, at_y, mat, local, pieces, block):
    core = place[0] if not flip else 1 - place[0]
    line, along_x, along_y, diagonal = pieces
    for x in range(2):
        spot = place[1 + 2 * at_y + x]
        block[x, 0] = local[core * 4 + spot]
        if at_y and x:
            block[x, 1:4] = diagonal[...]
        else:
            block[x, 1:4] = (along_y if at_y else along_x if x else line)[mat]


def expand_kernel(
    place, normed, mid, bias, local_up, local_down, line, line_far, xs, xs_far, ys, ys_far, du, du_far, dd, dd_far,
    d_bias, active, slope, out, up, down, total,
):
    step = pl.program_id(0)
    for j in range(4):

        @pl.when(step == j)
        def _():
            flip = j // 2
            three = (line_far, xs_far, ys_far) if flip else (line, xs, ys)
            load_block(place, flip, j % 2, 0, local_up, three + ((du_far if flip else du),), up)
            load_block(place, flip, j % 2, 1, local_down, three + ((dd_far if flip else dd),), down)

    width = normed.shape[1]
    hidden = dot(normed[...], up[...].reshape(width, width), NT) + bias[0]
    cdf = 0.5 * (1.0 + lax.erf(hidden * (0.5**0.5)))
    pulled = cdf + hidden * jnp.exp(-0.5 * hidden * hidden) * 0.3989422804014327
    slope[...] = pulled.astype(BF)
    active[...] = (hidden * cdf).astype(BF)
    part = dot(active[...], down[...].reshape(width, width), NN)

    @pl.when(step == 0)
    def _():
        total[...] = mid[...] + d_bias[...] + part

    @pl.when((step > 0) & (step < 3))
    def _():
        total[...] += part

    @pl.when(step == 3)
    def _():
        out[...] = (total[...] + part).astype(BF)


def expand(place, normed, mid, bias, local_up, local_down, pieces, d_bias):
    tokens, width = normed.shape
    piece = width // 8
    args = (place, normed, mid, bias, local_up, local_down, *pieces, d_bias)
    hidden = pl.BlockSpec((tokens, width), lambda j: (0, j))
    shapes = [
        jax.ShapeDtypeStruct((tokens, 4 * width), BF),
        jax.ShapeDtypeStruct((tokens, 4 * width), BF),
        jax.ShapeDtypeStruct((tokens, width), BF),
    ]
    specs = [scalars()] + [whole(x) for x in args[1:]]
    specs[3] = pl.BlockSpec((1, 1, width), lambda j: (j, 0, 0))
    return call(
        expand_kernel,
        "expand",
        24,
        (4,),
        specs,
        [hidden, hidden, whole(shapes[2])],
        shapes,
        [pltpu.VMEM((2, 4, piece, width), BF)] * 2 + [pltpu.VMEM((tokens, width), F32)],
        16 * tokens * width * width,
        20 * width * width,
        args,
    )


def expand_back_kernel(
    flip, place, grad_one, grad_two, normed, active, slope, local_up, local_down, line, xs, ys, du, dd, before,
    up_grad, down_grad, normed_grad, bias_grad, up, down,
):
    step = pl.program_id(0)
    for j in range(2):

        @pl.when(step == j)
        def _():
            load_block(place, flip, j, 0, local_up, (line, xs, ys, du), up)
            load_block(place, flip, j, 1, local_down, (line, xs, ys, dd), down)

    width = normed.shape[1]
    wide = up.shape
    grad = jnp.concatenate([grad_one[...], grad_two[...]], axis=0)
    incoming = dot(grad, down[...].reshape(width, width), NT)
    grad_hidden = (incoming * slope[...].astype(F32)).astype(BF)
    bias_grad[0] = jnp.sum(grad_hidden.astype(F32), axis=0, keepdims=True)
    down_grad[...] = dot(active[...], grad, TN).astype(BF).reshape(2, 1, *wide[1:])
    up_grad[0] = dot(grad_hidden, normed[...], TN).astype(BF).reshape(wide)
    part = dot(grad_hidden, up[...].reshape(width, width), NN)

    @pl.when(step == 0)
    def _():
        if before is None:
            normed_grad[...] = part
        else:
            normed_grad[...] = before[...] + part

    @pl.when(step > 0)
    def _():
        normed_grad[...] += part


def expand_back(flip, place, grad, normed, active, slope, local_up, local_down, pieces, before):
    tokens, width = normed.shape
    piece = width // 8
    args = (place, *grad, normed, active, slope, local_up, local_down, *pieces)
    if before is not None:
        args = args + (before,)

    def kernel(*refs):
        if before is None:
            refs = refs[:13] + (None,) + refs[13:]
        return expand_back_kernel(flip, *refs)

    hidden = pl.BlockSpec((tokens, width), lambda j: (0, j + 2 * flip))
    shapes = [
        jax.ShapeDtypeStruct((2, 2, 4, piece, width), BF),
        jax.ShapeDtypeStruct((2, 2, 4, piece, width), BF),
        jax.ShapeDtypeStruct((tokens, width), F32),
        jax.ShapeDtypeStruct((2, 1, width), F32),
    ]
    specs = [scalars()] + [whole(x) for x in args[1:]]
    specs[4] = specs[5] = hidden
    return call(
        kernel,
        "expand_back_other" if flip else "expand_back_own",
        20,
        (2,),
        specs,
        [
            pl.BlockSpec((1, 2, 4, piece, width), lambda j: (j, 0, 0, 0, 0)),
            pl.BlockSpec((2, 1, 4, piece, width), lambda j: (0, j, 0, 0, 0)),
            whole(shapes[2]),
            pl.BlockSpec((1, 1, width), lambda j: (j, 0, 0)),
        ],
        shapes,
        [pltpu.VMEM((2, 4, piece, width), BF)] * 2,
        20 * tokens * width * width,
        16 * width * width,
        args,
    )


def settle_kernel(incoming, mid, grad_one, grad_two, gain, wo, grad_mid, grad_attn, grad_context, sums):
    strip = grad_one.shape[0]
    parts = None
    for at in range(0, mid.shape[0], strip):
        span = slice(at, at + strip)
        unit, inv_scale = centre(mid[span, :])
        given = incoming[span, :]
        outer = (grad_two if at else grad_one)[...].astype(F32)
        made = outer + centre_back(given, unit, inv_scale, gain[...])
        grad_mid[span, :] = made
        grad_attn[span, :] = made.astype(BF)
        grad_context[span, :] = dot(made.astype(BF), wo[...], NT).astype(BF)
        rows = [jnp.sum(v, axis=0, keepdims=True) for v in (made, given * unit, given, outer)]
        parts = rows if parts is None else [a + b for a, b in zip(parts, rows)]
    for i, row in enumerate(parts):
        sums[i : i + 1, :] = row


def settle(incoming, mid, grad, gain, weights):
    tokens, width = mid.shape
    args = (incoming, mid, *grad, gain, weights)
    specs = [whole(x) for x in args]
    specs[5] = pl.BlockSpec((width, width), lambda i: (3, 0))
    shapes = [
        jax.ShapeDtypeStruct((tokens, width), F32),
        jax.ShapeDtypeStruct((tokens, width), BF),
        jax.ShapeDtypeStruct((tokens, width), BF),
        jax.ShapeDtypeStruct((8, width), F32),
    ]
    return call(
        settle_kernel,
        "settle",
        13,
        (1,),
        specs,
        [whole(x) for x in shapes],
        shapes,
        [],
        2 * tokens * width * width,
        14 * tokens * width,
        args,
    )


def quarter_block(value, at):
    rank = value.ndim
    shape = (1,) * len(at) + value.shape[len(at) :]
    return pl.BlockSpec(shape, lambda *i: at + (0,) * (rank - len(at)), pipeline_mode=pl.Buffered(1))


def onward_kernel(*refs):
    for i in range(2):
        own, got, sent = (ref[...].astype(F32) for ref in refs[3 * i : 3 * i + 3])
        refs[6 + i][...] = (own[0, 0] + got[0, 0] + sent[0]).astype(BF)


def onward(up, down):
    args = up + down
    shape = jax.ShapeDtypeStruct(up[0].shape[2:], BF)
    return call(
        onward_kernel,
        "onward",
        12,
        (1,),
        [quarter_block(x, (0, 1) if x.ndim == 5 else (1,)) for x in args],
        [whole(shape)] * 2,
        [shape] * 2,
        [],
        0,
        0,
        args,
    )


def merge_kernel(*refs):
    kept, passed = refs[8:]
    for i in range(2):
        own, got, sent, second = refs[4 * i : 4 * i + 4]
        for part, out in ((slice(0, 2), kept), (slice(2, 4), passed)):
            total = own[0, 0, part].astype(F32) + got[0, 0, part].astype(F32)
            total = total + sent[0, part].astype(F32) + second[part].astype(F32)
            out[:, i] = total.astype(BF)


def merge(up, down):
    args = up + down
    shapes = [jax.ShapeDtypeStruct((2, 2) + up[0].shape[3:], BF)] * 2
    specs = [
        quarter_block(x, (0, 0)) if x.ndim == 5 else quarter_block(x, (0,)) if x.ndim == 4 else whole(x) for x in args
    ]
    return call(merge_kernel, "merge", 60, (1,), specs, [whole(x) for x in shapes], shapes, [], 0, 0, args)


def close_pair_kernel(place, near, other, up_grad, down_grad, vectors, up_bias, qv_bias):
    width = near.shape[2]
    piece = width // 8
    for c in range(2):
        for ref, core in ((near, place[0]), (other, 1 - place[0])):

            @pl.when(core == c)
            def _():
                for k in range(4):
                    at = (4 * c + k) * piece
                    down_grad[at : at + piece, :] = ref[k, piece : 2 * piece].astype(F32)
                rows = jnp.concatenate([ref[k, :piece] for k in range(4)], axis=0)
                up_grad[:, 4 * c * piece : 4 * (c + 1) * piece] = rows.astype(F32).T

    total = None
    for k in range(4):
        for at in (2 * piece, 2 * piece + EXTRA):
            part = near[k, at : at + EXTRA].astype(F32)
            total = part if total is None else total + part
    vectors[...] = total[:8]

    def slot(entry):
        r, g = 7 + entry // 6, entry % 6
        return total[r : r + 1, 128 * g : 128 * g + piece]

    for z in range(4):

        @pl.when(place[5] == z)
        def _():
            for k in range(8):
                up_bias[:, k * piece : (k + 1) * piece] = slot(8 * z + k)
            for i in range(2):
                for half in range(2):
                    qv_bias[i : i + 1, half * piece : (half + 1) * piece] = slot(32 + 8 * i + 2 * z + half)


def close_pair(place, near, other):
    width = near.shape[2]
    args = (place, near, other)
    shapes = [
        jax.ShapeDtypeStruct((width, width), F32),
        jax.ShapeDtypeStruct((width, width), F32),
        jax.ShapeDtypeStruct((8, width), F32),
        jax.ShapeDtypeStruct((1, width), F32),
        jax.ShapeDtypeStruct((2, width // 4), F32),
    ]
    return call(
        close_pair_kernel,
        "close_pair",
        12,
        (1,),
        [scalars(), whole(near), whole(other)],
        [whole(x) for x in shapes],
        shapes,
        [],
        0,
        0,
        args,
    )


def close_attention_kernel(place, near, other, qkv_grad, out_grad):
    piece = near.shape[1]
    for c in range(2):
        for ref, core in ((near, place[0]), (other, 1 - place[0])):

            @pl.when(core == c)
            def _():
                for k in range(4):
                    span = slice(k % 2 * piece, (k % 2 + 1) * piece)
                    part = ref[k].astype(F32)
                    if 2 * c + k // 2 < 3:
                        qkv_grad[2 * c + k // 2, span, :] = part
                    else:
                        out_grad[span, :] = part


def close_attention(place, near, other):
    piece, width = near.shape[1:]
    args = (place, near, other)
    shapes = [
        jax.ShapeDtypeStruct((3, 2 * piece, width), F32),
        jax.ShapeDtypeStruct((2 * piece, width), F32),
    ]
    return call(
        close_attention_kernel,
        "close_attention",
        6,
        (1,),
        [scalars(), whole(near), whole(other)],
        [whole(x) for x in shapes],
        shapes,
        [],
        0,
        0,
        args,
    )


def flip_kernel(value, out):
    out[...] = value[...].T


def flip(value):
    shape = jax.ShapeDtypeStruct(value.shape[::-1], value.dtype)
    return call(flip_kernel, "flip", 4, (1,), [whole(value)], whole(shape), shape, [], 0, 0, (value,))


def weigh_kernel(flip, place, dq, mine, got, context, normed, grad, before, out, left, right):
    core = place[0] if not flip else 1 - place[0]
    width = dq.shape[1]
    piece = width // 8

    @pl.when(core == 0)
    def _():
        left[0] = dq[...]
        left[1] = (mine[0].astype(F32) + got[0].astype(F32)).astype(BF)
        right[...] = normed[...]

    @pl.when(core == 1)
    def _():
        left[0] = (mine[1].astype(F32) + got[1].astype(F32)).astype(BF)
        left[1] = context[...]
        right[...] = grad[...]

    for i in range(2):
        rows = normed[...] if i == 0 else right[...]
        made = dot(left[i], rows, TN).reshape(4, 2, piece, width)
        for k in range(2):
            part = made[:, k]
            if before is not None:
                part = part + before[2 * i + k].astype(F32)
            out[2 * i + k] = part.astype(BF)


def weigh(flip, place, dq, mine, got, context, normed, grad, before):
    tokens, width = dq.shape
    args = (place, dq, mine, got, context, normed, grad)
    if before is not None:
        args = args + (before,)

    def kernel(*refs):
        if before is None:
            refs = refs[:7] + (None,) + refs[7:]
        return weigh_kernel(flip, *refs)

    shape = jax.ShapeDtypeStruct((4, 4, width // 8, width), BF)
    return call(
        kernel,
        "weigh_other" if flip else "weigh_own",
        13,
        (1,),
        [scalars()] + [whole(x) for x in args[1:]],
        whole(shape),
        shape,
        [pltpu.VMEM((2, tokens, width), BF), pltpu.VMEM((tokens, width), BF)],
        4 * tokens * width * width,
        8 * width * width,
        args,
    )


def finish_kernel(
    place, dq, mine, got, weights, one, two, gain, grad_mid, sums_two,
    out_one, out_two, small, total,
):
    width = dq.shape[1]
    keys = (mine[0].astype(F32) + got[0].astype(F32)).astype(BF)
    values = (mine[1].astype(F32) + got[1].astype(F32)).astype(BF)
    total[...] = dot(dq[...], weights[0].reshape(width, width), NN)
    total[...] += dot(keys, weights[1].reshape(width, width), NN)
    total[...] += dot(values, weights[2].reshape(width, width), NN)
    strip = dq.shape[0] // 2
    gathered = None
    for i, rows in enumerate((one, two)):
        span = slice(i * strip, (i + 1) * strip)
        unit, inv_scale = centre(rows[:strip].astype(F32))
        incoming = total[span, :]
        grad_start = grad_mid[span, :] + centre_back(incoming, unit, inv_scale, gain[...])
        high = grad_start.astype(BF)
        (out_two if i else out_one)[...] = high
        low = (grad_start - high.astype(F32)).astype(BF)
        flags = rows[strip : strip + 16, :strip]
        masked = (dot(flags, high, NN) + dot(flags, low, NN))[:1]
        parts = [masked] + [jnp.sum(v, axis=0, keepdims=True) for v in (incoming * unit, incoming)]
        gathered = parts if gathered is None else [a + b for a, b in zip(gathered, parts)]
    small[...] = jnp.zeros_like(small)
    gathered += [sums_two[i : i + 1, :] for i in range(4)]
    for r, line in enumerate(gathered):
        for g in range(width // 128):
            small[16 * g + r : 16 * g + r + 1, :] = line[:, 128 * g : 128 * g + 128]
    piece = width // 8
    for i, value in enumerate((dq[...], values)):
        line = jnp.sum(value.astype(F32), axis=0, keepdims=True)
        for j, distance in enumerate(BLOCK_ORDER):
            for half in range(2):
                entry = 32 + 8 * i + place[5 + distance] * 2 + half
                at = 16 * lax.rem(entry, 6) + 7 + entry // 6
                span = slice((2 * j + half) * piece, (2 * j + half + 1) * piece)
                small[pl.ds(at, 1), :piece] = line[:, span]


def finish(place, dq, mine, got, weights, one, two, gain, grad_mid, sums_two):
    tokens, width = dq.shape
    args = (place, dq, mine, got, weights, one, two, gain, grad_mid, sums_two)
    specs = [scalars()] + [whole(x) for x in args[1:]]
    specs[4] = pl.BlockSpec((3,) + weights.shape[1:], lambda i: (0,) * 5, pipeline_mode=pl.Buffered(1))
    shapes = [
        jax.ShapeDtypeStruct((tokens // 2, width), BF),
        jax.ShapeDtypeStruct((tokens // 2, width), BF),
        jax.ShapeDtypeStruct((96, 128), F32),
    ]
    return call(
        finish_kernel,
        "finish",
        14,
        (1,),
        specs,
        [whole(x) for x in shapes],
        shapes,
        [pltpu.VMEM((tokens, width), F32)],
        0,
        0,
        args,
    )


def tally_kernel(place, table, own, other, out):
    out[...] = table[...]
    width = own.shape[2]
    piece = width // 8
    for flip, sums in enumerate((own, other)):
        core = place[0] if not flip else 1 - place[0]
        for y in range(2):
            line = sums[y]
            for x in range(2):
                spot = place[1 + 2 * y + x]
                for i, distance in enumerate(BLOCK_ORDER):
                    entry = place[5 + distance] * 8 + core * 4 + spot
                    at = 16 * lax.rem(entry, 6) + 7 + entry // 6
                    span = slice((4 * x + i) * piece, (4 * x + i + 1) * piece)
                    out[pl.ds(at, 1), :piece] = line[:, span]


def tally(place, table, own, other):
    args = (place, table, own, other)
    shape = jax.ShapeDtypeStruct(table.shape, F32)
    specs = [scalars()] + [whole(x) for x in args[1:]]
    return call(tally_kernel, "tally", 4, (1,), specs, whole(shape), shape, [], 0, 0, args)


def pack_kernel(kept, got, small, out):
    piece, width = kept.shape[2:]
    for i in range(2):
        out[i * piece : (i + 1) * piece, :] = (kept[0, i].astype(F32) + got[i].astype(F32)).astype(BF)
    for g in range(width // 128):
        lanes = slice(128 * g, 128 * g + 128)
        value = small[16 * g : 16 * g + 16, :]
        high = value.astype(BF)
        out[2 * piece : 2 * piece + 16, lanes] = high
        out[2 * piece + 16 :, lanes] = (value - high.astype(F32)).astype(BF)


def pack(kept, got, small):
    piece, width = kept.shape[2:]
    args = (kept, got, small)
    shape = jax.ShapeDtypeStruct((2 * piece + 32, width), BF)
    specs = [quarter_block(kept, (0,)), whole(got), whole(small)]
    return call(pack_kernel, "pack", 4, (1,), specs, whole(shape), shape, [], 0, 0, args)


def attend_back_kernel(
    q_ref,
    own_ref,
    far_ref,
    g_ref,
    ctx_ref,
    lse_ref,
    segq_ref,
    segk_ref,
    dq_ref,
    own_grad_ref,
    far_grad_ref,
    keys,
    keys_t,
    values,
    dk_total,
    dv_total,
    key_ids,
):
    half = own_ref.shape[1]

    @pl.when(pl.program_id(0) == 0)
    def _():
        key_ids[...] = upright(segk_ref[...])

    keys[:half] = own_ref[0]
    keys[half:] = far_ref[0]
    keys_t[:, :half] = own_ref[0].T
    keys_t[:, half:] = far_ref[0].T
    values[:half] = own_ref[1]
    values[half:] = far_ref[1]
    total = q_ref.shape[0]
    block = 256
    scale = jnp.asarray(HD**-0.5, BF)
    for start in range(0, total, block):
        span = slice(start, start + block)
        same = key_ids[:, 0:1] == segq_ref[:, span]
        query = q_ref[span, :] * scale
        grad = g_ref[span, :]
        product = (grad.astype(F32) * ctx_ref[span, :].astype(F32)).T
        lanes = lax.broadcasted_iota(jnp.int32, query.shape, 1)
        pieces = []
        for head in range(2):
            own = (lanes >= HD) if head else (lanes < HD)
            query_own = jnp.where(own, query, jnp.zeros_like(query))
            grad_own = jnp.where(own, grad, jnp.zeros_like(grad))
            scores = dot(keys[...], query_own, NT)
            probs = jnp.exp(jnp.where(same, scores, NEG_FILL) - lse_ref[0, head : head + 1, span])
            grad_probs = dot(values[...], grad_own, NT)
            row_dot = jnp.sum(product[head * HD : (head + 1) * HD, :], axis=0, keepdims=True)
            grad_scores = (probs * (grad_probs - row_dot)).astype(BF)
            dv = dot(probs.astype(BF), grad_own, NN)
            dk = dot(grad_scores, query_own, NN)
            if start == 0 and head == 0:
                dv_total[...] = dv
                dk_total[...] = dk
            else:
                dv_total[...] += dv
                dk_total[...] += dk
            pieces.append(dot(keys_t[head * HD : (head + 1) * HD, :], grad_scores, NN))
        dq_ref[span, :] = (jnp.concatenate(pieces, axis=0).T * HD**-0.5).astype(BF)
    own_grad_ref[0] = dk_total[:half].astype(BF)
    far_grad_ref[0] = dk_total[half:].astype(BF)
    own_grad_ref[1] = dv_total[:half].astype(BF)
    far_grad_ref[1] = dv_total[half:].astype(BF)


def attend_back(q, own, far, grad, ctx, lse, seg_q, seg_k):
    rows, width = q.shape
    pairs = width // 128
    half = own.shape[1]
    args = (q, own, far, grad, ctx, lse, seg_q, seg_k)
    head_block = pl.BlockSpec((rows, 128), lambda i: (0, i))
    key_block = pl.BlockSpec((2, half, 128), lambda i: (0, 0, i))
    lse_block = pl.BlockSpec((1, 2, rows), lambda i: (i, 0, 0))
    shapes = [jax.ShapeDtypeStruct((rows, width), BF)] + [jax.ShapeDtypeStruct((2, half, width), BF)] * 2
    return call(
        attend_back_kernel,
        "attend_back",
        13,
        (pairs,),
        [head_block, key_block, key_block, head_block, head_block, lse_block, whole(seg_q), whole(seg_k)],
        [head_block, key_block, key_block],
        shapes,
        [
            pltpu.VMEM((2 * half, 128), BF),
            pltpu.VMEM((128, 2 * half), BF),
            pltpu.VMEM((2 * half, 128), BF),
            pltpu.VMEM((2 * half, 128), F32),
            pltpu.VMEM((2 * half, 128), F32),
            pltpu.VMEM((2 * half, 128), jnp.int32),
        ],
        0,
        0,
        args,
    )


def make_body(dp_size):
    def body(
        tokens,
        segment_ids,
        mask_flags,
        mask_embed,
        first_gain,
        first_shift,
        query_key_value_weight,
        qv_bias,
        output_weight,
        out_bias,
        second_gain,
        second_shift,
        up_weight,
        expand_bias,
        down_weight,
        down_bias,
        out_grad,
    ):
        dp_at = lax.axis_index("dp")
        mp_at = lax.axis_index("mp")
        core = dp_at % 2
        spot = (dp_at // 2) % 4
        parity = mp_at % 2
        width = tokens.shape[2]
        strip = tokens.shape[1]
        piece = width // 8
        place = jnp.stack([core] + [spot ^ r for r in range(4)] + [mp_at ^ d for d in range(4)]).astype(jnp.int32)

        def across(value, bit):
            return swap_dp(value, bit, dp_size)

        def pick(values):
            return (
                lax.dynamic_index_in_dim(values, parity, 0, keepdims=False),
                lax.dynamic_index_in_dim(values, 1 - parity, 0, keepdims=False),
            )

        def row(vector):
            return vector.reshape(1, -1)

        local_attention = jnp.concatenate(
            [query_key_value_weight.transpose(0, 2, 1).reshape(-1, width), output_weight], axis=0
        )
        offset = (core * 4 + spot) * piece
        vectors = jnp.concatenate([qv_bias.reshape(-1), expand_bias])
        vector_high = vectors.astype(BF)
        vector_low = (vectors - vector_high.astype(F32)).astype(BF)
        vector_rows = jnp.concatenate([vector_high, vector_low]).reshape(-1, width)
        share_a = jnp.concatenate(
            [
                lax.dynamic_slice_in_dim(local_attention, offset, piece, 0),
                jnp.pad(vector_rows, ((0, EXTRA - vector_rows.shape[0]), (0, 0))),
            ],
            axis=0,
        )
        local_up = flip(up_weight)
        share_f = jnp.stack(
            [
                lax.dynamic_slice_in_dim(local_up, offset, piece, 0),
                lax.dynamic_slice_in_dim(down_weight, offset, piece, 0),
            ]
        )
        start_rows = jnp.where((mask_flags == 1)[:, :, None], mask_embed.astype(BF), tokens)
        flag_rows = jnp.pad(mask_flags.astype(BF)[:, None, :], ((0, 0), (0, 0), (0, width - strip)))
        segment_rows = segment_ids.astype(BF).reshape(segment_ids.shape[0], 2, -1)
        segment_rows = jnp.pad(segment_rows, ((0, 0), (0, EXTRA - 3), (0, width - segment_rows.shape[2])))
        messages = jnp.concatenate([start_rows, flag_rows, segment_rows], axis=1)
        rows_one, rows_two = pick(messages)
        grads_one, grads_two = pick(out_grad)

        def line_of(share, far):
            near = swap_mp(jnp.stack([share, far]), 1)
            return jnp.stack([far, near[0], near[1]])

        far_a = swap_mp(share_a, 2)
        far_a, share_f = tie(far_a, share_f)
        line_a = line_of(share_a, far_a)
        far_f = swap_mp(share_f, 2)
        line_a, far_f, rows_one, rows_two = tie(line_a, far_f, rows_one, rows_two)
        near_a = plane_gather(line_a[:, :piece], dp_size)
        rows_one, rows_two = to_rows(rows_one, rows_two, dp_size)
        near_f = swap_mp(jnp.stack([share_f, far_f]), 1)
        line_f = jnp.stack([far_f, near_f[0], near_f[1]], axis=1)
        got = line_a[:, piece : piece + vector_rows.shape[0]].astype(F32).reshape(3, 2, -1)
        vectors = jnp.concatenate([vectors[None], got[:, 0] + got[:, 1]])
        q_width = qv_bias.shape[1]
        q_bias = vectors[:, :q_width].reshape(1, -1)
        v_bias = vectors[:, q_width : 2 * q_width].reshape(1, -1)

        def turn(values, axes):
            for axis, bit in zip(axes, (core, spot // 2, spot % 2)):
                values = jnp.where(bit == 1, jnp.flip(values, axis), values)
            return values

        hidden_bias = turn(vectors[:, 2 * q_width :].reshape(4, 2, 2, 2, piece), (1, 2, 3))
        hidden_bias = hidden_bias.transpose(1, 2, 3, 0, 4).reshape(4, 1, width)

        local_rows = local_attention.reshape(4, 2, piece, width)
        rows_one, rows_two, line_f, near_a, local_rows, local_up, grads_one, grads_two, hidden_bias, q_bias = tie(
            rows_one, rows_two, line_f, near_a, local_rows, local_up, grads_one, grads_two, hidden_bias, q_bias
        )
        other_a = across(near_a, 1)
        xs = across(line_f, 2)
        ys = across(line_f, 4)
        grads_one, grads_two = to_rows(grads_one, grads_two, dp_size)

        quarters = rows_one[strip + 1 : strip + 3, : 2 * strip].astype(jnp.int32).reshape(4, strip)

        def quarter(at):
            return lax.dynamic_index_in_dim(quarters, at, 0, keepdims=False)

        own_segments = jnp.concatenate([quarter(2 * core + parity), quarter(2 * core + 1 - parity)])
        far_segments = jnp.concatenate([quarter(2 - 2 * core + parity), quarter(3 - 2 * core - parity)])
        seg_q = own_segments[None, :]
        seg_k = jnp.concatenate([own_segments, far_segments])[None, :]

        normed_one, queries, own_kv, weights = project(
            place,
            rows_one,
            rows_two,
            row(first_gain),
            row(first_shift),
            local_rows,
            near_a,
            other_a,
            q_bias,
            v_bias,
        )
        flat_weights = weights.reshape(-1, width)
        xs, ys, own_kv, line_f, seg_q, seg_k, grads_one, grads_two = tie(
            xs, ys, own_kv, line_f, seg_q, seg_k, grads_one, grads_two
        )
        grads_in = (grads_one, grads_two)
        far_kv = across(own_kv, 1)
        du = across(xs[0], 4)
        dd = across(ys[1], 2)
        line_far = across(line_f, 1)
        xs_far = across(xs, 1)
        ys_far = across(ys, 1)
        far_kv, line_far, xs_far, ys_far = tie(far_kv, line_far, xs_far, ys_far)
        heads = (queries, own_kv, far_kv)
        context, log_total, mid_rows, normed_two = attend(
            *heads,
            seg_q,
            seg_k,
            flat_weights,
            rows_one,
            rows_two,
            row(out_bias),
            row(second_gain),
            row(second_shift),
        )
        du, dd, normed_two = tie(du, dd, normed_two)
        du_far = across(du, 1)
        dd_far = across(dd, 1)
        local_up = local_up.reshape(8, piece, width)
        local_down = down_weight.reshape(8, piece, width)
        both = (line_f, line_far, xs, xs_far, ys, ys_far, du, du_far, dd, dd_far)
        active, slope, final_rows = expand(
            place, normed_two, mid_rows, hidden_bias, local_up, local_down, both, row(down_bias)
        )

        back_one, back_two = from_rows(final_rows[:strip], final_rows[strip:], dp_size)
        up_other, down_other, normed_grad, bias_other = expand_back(
            1, place, grads_in, normed_two, active, slope, local_up, local_down, both[1::2], None
        )
        up_got = across(up_other, 1)
        down_got = across(down_other, 1)
        up_own, down_own, normed_grad, bias_own = expand_back(
            0, place, grads_in, normed_two, active, slope, local_up, local_down, both[0::2], normed_grad
        )
        up_got, down_got, normed_grad = tie(up_got, down_got, normed_grad)
        up_sent = add(up_own[1], up_got[1])
        down_sent = add(down_own[1], down_got[1])
        up_sent, down_sent, normed_grad = tie(up_sent, down_sent, normed_grad)
        up_sent = across(up_sent, 4)
        down_sent = across(down_sent, 2)
        grad_mid, grad_attn, grad_context, sums_two = settle(
            normed_grad, mid_rows, grads_in, row(second_gain), flat_weights
        )
        inputs = heads + (grad_context, context, log_total, seg_q, seg_k)
        dq, own_grad, far_grad = attend_back(*inputs)
        up_sent, down_sent, far_grad, back_one, back_two = tie(up_sent, down_sent, far_grad, back_one, back_two)
        got_kv = across(far_grad, 1)
        up_second, down_second = onward((up_own, up_got, up_sent), (down_own, down_got, down_sent))
        up_second, down_second, got_kv, grad_mid = tie(up_second, down_second, got_kv, grad_mid)
        up_second = across(up_second, 2)
        down_second = across(down_second, 4)
        attention_other = weigh(1, place, dq, own_grad, got_kv, context, normed_one, grad_attn, None)
        attention_got = across(attention_other, 1)
        attention_other, grad_mid = tie(attention_other, grad_mid)
        out_one, out_two, small = finish(
            place,
            dq,
            own_grad,
            got_kv,
            weights,
            rows_one,
            rows_two,
            row(first_gain),
            grad_mid,
            sums_two,
        )
        back_routes = [[(target, source) for source, target in route] for route in row_routes(dp_size)]
        out_one, out_two, attention_got = tie(out_one, out_two, attention_got)
        start_one = lax.ppermute(out_one, BOTH, back_routes[0])
        attention_grad = weigh(0, place, dq, own_grad, got_kv, context, normed_one, grad_attn, attention_got)
        attention_grad, start_one, up_second, down_second, out_two, small = tie(
            attention_grad, start_one, up_second, down_second, out_two, small
        )
        attention_grad = plane_scatter(attention_grad, dp_size)
        pair, pair_sent = merge((up_own, up_got, up_sent, up_second), (down_own, down_got, down_sent, down_second))
        pair_sent, small, bias_own, bias_other = tie(pair_sent, small, bias_own, bias_other)
        small = tally(place, small, bias_own, bias_other)
        small = small + across(small, 1)
        small_got = swap_mp(small, 1)
        pair_sent = swap_mp(pair_sent, 1)
        pair_sent, small_got = tie(pair_sent, small_got)

        bits = [1 << n for n in range(dp_size.bit_length() - 1)]
        small = small + small_got
        pair = add(pair, pair_sent)
        pair_sent = swap_mp(pair[1], 2)
        small_far = swap_mp(small, 2)
        attention_grad, small_far = tie(attention_grad, small_far)
        small = small + small_far
        activations = jnp.where(
            parity == 0, jnp.stack([back_one, back_two]), jnp.stack([back_two, back_one])
        )

        def lift(value):
            for bit in bits[3:]:
                value = value + across(value, bit)
            return value

        small = lift(small)
        attention_sent = swap_mp(attention_grad[2:], 1)
        pair, pair_sent, activations, _ = tie(pair, pair_sent, activations, attention_sent)
        if dp_size > 8:
            pair_sent = lift(add(pair[0], pair_sent))
            pair = jnp.zeros_like(pair)
        pair = plane_gather(pack(pair, pair_sent, small), dp_size)
        attention_sent, out_two = tie(attention_sent, out_two)
        half = strip // 2
        start_two = jnp.concatenate(
            [
                lax.ppermute(out_two[:half], BOTH, back_routes[1]),
                lax.ppermute(out_two[half:], BOTH, back_routes[1]),
            ],
            axis=0,
        )
        attention_grad = add(attention_grad[:2], attention_sent)
        attention_sent = swap_mp(attention_grad[1], 2)
        attention_sent, pair, start_two = tie(attention_sent, pair, start_two)
        grad_start = jnp.where(
            parity == 0, jnp.stack([start_one, start_two]), jnp.stack([start_two, start_one])
        )
        tokens_grad = jnp.where((mask_flags == 1)[:, :, None], 0.0, grad_start.astype(F32))
        attention_grad = lift(add(attention_grad[0], attention_sent))
        attention_grad = plane_gather(attention_grad, dp_size)
        up_weight_grad, down_weight_grad, small, up_bias_grad, qv_bias_grad = close_pair(place, pair, across(pair, 1))
        attention_grad, up_weight_grad, down_weight_grad, small, tokens_grad = tie(
            attention_grad, up_weight_grad, down_weight_grad, small, tokens_grad
        )
        w_qkv_grad, w_out_grad = close_attention(place, attention_grad, across(attention_grad, 1))
        w_qkv_grad = w_qkv_grad.transpose(0, 2, 1)
        up_bias_grad = up_bias_grad.reshape(-1)
        return (
            activations,
            tokens_grad,
            small[0],
            small[1],
            small[2],
            w_qkv_grad,
            qv_bias_grad,
            w_out_grad,
            small[3],
            small[4],
            small[5],
            up_weight_grad,
            up_bias_grad,
            down_weight_grad,
            small[6],
        )

    return body


def solution(mesh):
    in_specs = (
        P("dp", "mp", None),
        P("dp", None),
        P("dp", "mp"),
        P(),
        P(),
        P(),
        P(None, None, "mp"),
        P(None, "mp"),
        P("mp", None),
        P(),
        P(),
        P(),
        P(None, "mp"),
        P("mp"),
        P("mp", None),
        P(),
        P("dp", "mp", None),
    )
    out_specs = (
        P("dp", "mp", None),
        P("dp", "mp", None),
        P(),
        P(),
        P(),
        P(None, None, "mp"),
        P(None, "mp"),
        P("mp", None),
        P(),
        P(),
        P(),
        P(None, "mp"),
        P("mp"),
        P("mp", None),
        P(),
    )
    return jax.shard_map(
        make_body(mesh.shape["dp"]), mesh=mesh, in_specs=in_specs, out_specs=out_specs, check_vma=False
    )
```
